512 devices in a mesh: dp: 32 (over x, y), segment: 2 (over core), mp: 8 (over z).
Axes of the slice: x: 4, y: 8, z: 8, core: 2. Of those that a mesh axis runs over, the one named last changes fastest.
Arguments:
- frames: bfloat16 [2, 8192, 1280], P(None, ('dp', 'mp')), may hold values from -8 to 8
- dec_states: bfloat16 [2, 2048, 1280], P(None, 'dp'), may hold values from -8 to 8
- out_grad: bfloat16 [2, 2048, 1280], P(None, 'dp'), may hold values from -3 to 3
- frame_lengths: int32 [2, 32, 4], P(None, 'dp'), may hold values from 1 to 128, 256 in all within a row
- token_lengths: int32 [2, 32, 4], P(None, 'dp'), may hold values from 1 to 32, 64 in all within a row
- weights: bfloat16 [2, 4, 1024, 1280], P('segment', None, 'mp'), may hold values from -1 to 1
- norm_gains: float32 [3, 1280], replicated, may hold values from 0.25 to 1.75
- norm_biases: float32 [3, 1280], replicated, may hold values from -2 to 2
Outputs:
- gradient: float32 [2, 3, 1024, 1280], P('segment', None, 'mp')
The draws below stay inside these ranges and needn't reach their ends.
Inputs may be any that keep to these rules, and one draw needn't show every extreme that they name: `frame_lengths`: the 4 utterance lengths of each micro-batch and group sum to 256. `token_lengths`: the 4 token counts of each micro-batch and group sum to 64.
All inputs are finite; a program needn't handle non-finite values.
Results may differ from the reference program's by a relative error of at most 0.04.
Values may be sent and summed in bfloat16 or wider, within the bound.
No kernel may reach another device: no remote copies, remote signals or barrier semaphores. Data moves between devices by JAX's collectives and lax.ppermute only.
A program may use at most 64 MiB of HBM per device.

```python
import math
import jax
import jax.numpy as jnp
import numpy as np
from jax import lax

D = 1280
HS = 64
FRM = 256
TKM = 64
UTT = 4
MB = 2
HD = 1024
GROUPS = 32
FRAMES = 8192
TOKENS = 2048
N_DP = 32
N_MP = 8


def drawn_rows(key, salt, shape):
    drawn_values = jax.random.truncated_normal(jax.random.fold_in(key, salt), -6.0, 6.0, shape, jnp.float32)
    return drawn_values


def draw_frames(key, part):
    return drawn_rows(key, 11, (MB, FRAMES, D)).astype(jnp.bfloat16)


def draw_dec_states(key, part):
    return drawn_rows(key, 21, (MB, TOKENS, D)).astype(jnp.bfloat16)


def draw_weights(key, part):
    drawn_values = jax.random.truncated_normal(jax.random.fold_in(key, 31), -6.0, 6.0, (2, 4, HD, D), jnp.float32) / math.sqrt(D)
    return drawn_values.astype(jnp.bfloat16)


def steps_of(rng, dims, pieces, smallest, largest):
    def one(dim, shards_of):
        steps = jax.random.uniform(jax.random.fold_in(jax.random.fold_in(rng, 6), dim), (shards_of,), jnp.float32, smallest / len(pieces), largest / len(pieces))
        return jnp.repeat(jnp.exp(steps), dims[dim] // shards_of).reshape((-1,) + (1,) * (len(dims) - dim - 1))

    factor_of = one(*pieces[0])
    for cut in pieces[1:]:
        factor_of = factor_of * one(*cut)
    return factor_of


def profile(amount, total, most, lean):
    weights = [(1 << 20) // math.isqrt(rank ** lean) + 1 for rank in range(2, amount + 1)]
    rest, counts = total - most - (amount - 1), [1] * (amount - 1)
    while rest > 0:
        free = [i for i in range(amount - 1) if counts[i] < most]
        whole, left = sum([weights[i] for i in free]), rest
        for i in free:
            more = min(most - counts[i], max(1, left * weights[i] // whole), rest)
            counts[i] = counts[i] + more
            rest = rest - more
    return np.array([most] + counts)


def uneven_parts(own_key, amount, total, reach, slope):
    if amount == 2:
        one = jax.random.randint(own_key, (), max(1, total - reach), min(reach, total - 1) + 1)
        return jnp.stack([one, total - one])
    sizes = jnp.asarray(profile(amount, total, reach, slope), jnp.int32)
    pairs = (amount - 1) // 2
    source_of, sink = sizes[1:1 + 2 * pairs:2], sizes[2:2 + 2 * pairs:2]
    slack = jnp.minimum(source_of - 1, reach - sink)
    moved = jax.random.randint(jax.random.fold_in(own_key, 1), (pairs,), 0, 1 << 20) % (slack + 1)
    sizes = sizes.at[1:1 + 2 * pairs:2].set(source_of - moved).at[2:2 + 2 * pairs:2].set(sink + moved)
    return sizes[jax.random.permutation(jax.random.fold_in(own_key, 2), amount)]


def scatter_about(stream_key, extent, deviation, reach, shards=(), kind=jnp.bfloat16):
    result = deviation * jax.random.normal(stream_key, extent, jnp.float32)
    if shards:
        result = result * steps_of(stream_key, extent, shards, -0.22, 0.18)
    return jnp.clip(result, -reach, reach).astype(kind)


def setup_inputs(seed: int = 0) -> dict:
    key_of = jax.random.split(jax.random.key(seed), 9)
    return {
        "frames": draw_frames(jax.random.fold_in(key_of[8], 71), 0),
        "dec_states": draw_dec_states(jax.random.fold_in(key_of[8], 71), 0),
        "out_grad": scatter_about(key_of[2], (MB, TOKENS, D), 0.5, 3.0, ((1, 32),)),
        "frame_lengths": jax.vmap(lambda own: uneven_parts(own, UTT, FRM, FRM // 2, 2))(jax.random.split(key_of[3], MB * GROUPS)).reshape((MB, GROUPS, UTT)).astype(jnp.int32),
        "token_lengths": jax.vmap(lambda own: uneven_parts(own, UTT, TKM, TKM // 2, 2))(jax.random.split(key_of[4], MB * GROUPS)).reshape((MB, GROUPS, UTT)).astype(jnp.int32),
        "weights": draw_weights(jax.random.fold_in(key_of[8], 71), 0),
        "norm_gains": jnp.clip(1.0 + 0.15 * jax.random.normal(key_of[6], (3, D), jnp.float32), 0.25, 1.75),
        "norm_biases": scatter_about(key_of[7], (3, D), 0.3, 2.0, (), jnp.float32),
    }


EPSILON = 1e-05

def layer_norm(values, norm_gain, offset):
    center = values - lax.optimization_barrier(jnp.mean(values, axis=-1, keepdims=True))
    variance = lax.optimization_barrier(jnp.mean(center * center, axis=-1, keepdims=True))
    return center * lax.rsqrt(variance + EPSILON) * norm_gain + offset

def norm_backward(grad_out, values, norm_gain):
    center = values - lax.optimization_barrier(jnp.mean(values, axis=-1, keepdims=True))
    variance = lax.optimization_barrier(jnp.mean(center * center, axis=-1, keepdims=True))
    inverse = lax.rsqrt(variance + EPSILON)
    normed = center * inverse
    scaled = grad_out * norm_gain
    return inverse * (scaled - lax.optimization_barrier(jnp.mean(scaled, axis=-1, keepdims=True)) - normed * lax.optimization_barrier(jnp.mean(scaled * normed, axis=-1, keepdims=True)))

def utterance_ids(lengths, row_count):
    bounds = jnp.cumsum(lengths, dtype=jnp.int32)
    places = jnp.arange(row_count, dtype=jnp.int32)
    return lax.optimization_barrier(jnp.sum((places[:, None] >= bounds[None, :]).astype(jnp.int32), axis=1))

def project(row_block, matrix):
    return jnp.dot(row_block, matrix.T, preferred_element_type=jnp.float32).astype(jnp.bfloat16)

def outer_rows(left_rows, right_rows):
    return jnp.dot(left_rows.T, right_rows, preferred_element_type=jnp.float32)

def split_heads(row_block):
    return row_block.astype(jnp.float32).reshape(row_block.shape[0], -1, HS)

def rounded_copy(values):
    return lax.optimization_barrier(values.astype(jnp.bfloat16)).astype(jnp.float32)

def attend(queries, key_rows, value_rows, allowed):
    scaling = 1.0 / math.sqrt(HS)
    scores = jnp.einsum('qhd,khd->hqk', split_heads(queries), split_heads(key_rows)) * scaling
    scores = jnp.where(allowed[None], scores, -1e+30)
    highest = lax.optimization_barrier(jnp.max(scores, axis=-1, keepdims=True))
    raised = jnp.exp(scores - highest)
    attn_probs = raised / lax.optimization_barrier(jnp.sum(raised, axis=-1, keepdims=True))
    context = jnp.einsum('hqk,khd->qhd', rounded_copy(attn_probs), split_heads(value_rows))
    return (context.reshape(queries.shape[0], -1).astype(jnp.bfloat16), attn_probs)

def attend_backward(queries, key_rows, value_rows, attn_probs, grad_context):
    scaling = 1.0 / math.sqrt(HS)
    grad_heads = split_heads(grad_context)
    grad_probs = jnp.einsum('qhd,khd->hqk', grad_heads, split_heads(value_rows))
    grad_scores = attn_probs * (grad_probs - lax.optimization_barrier(jnp.sum(grad_probs * attn_probs, axis=-1, keepdims=True)))
    grad_scores = rounded_copy(grad_scores)
    key_grad = jnp.einsum('hqk,qhd->khd', grad_scores, split_heads(queries)) * scaling
    key_grad = key_grad.reshape(key_rows.shape[0], -1).astype(jnp.bfloat16)
    value_grad = jnp.einsum('hqk,qhd->khd', rounded_copy(attn_probs), grad_heads)
    value_grad = value_grad.reshape(key_rows.shape[0], -1).astype(jnp.bfloat16)
    return (key_grad, value_grad)

def blocked_sum(products):
    gathered = None
    for left_rows, right_rows in products:
        left_split = left_rows.astype(jnp.float32).reshape(left_rows.shape[0], N_MP, -1)
        right_split = right_rows.astype(jnp.float32).reshape(N_MP, -1, right_rows.shape[1])
        piece_sum = jnp.einsum('rjc,jcd->jrd', left_split, right_split)
        gathered = piece_sum if gathered is None else gathered + piece_sum
    return lax.optimization_barrier(jnp.sum(rounded_copy(gathered), axis=0))

def group_terms(frames_group, tokens_group, upstream_group, frame_lens, token_lens, weights, norm_gains, norm_biases):
    encoder_sum = jnp.zeros((3, HD, D), jnp.float32)
    decoder_sum = jnp.zeros((3, HD, D), jnp.float32)
    for micro_index in range(MB):
        frame_ids = utterance_ids(frame_lens[micro_index], FRM)
        token_ids = utterance_ids(token_lens[micro_index], TKM)
        inputs = frames_group[micro_index]
        normed = layer_norm(inputs.astype(jnp.float32), norm_gains[0], norm_biases[0]).astype(jnp.bfloat16)
        queries = project(normed, weights[0, 0])
        key_rows = project(normed, weights[0, 1])
        value_rows = project(normed, weights[0, 2])
        context, attn_probs = attend(queries, key_rows, value_rows, frame_ids[:, None] == frame_ids[None, :])
        states = (inputs.astype(jnp.float32) + blocked_sum(((context, weights[0, 3]),))).astype(jnp.bfloat16)
        state_normed = layer_norm(states.astype(jnp.float32), norm_gains[2], norm_biases[2]).astype(jnp.bfloat16)
        token_normed = layer_norm(tokens_group[micro_index].astype(jnp.float32), norm_gains[1], norm_biases[1]).astype(jnp.bfloat16)
        dec_queries = project(token_normed, weights[1, 0])
        dec_keys = project(state_normed, weights[1, 1])
        dec_values = project(state_normed, weights[1, 2])
        dec_context, dec_probs = attend(dec_queries, dec_keys, dec_values, token_ids[:, None] == frame_ids[None, :])
        upstream = upstream_group[micro_index]
        grad_context = project(upstream, weights[1, 3])
        dec_key_grad, dec_value_grad = attend_backward(dec_queries, dec_keys, dec_values, dec_probs, grad_context)
        decoder_sum = decoder_sum + jnp.stack([outer_rows(dec_key_grad, state_normed), outer_rows(dec_value_grad, state_normed), outer_rows(dec_context, upstream)])
        grad_normed = blocked_sum(((dec_key_grad, weights[1, 1]), (dec_value_grad, weights[1, 2])))
        states_grad = norm_backward(grad_normed, states.astype(jnp.float32), norm_gains[2]).astype(jnp.bfloat16)
        att_grad = project(states_grad, weights[0, 3])
        enc_key_grad, enc_value_grad = attend_backward(queries, key_rows, value_rows, attn_probs, att_grad)
        encoder_sum = encoder_sum + jnp.stack([outer_rows(enc_key_grad, normed), outer_rows(enc_value_grad, normed), outer_rows(context, states_grad)])
    return jnp.stack([encoder_sum, decoder_sum]).astype(jnp.bfloat16)

def reference(frames, dec_states, out_grad, frame_lengths, token_lengths, weights, norm_gains, norm_biases):
    frames_split = frames.reshape(MB, N_DP, FRM, D).transpose(1, 0, 2, 3)
    tokens_split = dec_states.reshape(MB, N_DP, TKM, D).transpose(1, 0, 2, 3)
    upstream_split = out_grad.reshape(MB, N_DP, TKM, D).transpose(1, 0, 2, 3)
    frame_lens = frame_lengths.transpose(1, 0, 2)
    token_lens = token_lengths.transpose(1, 0, 2)

    def accumulate(running, group_items):
        group = group_terms(group_items[0], group_items[1], group_items[2], group_items[3], group_items[4], weights, norm_gains, norm_biases)
        return (running + lax.optimization_barrier(group).astype(jnp.float32), None)
    running, _ = lax.scan(accumulate, jnp.zeros((2, 3, HD, D), jnp.float32), (frames_split, tokens_split, upstream_split, frame_lens, token_lens))
    return running
```

```python
import math

import jax
import jax.numpy as jnp
from jax import lax
from jax.sharding import PartitionSpec as P

HS = 64
EPSILON = 1e-05
ROWS_DIMS = (((0,), (0,)), ((), ()))
FEAT_DIMS = (((1,), (1,)), ((), ()))


def layer_norm(values, norm_gain, offset):
    center = values - jnp.mean(values, axis=-1, keepdims=True)
    variance = jnp.mean(center * center, axis=-1, keepdims=True)
    return center * lax.rsqrt(variance + EPSILON) * norm_gain + offset


def norm_backward(grad_out, values, norm_gain):
    center = values - jnp.mean(values, axis=-1, keepdims=True)
    variance = jnp.mean(center * center, axis=-1, keepdims=True)
    inverse = lax.rsqrt(variance + EPSILON)
    normed = center * inverse
    scaled = grad_out * norm_gain
    return inverse * (
        scaled
        - jnp.mean(scaled, axis=-1, keepdims=True)
        - normed * jnp.mean(scaled * normed, axis=-1, keepdims=True)
    )


def utterance_ids(lengths, row_count):
    bounds = jnp.cumsum(lengths, dtype=jnp.int32)
    places = jnp.arange(row_count, dtype=jnp.int32)
    return jnp.sum((places[:, None] >= bounds[None, :]).astype(jnp.int32), axis=1)


def project(row_block, matrix):
    return lax.dot_general(row_block, matrix, FEAT_DIMS, preferred_element_type=jnp.float32).astype(
        jnp.bfloat16
    )


def outer_rows(left_rows, right_rows):
    return lax.dot_general(left_rows, right_rows, ROWS_DIMS, preferred_element_type=jnp.float32)


def split_heads(row_block):
    return row_block.reshape(row_block.shape[0], -1, HS)


def attend(queries, key_rows, value_rows, allowed):
    scaling = 1.0 / math.sqrt(HS)
    scores = (
        jnp.einsum(
            "qhd,khd->hqk",
            split_heads(queries),
            split_heads(key_rows),
            preferred_element_type=jnp.float32,
        )
        * scaling
    )
    scores = jnp.where(allowed[None], scores, -1e30)
    highest = jnp.max(scores, axis=-1, keepdims=True)
    raised = jnp.exp(scores - highest)
    attn_probs = raised / jnp.sum(raised, axis=-1, keepdims=True)
    context = jnp.einsum(
        "hqk,khd->qhd",
        attn_probs.astype(jnp.bfloat16),
        split_heads(value_rows),
        preferred_element_type=jnp.float32,
    )
    return (context.reshape(queries.shape[0], -1).astype(jnp.bfloat16), attn_probs)


def attend_backward(queries, key_rows, value_rows, attn_probs, grad_context):
    scaling = 1.0 / math.sqrt(HS)
    grad_heads = split_heads(grad_context)
    grad_probs = jnp.einsum(
        "qhd,khd->hqk", grad_heads, split_heads(value_rows), preferred_element_type=jnp.float32
    )
    grad_scores = (
        attn_probs * (grad_probs - jnp.sum(grad_probs * attn_probs, axis=-1, keepdims=True))
    ).astype(jnp.bfloat16)
    key_grad = (
        jnp.einsum(
            "hqk,qhd->khd", grad_scores, split_heads(queries), preferred_element_type=jnp.float32
        )
        * scaling
    )
    key_grad = key_grad.reshape(key_rows.shape[0], -1).astype(jnp.bfloat16)
    value_grad = jnp.einsum(
        "hqk,qhd->khd",
        attn_probs.astype(jnp.bfloat16),
        grad_heads,
        preferred_element_type=jnp.float32,
    )
    value_grad = value_grad.reshape(key_rows.shape[0], -1).astype(jnp.bfloat16)
    return (key_grad, value_grad)


def spread(block, axis):
    size = lax.axis_size(axis)
    return lax.all_to_all(jnp.broadcast_to(block[None], (size,) + block.shape), axis, 0, 0)


def share_sum(blocks, axis):
    return jnp.sum(lax.all_to_all(blocks, axis, 0, 0).astype(jnp.float32), axis=0)


def shards(
    frames, dec_states, out_grad, frame_lengths, token_lengths, weights, norm_gains, norm_biases
):
    core = lax.axis_index("segment")
    first = core == 0
    own = weights[0]
    other = lax.ppermute(own, "segment", [(0, 1), (1, 0)])
    shard_rows, features = frames.shape[1:]
    mp = lax.axis_size("mp")
    head_cols = own.shape[1]
    rows = shard_rows * mp

    def mine(array):
        return lax.dynamic_index_in_dim(array, core, 0, keepdims=False)

    inputs = mine(frames)
    tokens = mine(dec_states)
    upstream = mine(out_grad)
    frame_ids = utterance_ids(mine(frame_lengths)[0], rows)
    token_ids = utterance_ids(mine(token_lengths)[0], tokens.shape[0])

    enc_full = spread(inputs, "mp").reshape(rows, features)
    enc = jnp.where(first, own, other)
    dec = jnp.where(first, other, own)

    normed = layer_norm(enc_full.astype(jnp.float32), norm_gains[0], norm_biases[0]).astype(
        jnp.bfloat16
    )
    queries = project(normed, enc[0])
    key_rows = project(normed, enc[1])
    value_rows = project(normed, enc[2])
    context, probs = attend(queries, key_rows, value_rows, frame_ids[:, None] == frame_ids[None, :])
    partial = jnp.dot(context, enc[3], preferred_element_type=jnp.float32).astype(jnp.bfloat16)
    summed = share_sum(partial.reshape(mp, shard_rows, features), "mp")
    states = (inputs.astype(jnp.float32) + summed).astype(jnp.bfloat16)
    states_full = spread(states, "mp").reshape(rows, features)

    state_normed = layer_norm(
        states_full.astype(jnp.float32), norm_gains[2], norm_biases[2]
    ).astype(jnp.bfloat16)
    token_normed = layer_norm(tokens.astype(jnp.float32), norm_gains[1], norm_biases[1]).astype(
        jnp.bfloat16
    )
    dec_queries = project(token_normed, dec[0])
    dec_keys = project(state_normed, dec[1])
    dec_values = project(state_normed, dec[2])
    dec_context, dec_probs = attend(
        dec_queries, dec_keys, dec_values, token_ids[:, None] == frame_ids[None, :]
    )
    grad_context = project(upstream, dec[3])
    dec_key_grad, dec_value_grad = attend_backward(
        dec_queries, dec_keys, dec_values, dec_probs, grad_context
    )
    partial = (
        jnp.dot(dec_key_grad, dec[1], preferred_element_type=jnp.float32)
        + jnp.dot(dec_value_grad, dec[2], preferred_element_type=jnp.float32)
    ).astype(jnp.bfloat16)
    summed = share_sum(partial.reshape(mp, shard_rows, features), "mp")
    grads = norm_backward(summed, states.astype(jnp.float32), norm_gains[2]).astype(jnp.bfloat16)
    dec_term = jnp.concatenate(
        [
            outer_rows(dec_key_grad, state_normed),
            outer_rows(dec_value_grad, state_normed),
            outer_rows(dec_context, upstream),
        ]
    )
    dec_sent = lax.ppermute(dec_term.astype(jnp.bfloat16), "segment", [(0, 1)])
    grads_full = spread(grads, "mp").reshape(rows, features)

    att_grad = project(grads_full, enc[3])
    enc_key_grad, enc_value_grad = attend_backward(queries, key_rows, value_rows, probs, att_grad)
    enc_term = jnp.concatenate(
        [
            outer_rows(enc_key_grad, normed),
            outer_rows(enc_value_grad, normed),
            outer_rows(context, grads_full),
        ]
    )
    enc_sent = lax.ppermute(enc_term.astype(jnp.bfloat16), "segment", [(1, 0)])
    term = jnp.where(
        first,
        enc_term + enc_sent.astype(jnp.float32),
        dec_term + dec_sent.astype(jnp.float32),
    ).astype(jnp.bfloat16)

    dp = lax.axis_size("dp")
    high, wide = 3 * head_cols // 8, features // 128
    tiles = term.reshape(high, 8, wide, 128).transpose(0, 2, 1, 3)
    tiles = tiles.reshape(dp, high * wide // dp, 8, 128)
    total = share_sum(tiles, "dp").astype(jnp.bfloat16)
    gradient = spread(total, "dp").astype(jnp.float32)
    gradient = gradient.reshape(high, wide, 8, 128).transpose(0, 2, 1, 3)
    return gradient.reshape(1, 3, head_cols, features)


def solution(mesh):
    placed = (
        P(None, ("dp", "mp"), None),
        P(None, "dp", None),
        P(None, "dp", None),
        P(None, "dp", None),
        P(None, "dp", None),
        P("segment", None, "mp", None),
        P(),
        P(),
    )
    return jax.shard_map(
        shards,
        mesh=mesh,
        in_specs=placed,
        out_specs=P("segment", None, "mp", None),
        check_vma=False,
    )
```

```python
import math

import jax
import jax.numpy as jnp
from jax import lax
from jax.sharding import PartitionSpec as P

HS = 64
EPSILON = 1e-05
ROWS_DIMS = (((0,), (0,)), ((), ()))
FEAT_DIMS = (((1,), (1,)), ((), ()))


def layer_norm(values, norm_gain, offset):
    center = values - jnp.mean(values, axis=-1, keepdims=True)
    variance = jnp.mean(center * center, axis=-1, keepdims=True)
    return center * lax.rsqrt(variance + EPSILON) * norm_gain + offset


def norm_backward(grad_out, values, norm_gain):
    center = values - jnp.mean(values, axis=-1, keepdims=True)
    variance = jnp.mean(center * center, axis=-1, keepdims=True)
    inverse = lax.rsqrt(variance + EPSILON)
    normed = center * inverse
    scaled = grad_out * norm_gain
    return inverse * (
        scaled
        - jnp.mean(scaled, axis=-1, keepdims=True)
        - normed * jnp.mean(scaled * normed, axis=-1, keepdims=True)
    )


def utterance_ids(lengths, row_count):
    bounds = jnp.cumsum(lengths, dtype=jnp.int32)
    places = jnp.arange(row_count, dtype=jnp.int32)
    return jnp.sum((places[:, None] >= bounds[None, :]).astype(jnp.int32), axis=1)


def project(row_block, matrix):
    return lax.dot_general(row_block, matrix, FEAT_DIMS, preferred_element_type=jnp.float32).astype(
        jnp.bfloat16
    )


def outer_rows(left_rows, right_rows):
    return lax.dot_general(left_rows, right_rows, ROWS_DIMS, preferred_element_type=jnp.float32)


def split_heads(row_block):
    return row_block.reshape(row_block.shape[0], -1, HS)


def attend(queries, key_rows, value_rows, allowed):
    scaling = 1.0 / math.sqrt(HS)
    scores = (
        jnp.einsum(
            "qhd,khd->hqk",
            split_heads(queries),
            split_heads(key_rows),
            preferred_element_type=jnp.float32,
        )
        * scaling
    )
    scores = jnp.where(allowed[None], scores, -1e30)
    highest = jnp.max(scores, axis=-1, keepdims=True)
    raised = jnp.exp(scores - highest)
    attn_probs = raised / jnp.sum(raised, axis=-1, keepdims=True)
    context = jnp.einsum(
        "hqk,khd->qhd",
        attn_probs.astype(jnp.bfloat16),
        split_heads(value_rows),
        preferred_element_type=jnp.float32,
    )
    return (context.reshape(queries.shape[0], -1).astype(jnp.bfloat16), attn_probs)


def attend_backward(queries, key_rows, value_rows, attn_probs, grad_context):
    scaling = 1.0 / math.sqrt(HS)
    grad_heads = split_heads(grad_context)
    grad_probs = jnp.einsum(
        "qhd,khd->hqk", grad_heads, split_heads(value_rows), preferred_element_type=jnp.float32
    )
    grad_scores = (
        attn_probs * (grad_probs - jnp.sum(grad_probs * attn_probs, axis=-1, keepdims=True))
    ).astype(jnp.bfloat16)
    key_grad = (
        jnp.einsum(
            "hqk,qhd->khd", grad_scores, split_heads(queries), preferred_element_type=jnp.float32
        )
        * scaling
    )
    key_grad = key_grad.reshape(key_rows.shape[0], -1).astype(jnp.bfloat16)
    value_grad = jnp.einsum(
        "hqk,qhd->khd",
        attn_probs.astype(jnp.bfloat16),
        grad_heads,
        preferred_element_type=jnp.float32,
    )
    value_grad = value_grad.reshape(key_rows.shape[0], -1).astype(jnp.bfloat16)
    return (key_grad, value_grad)


def spread(block, axis):
    size = lax.axis_size(axis)
    return lax.all_to_all(jnp.broadcast_to(block[None], (size,) + block.shape), axis, 0, 0)


def share_sum(blocks, axis):
    return jnp.sum(lax.all_to_all(blocks, axis, 0, 0).astype(jnp.float32), axis=0)


def swap(block):
    return lax.ppermute(block, "segment", [(0, 1), (1, 0)])


def to_chunks(block, parts):
    high, wide = block.shape[0] // 8, block.shape[1] // 128
    tiles = block.reshape(high, 8, wide, 128).transpose(0, 2, 1, 3).reshape(-1, 8, 128)
    each = -(-tiles.shape[0] // parts)
    tiles = jnp.pad(tiles, ((0, each * parts - tiles.shape[0]), (0, 0), (0, 0)))
    return tiles.reshape(parts, each, 8, 128)


def from_chunks(chunks, rows, cols):
    high, wide = rows // 8, cols // 128
    tiles = chunks.reshape(-1, 8, 128)[: high * wide]
    return tiles.reshape(high, wide, 8, 128).transpose(0, 2, 1, 3).reshape(rows, cols)


def shards(
    frames, dec_states, out_grad, frame_lengths, token_lengths, weights, norm_gains, norm_biases
):
    core = lax.axis_index("segment")
    first = core == 0
    own = weights[0]
    shard_rows, features = frames.shape[1:]
    mp = lax.axis_size("mp")
    dp = lax.axis_size("dp")
    head_cols = own.shape[1]
    rows = shard_rows * mp
    half = features // 2

    def mine(array):
        return lax.dynamic_index_in_dim(array, core, 0, keepdims=False)

    inputs = mine(frames)
    tokens = mine(dec_states)
    upstream = mine(out_grad)
    frame_ids = utterance_ids(mine(frame_lengths)[0], rows)
    token_ids = utterance_ids(mine(token_lengths)[0], tokens.shape[0])

    out_sent = lax.ppermute(own[3, :, half:], "segment", [(0, 1)])
    out_part = jnp.where(first, own[3, :, :half], out_sent)
    out_part = lax.all_gather(out_part, "mp", axis=0, tiled=True)
    out_rest = swap(out_part)

    enc_full = spread(inputs, "mp").reshape(rows, features)
    other = swap(own)
    enc = jnp.where(first, own, other)
    dec = jnp.where(first, other, own)

    normed = layer_norm(enc_full.astype(jnp.float32), norm_gains[0], norm_biases[0]).astype(
        jnp.bfloat16
    )
    queries = project(normed, enc[0])
    key_rows = project(normed, enc[1])
    value_rows = project(normed, enc[2])
    context, probs = attend(queries, key_rows, value_rows, frame_ids[:, None] == frame_ids[None, :])
    context_full = spread(context, "mp").transpose(1, 0, 2).reshape(rows, mp * head_cols)
    out_mine = jnp.dot(context_full, out_part, preferred_element_type=jnp.float32)
    out_other = jnp.dot(context_full, out_rest, preferred_element_type=jnp.float32)
    summed = jnp.concatenate(
        [jnp.where(first, out_mine, out_other), jnp.where(first, out_other, out_mine)], axis=1
    )
    states_full = (enc_full.astype(jnp.float32) + summed).astype(jnp.bfloat16)
    states = lax.dynamic_slice_in_dim(
        states_full, lax.axis_index("mp") * shard_rows, shard_rows, 0
    )

    state_normed = layer_norm(
        states_full.astype(jnp.float32), norm_gains[2], norm_biases[2]
    ).astype(jnp.bfloat16)
    token_normed = layer_norm(tokens.astype(jnp.float32), norm_gains[1], norm_biases[1]).astype(
        jnp.bfloat16
    )
    dec_queries = project(token_normed, dec[0])
    dec_keys = project(state_normed, dec[1])
    dec_values = project(state_normed, dec[2])
    dec_context, dec_probs = attend(
        dec_queries, dec_keys, dec_values, token_ids[:, None] == frame_ids[None, :]
    )
    grad_context = project(upstream, dec[3])
    dec_key_grad, dec_value_grad = attend_backward(
        dec_queries, dec_keys, dec_values, dec_probs, grad_context
    )
    partial = (
        jnp.dot(dec_key_grad, dec[1], preferred_element_type=jnp.float32)
        + jnp.dot(dec_value_grad, dec[2], preferred_element_type=jnp.float32)
    ).astype(jnp.bfloat16)

    def combine(term):
        left, right = term[:, :half], term[:, half:]
        sent = swap(jnp.where(first, right, left).astype(jnp.bfloat16))
        return (jnp.where(first, left, right) + sent.astype(jnp.float32)).astype(jnp.bfloat16)

    def reduce_groups(term):
        total = share_sum(to_chunks(term, dp), "dp").astype(jnp.bfloat16)
        return from_chunks(spread(total, "dp"), 3 * head_cols, half)

    dec_term = jnp.concatenate(
        [
            outer_rows(dec_key_grad, state_normed),
            outer_rows(dec_value_grad, state_normed),
            outer_rows(dec_context, upstream),
        ]
    )
    pieces = lax.all_to_all(partial.reshape(mp, shard_rows, features), "mp", 0, 0)
    pieces, dec_part = lax.optimization_barrier((pieces, combine(dec_term)))
    dec_total = lax.psum(dec_part, "dp")
    summed = jnp.sum(pieces.astype(jnp.float32), axis=0)
    grads = norm_backward(summed, states.astype(jnp.float32), norm_gains[2]).astype(jnp.bfloat16)
    grads_full = spread(grads, "mp").reshape(rows, features)

    att_grad = project(grads_full, enc[3])
    enc_key_grad, enc_value_grad = attend_backward(queries, key_rows, value_rows, probs, att_grad)
    enc_term = jnp.concatenate(
        [
            outer_rows(enc_key_grad, normed),
            outer_rows(enc_value_grad, normed),
            outer_rows(context, grads_full),
        ]
    )
    enc_total = reduce_groups(combine(enc_term))
    kept = jnp.where(first, enc_total, dec_total)
    got = swap(jnp.where(first, dec_total, enc_total))
    gradient = jnp.concatenate(
        [jnp.where(first, kept, got), jnp.where(first, got, kept)], axis=1
    ).astype(jnp.float32)
    return gradient.reshape(1, 3, head_cols, features)


def solution(mesh):
    placed = (
        P(None, ("dp", "mp"), None),
        P(None, "dp", None),
        P(None, "dp", None),
        P(None, "dp", None),
        P(None, "dp", None),
        P("segment", None, "mp", None),
        P(),
        P(),
    )
    return jax.shard_map(
        shards,
        mesh=mesh,
        in_specs=placed,
        out_specs=P("segment", None, "mp", None),
        check_vma=False,
    )
```

```python
import functools
import math

import jax
import jax.numpy as jnp
from jax import lax
from jax.experimental import pallas as pl
from jax.experimental.pallas import tpu as pltpu
from jax.sharding import PartitionSpec as P

HS = 64
SCALING = 1.0 / math.sqrt(HS)
EPSILON = 1e-05
ROWS_DIMS = (((0,), (0,)), ((), ()))
FEAT_DIMS = (((1,), (1,)), ((), ()))


def dot_nn(a, b):
    return lax.dot_general(a, b, (((1,), (0,)), ((), ())), preferred_element_type=jnp.float32)


def dot_nt(a, b):
    return lax.dot_general(a, b, FEAT_DIMS, preferred_element_type=jnp.float32)


def dot_tn(a, b):
    return lax.dot_general(a, b, ROWS_DIMS, preferred_element_type=jnp.float32)


def row_stats(values):
    center = values - jnp.mean(values, axis=-1, keepdims=True)
    variance = jnp.mean(center * center, axis=-1, keepdims=True)
    return center, lax.rsqrt(variance + EPSILON)


def layer_norm(values, norm_gain, offset):
    center, inverse = row_stats(values.astype(jnp.float32))
    return (center * inverse * norm_gain + offset).astype(jnp.bfloat16)


def ids_along(lengths_ref, shape, axis):
    places = lax.broadcasted_iota(jnp.int32, shape, axis)
    bound = 0
    ids = jnp.zeros(shape, jnp.int32)
    for piece in range(lengths_ref.shape[0]):
        bound = bound + lengths_ref[piece]
        ids = ids + (places >= bound).astype(jnp.int32)
    return ids


def softmax(queries, keys, allowed):
    scores = jnp.where(allowed, dot_nt(queries, keys) * SCALING, -1e30)
    raised = jnp.exp(scores - jnp.max(scores, axis=-1, keepdims=True))
    return raised / jnp.sum(raised, axis=-1, keepdims=True)


def scores_grad(probs, grad_context, values):
    grad_probs = dot_nt(grad_context, values)
    inner = jnp.sum(grad_probs * probs, axis=-1, keepdims=True)
    return (probs * (grad_probs - inner)).astype(jnp.bfloat16)


def side_by_side(parts):
    return jnp.concatenate(parts, axis=1).astype(jnp.bfloat16)


def enc_forward_kernel(
    core, lengths, x, own, other, gains, biases, normed, queries, keys, values, context, probs
):
    first = core[0] == 0
    rows = x.shape[0]
    normed_rows = layer_norm(x[...], gains[0:1, :], biases[0:1, :])
    normed[...] = normed_rows
    projected = []
    for kind, out in enumerate((queries, keys, values)):
        matrix = jnp.where(first, own[kind], other[kind])
        block = dot_nt(normed_rows, matrix).astype(jnp.bfloat16)
        out[...] = block
        projected.append(block)
    allowed = ids_along(lengths, (rows, 1), 0) == ids_along(lengths, (1, rows), 1)
    parts = []
    for head in range(queries.shape[1] // HS):
        at = slice(head * HS, (head + 1) * HS)
        weights = softmax(projected[0][:, at], projected[1][:, at], allowed)
        probs[head] = weights
        parts.append(dot_nn(weights.astype(jnp.bfloat16), projected[2][:, at]))
    block = side_by_side(parts)
    for copy in range(context.shape[0]):
        context[copy] = block


def dec_kernel(
    core, place, frame_lens, token_lens, x, context, out_part, out_rest, own, other, tokens,
    upstream, gains, biases, partial, states, normed, key_grad, value_grad, dec_context, scratch,
):
    first = core[0] == 0
    rows, features = x.shape
    half = features // 2
    all_context = jnp.concatenate([context[c] for c in range(context.shape[0])], axis=1)
    mine = dot_nn(all_context, out_part[...])
    rest = dot_nn(all_context, out_rest[...])
    summed = jnp.concatenate(
        [jnp.where(first, mine, rest), jnp.where(first, rest, mine)], axis=1
    )
    scratch[...] = x[...].astype(jnp.float32) + summed
    all_states = scratch[...].astype(jnp.bfloat16)
    shard = states.shape[0]
    start = pl.multiple_of(place[0] * shard, shard)
    states[...] = scratch[pl.ds(start, shard), :].astype(jnp.bfloat16)
    normed_rows = layer_norm(all_states, gains[2:3, :], biases[2:3, :])
    normed[...] = normed_rows
    normed_tokens = layer_norm(tokens[...], gains[1:2, :], biases[1:2, :])
    matrix = [jnp.where(first, other[kind], own[kind]) for kind in range(4)]
    queries = dot_nt(normed_tokens, matrix[0]).astype(jnp.bfloat16)
    keys = dot_nt(normed_rows, matrix[1]).astype(jnp.bfloat16)
    values = dot_nt(normed_rows, matrix[2]).astype(jnp.bfloat16)
    grad_context = dot_nt(upstream[...], matrix[3]).astype(jnp.bfloat16)
    count = tokens.shape[0]
    allowed = ids_along(token_lens, (count, 1), 0) == ids_along(frame_lens, (1, rows), 1)
    key_parts, value_parts, context_parts = [], [], []
    for head in range(queries.shape[1] // HS):
        at = slice(head * HS, (head + 1) * HS)
        weights = softmax(queries[:, at], keys[:, at], allowed)
        rounded = weights.astype(jnp.bfloat16)
        context_parts.append(dot_nn(rounded, values[:, at]))
        grad_scores = scores_grad(weights, grad_context[:, at], values[:, at])
        key_parts.append(dot_tn(grad_scores, queries[:, at]) * SCALING)
        value_parts.append(dot_tn(rounded, grad_context[:, at]))
    key_block, value_block = side_by_side(key_parts), side_by_side(value_parts)
    key_grad[...] = key_block
    value_grad[...] = value_block
    dec_context[...] = side_by_side(context_parts)
    partial[...] = (dot_nn(key_block, matrix[1]) + dot_nn(value_block, matrix[2])).astype(
        jnp.bfloat16
    )


def store_terms(products, term):
    high = products[0].shape[0]
    for index, product in enumerate(products):
        term[index * high : (index + 1) * high, :] = product.astype(jnp.bfloat16)


def dec_terms_kernel(key_grad, value_grad, context, normed, upstream, term):
    products = [
        dot_tn(key_grad[...], normed[...]),
        dot_tn(value_grad[...], normed[...]),
        dot_tn(context[...], upstream[...]),
    ]
    store_terms(products, term)


def norm_backward_kernel(pieces, states, gains, grads):
    summed = pieces[0].astype(jnp.float32)
    for index in range(1, pieces.shape[0]):
        summed = summed + pieces[index].astype(jnp.float32)
    center, inverse = row_stats(states[...].astype(jnp.float32))
    normed = center * inverse
    scaled = summed * gains[2:3, :]
    result = inverse * (
        scaled
        - jnp.mean(scaled, axis=-1, keepdims=True)
        - normed * jnp.mean(scaled * normed, axis=-1, keepdims=True)
    )
    block = result.astype(jnp.bfloat16)
    for copy in range(grads.shape[0]):
        grads[copy] = block


def enc_backward_kernel(
    core, grads, own, other, queries, values, probs, context, normed, term
):
    first = core[0] == 0
    grad_rows = grads[...]
    att_grad = dot_nt(grad_rows, jnp.where(first, own[0], other[0])).astype(jnp.bfloat16)
    query_rows, value_rows = queries[...], values[...]
    key_parts, value_parts = [], []
    for head in range(query_rows.shape[1] // HS):
        at = slice(head * HS, (head + 1) * HS)
        weights = probs[head]
        grad_scores = scores_grad(weights, att_grad[:, at], value_rows[:, at])
        key_parts.append(dot_tn(grad_scores, query_rows[:, at]) * SCALING)
        value_parts.append(dot_tn(weights.astype(jnp.bfloat16), att_grad[:, at]))
    products = [
        dot_tn(side_by_side(key_parts), normed[...]),
        dot_tn(side_by_side(value_parts), normed[...]),
        dot_tn(context[0], grad_rows),
    ]
    store_terms(products, term)


def chunks_kernel(core, enc_term, enc_sent, dec_term, dec_sent, tiles):
    first = core[0] == 0
    rows, cols = enc_term.shape
    high = rows // 8
    for block in range(cols // 128):
        at = slice(block * 128, (block + 1) * 128)
        kept = jnp.where(first, enc_term[:, at], dec_term[:, at])
        received = jnp.where(first, enc_sent[:, at], dec_sent[:, at])
        total = kept.astype(jnp.float32) + received.astype(jnp.float32)
        part = total.reshape(high, 8, 128)
        tiles[block * high : (block + 1) * high] = part.astype(jnp.bfloat16)


def sum_kernel(pieces, total):
    summed = pieces[0].astype(jnp.float32)
    for index in range(1, pieces.shape[0]):
        summed = summed + pieces[index].astype(jnp.float32)
    total[...] = summed.astype(jnp.bfloat16)


def sum_copies_kernel(pieces, copies):
    summed = pieces[0].astype(jnp.float32)
    for index in range(1, pieces.shape[0]):
        summed = summed + pieces[index].astype(jnp.float32)
    block = summed.astype(jnp.bfloat16)
    for copy in range(copies.shape[0]):
        copies[copy] = block


def copies_kernel(block, copies):
    for copy in range(copies.shape[0]):
        copies[copy] = block[...]


def from_chunks_kernel(tiles, gradient):
    rows, cols = gradient.shape
    high = rows // 8
    for block in range(cols // 128):
        part = tiles[block * high : (block + 1) * high].astype(jnp.float32)
        gradient[:, block * 128 : (block + 1) * 128] = part.reshape(rows, 128)


def call(kernel, outs, scalars, arrays, blocks=None, scratch=()):
    blocks = blocks or {}

    def spec(index, array):
        shape, at = blocks.get(index, (array.shape, (0,) * array.ndim))
        return pl.BlockSpec(shape, lambda i: at)

    result = pl.pallas_call(
        kernel,
        grid=(1,),
        out_shape=[jax.ShapeDtypeStruct(shape, dtype) for shape, dtype in outs],
        in_specs=[pl.BlockSpec(memory_space=pltpu.SMEM) for _ in scalars]
        + [spec(index, array) for index, array in enumerate(arrays)],
        out_specs=[
            pl.BlockSpec(shape, functools.partial(lambda n, i: (0,) * n, len(shape)))
            for shape, _ in outs
        ],
        scratch_shapes=list(scratch),
        compiler_params=pltpu.CompilerParams(vmem_limit_bytes=48 << 20),
    )(*scalars, *arrays)
    return result[0] if len(outs) == 1 else result


def swap(block):
    return lax.ppermute(block, "segment", [(0, 1), (1, 0)])


def shards(
    frames, dec_states, out_grad, frame_lengths, token_lengths, weights, norm_gains, norm_biases
):
    bf16, f32 = jnp.bfloat16, jnp.float32
    core = lax.axis_index("segment")
    first = core == 0
    own = weights[0]
    shard_rows, features = frames.shape[1:]
    mp = lax.axis_size("mp")
    dp = lax.axis_size("dp")
    head_cols = own.shape[1]
    heads = head_cols // HS
    rows = shard_rows * mp
    half = features // 2
    slow = 4 if dp % 4 == 0 else 1
    quick = dp // slow
    slow_groups = [[a * quick + b for a in range(slow)] for b in range(quick)]
    quick_groups = [[a * quick + b for b in range(quick)] for a in range(slow)]

    def mine(array):
        return lax.dynamic_index_in_dim(array, core, 0, keepdims=False)

    def exchange(blocks, axis="mp", groups=None):
        return lax.all_to_all(blocks, axis, 0, 0, axis_index_groups=groups)

    core_id = core.astype(jnp.int32).reshape(1)
    place = lax.axis_index("mp").astype(jnp.int32).reshape(1)
    inputs = mine(frames)
    tokens = mine(dec_states)
    upstream = mine(out_grad)
    frame_lens = mine(frame_lengths)[0]
    token_lens = mine(token_lengths)[0]

    out_sent = lax.ppermute(own[3, :, half:], "segment", [(0, 1)])
    out_part = jnp.where(first, own[3, :, :half], out_sent)
    out_part = lax.all_gather(out_part, "mp", axis=0, tiled=True)

    copies = jnp.broadcast_to(inputs[None], (mp, shard_rows, features))
    enc_full = exchange(copies).reshape(rows, features)
    other = swap(own)

    weight_block = ((3, head_cols, features), (0, 0, 0))
    normed, queries, keys, values, context, probs = call(
        enc_forward_kernel,
        [
            ((rows, features), bf16),
            ((rows, head_cols), bf16),
            ((rows, head_cols), bf16),
            ((rows, head_cols), bf16),
            ((mp, rows, head_cols), bf16),
            ((heads, rows, rows), f32),
        ],
        (core_id, frame_lens),
        (enc_full, own, other, norm_gains, norm_biases),
        {1: weight_block, 2: weight_block},
    )
    context_full, out_part = lax.optimization_barrier((exchange(context), out_part))
    out_rest = swap(out_part)
    partial, states, state_normed, dec_key_grad, dec_value_grad, dec_context = call(
        dec_kernel,
        [
            ((rows, features), bf16),
            ((shard_rows, features), bf16),
            ((rows, features), bf16),
            ((rows, head_cols), bf16),
            ((rows, head_cols), bf16),
            ((tokens.shape[0], head_cols), bf16),
        ],
        (core_id, place, frame_lens, token_lens),
        (
            enc_full, context_full, out_part, out_rest, own, other, tokens, upstream,
            norm_gains, norm_biases,
        ),
        scratch=[pltpu.VMEM((rows, features), f32)],
    )
    pieces = exchange(partial.reshape(mp, shard_rows, features))
    whole = [((3 * head_cols, features), bf16)]
    dec_term = call(
        dec_terms_kernel,
        whole,
        (),
        (dec_key_grad, dec_value_grad, dec_context, state_normed, upstream),
    )
    grads = call(
        norm_backward_kernel,
        [((mp, shard_rows, features), bf16)],
        (),
        (pieces, states, norm_gains),
    )
    grads_full = exchange(grads).reshape(rows, features)
    last_block = ((1, head_cols, features), (3, 0, 0))
    first_context = ((1, rows, head_cols), (0, 0, 0))
    enc_term = call(
        enc_backward_kernel,
        whole,
        (core_id,),
        (grads_full, own, other, queries, values, probs, context, normed),
        {1: last_block, 2: last_block, 6: first_context},
    )
    dec_sent = lax.ppermute(dec_term, "segment", [(0, 1)])
    enc_sent = lax.ppermute(enc_term, "segment", [(1, 0)])
    count = 3 * head_cols * features // 1024
    tiles = call(
        chunks_kernel,
        [((count, 8, 128), bf16)],
        (core_id,),
        (enc_term, enc_sent, dec_term, dec_sent),
    )
    parts = exchange(tiles.reshape(slow, count // slow, 8, 128), "dp", slow_groups)
    parts = call(sum_kernel, [((count // slow, 8, 128), bf16)], (), (parts,))
    parts = exchange(parts.reshape(quick, count // dp, 8, 128), "dp", quick_groups)
    parts = call(sum_copies_kernel, [((quick, count // dp, 8, 128), bf16)], (), (parts,))
    parts = exchange(parts, "dp", quick_groups).reshape(count // slow, 8, 128)
    parts = call(copies_kernel, [((slow, count // slow, 8, 128), bf16)], (), (parts,))
    parts = exchange(parts, "dp", slow_groups).reshape(count, 8, 128)
    gradient = call(from_chunks_kernel, [((3 * head_cols, features), f32)], (), (parts,))
    return gradient.reshape(1, 3, head_cols, features)


def solution(mesh):
    placed = (
        P(None, ("dp", "mp"), None),
        P(None, "dp", None),
        P(None, "dp", None),
        P(None, "dp", None),
        P(None, "dp", None),
        P("segment", None, "mp", None),
        P(),
        P(),
    )
    return jax.shard_map(
        shards,
        mesh=mesh,
        in_specs=placed,
        out_specs=P("segment", None, "mp", None),
        check_vma=False,
    )
```

```python
import functools
import math

import jax
import jax.numpy as jnp
from jax import lax
from jax.experimental import pallas as pl
from jax.experimental.pallas import tpu as pltpu
from jax.sharding import PartitionSpec as P

HS = 64
SCALING = 1.0 / math.sqrt(HS)
EPSILON = 1e-05
ROWS_DIMS = (((0,), (0,)), ((), ()))
FEAT_DIMS = (((1,), (1,)), ((), ()))


def dot_nn(a, b):
    return lax.dot_general(a, b, (((1,), (0,)), ((), ())), preferred_element_type=jnp.float32)


def dot_nt(a, b):
    return lax.dot_general(a, b, FEAT_DIMS, preferred_element_type=jnp.float32)


def dot_tn(a, b):
    return lax.dot_general(a, b, ROWS_DIMS, preferred_element_type=jnp.float32)


def row_stats(values):
    center = values - jnp.mean(values, axis=-1, keepdims=True)
    variance = jnp.mean(center * center, axis=-1, keepdims=True)
    return center, lax.rsqrt(variance + EPSILON)


def layer_norm(values, norm_gain, offset):
    center, inverse = row_stats(values.astype(jnp.float32))
    return (center * inverse * norm_gain + offset).astype(jnp.bfloat16)


def ids_along(lengths_ref, row, shape, axis):
    places = lax.broadcasted_iota(jnp.int32, shape, axis)
    bound = 0
    ids = jnp.zeros(shape, jnp.int32)
    for piece in range(lengths_ref.shape[2]):
        bound = bound + lengths_ref[row, 0, piece]
        ids = ids + (places >= bound).astype(jnp.int32)
    return ids


def softmax(queries, keys, allowed):
    scores = jnp.where(allowed, dot_nt(queries, keys) * SCALING, -1e30)
    raised = jnp.exp(scores - jnp.max(scores, axis=-1, keepdims=True))
    return raised / jnp.sum(raised, axis=-1, keepdims=True)


def scores_grad(probs, grad_context, values):
    grad_probs = dot_nt(grad_context, values)
    inner = jnp.sum(grad_probs * probs, axis=-1, keepdims=True)
    return (probs * (grad_probs - inner)).astype(jnp.bfloat16)


def side_by_side(parts):
    return jnp.concatenate(parts, axis=1).astype(jnp.bfloat16)


def enc_forward_kernel(
    core, lengths, x, own, other, gains, biases, normed, queries, values, context, copies, probs
):
    first = core[0] == 0
    rows = x.shape[0]
    normed_rows = layer_norm(x[...], gains[0:1, :], biases[0:1, :])
    normed[...] = normed_rows
    projected = []
    for kind in range(3):
        matrix = jnp.where(first, own[kind], other[kind])
        projected.append(dot_nt(normed_rows, matrix).astype(jnp.bfloat16))
    queries[...] = projected[0]
    values[...] = projected[2]
    allowed = ids_along(lengths, core[0], (rows, 1), 0) == ids_along(lengths, core[0], (1, rows), 1)
    parts = []
    for head in range(queries.shape[1] // HS):
        at = slice(head * HS, (head + 1) * HS)
        weights = softmax(projected[0][:, at], projected[1][:, at], allowed)
        probs[head] = weights
        parts.append(dot_nn(weights.astype(jnp.bfloat16), projected[2][:, at]))
    block = side_by_side(parts)
    context[...] = block
    for copy in range(copies.shape[0]):
        copies[copy] = block


def token_kernel(core, tokens, upstream, own, other, gains, biases, queries, grad_context):
    first = core[0] == 0
    own_tokens = jnp.where(first, tokens[0], tokens[1])
    normed_tokens = layer_norm(own_tokens, gains[1:2, :], biases[1:2, :])
    matrix = jnp.where(first, other[0], own[0])
    queries[...] = dot_nt(normed_tokens, matrix).astype(jnp.bfloat16)
    matrix = jnp.where(first, other[3], own[3])
    own_upstream = jnp.where(first, upstream[0], upstream[1])
    grad_context[...] = dot_nt(own_upstream, matrix).astype(jnp.bfloat16)


def half_context(context, second):
    heads = []
    for device in range(context.shape[0]):
        block = context[device]
        heads.append(jnp.where(second, block[:, HS:], block[:, :HS]))
    return jnp.concatenate(heads, axis=1)


def half_states_kernel(core, x, context, out_part, states):
    left = half_context(context, core[0] == 1)
    states[...] = x[...].astype(jnp.float32) + dot_nn(left, out_part[...])


def dec_kernel(
    core, place, frame_lens, token_lens, half_states, context, out_rest, own, other, token_queries,
    token_grads, gains, biases, partial, states, normed, key_grad, value_grad, dec_context, scratch,
):
    first = core[0] == 0
    rows = half_states.shape[0]
    left = half_context(context, core[0] == 0)
    scratch[...] = half_states[...] + dot_nn(left, out_rest[...])
    all_states = scratch[...].astype(jnp.bfloat16)
    shard = states.shape[0]
    start = pl.multiple_of(place[0] * shard, shard)
    states[...] = scratch[pl.ds(start, shard), :].astype(jnp.bfloat16)
    normed_rows = layer_norm(all_states, gains[2:3, :], biases[2:3, :])
    normed[...] = normed_rows
    matrix = [jnp.where(first, other[kind], own[kind]) for kind in (1, 2)]
    queries = token_queries[...]
    grad_context = token_grads[...]
    keys = dot_nt(normed_rows, matrix[0]).astype(jnp.bfloat16)
    values = dot_nt(normed_rows, matrix[1]).astype(jnp.bfloat16)
    count = queries.shape[0]
    token_ids = ids_along(token_lens, core[0], (count, 1), 0)
    allowed = token_ids == ids_along(frame_lens, core[0], (1, rows), 1)
    key_parts, value_parts, context_parts = [], [], []
    for head in range(queries.shape[1] // HS):
        at = slice(head * HS, (head + 1) * HS)
        weights = softmax(queries[:, at], keys[:, at], allowed)
        rounded = weights.astype(jnp.bfloat16)
        context_parts.append(dot_nn(rounded, values[:, at]))
        grad_scores = scores_grad(weights, grad_context[:, at], values[:, at])
        key_parts.append(dot_tn(grad_scores, queries[:, at]) * SCALING)
        value_parts.append(dot_tn(rounded, grad_context[:, at]))
    key_block, value_block = side_by_side(key_parts), side_by_side(value_parts)
    key_grad[...] = key_block
    value_grad[...] = value_block
    dec_context[...] = side_by_side(context_parts)
    partial[...] = (dot_nn(key_block, matrix[0]) + dot_nn(value_block, matrix[1])).astype(
        jnp.bfloat16
    )


def store_terms(products, term):
    high = products[0].shape[0]
    for index, product in enumerate(products):
        term[index * high : (index + 1) * high, :] = product.astype(jnp.bfloat16)


def dec_terms_kernel(core, key_grad, value_grad, context, normed, upstream, term):
    products = [
        dot_tn(key_grad[...], normed[...]),
        dot_tn(value_grad[...], normed[...]),
        dot_tn(context[...], jnp.where(core[0] == 0, upstream[0], upstream[1])),
    ]
    store_terms(products, term)


def norm_backward_kernel(pieces, states, gains, grads):
    summed = pieces[0].astype(jnp.float32)
    for index in range(1, pieces.shape[0]):
        summed = summed + pieces[index].astype(jnp.float32)
    center, inverse = row_stats(states[...].astype(jnp.float32))
    normed = center * inverse
    scaled = summed * gains[2:3, :]
    result = inverse * (
        scaled
        - jnp.mean(scaled, axis=-1, keepdims=True)
        - normed * jnp.mean(scaled * normed, axis=-1, keepdims=True)
    )
    block = result.astype(jnp.bfloat16)
    for copy in range(grads.shape[0]):
        grads[copy] = block


def enc_backward_kernel(
    core, grads, own, other, queries, values, probs, context, normed, term
):
    first = core[0] == 0
    grad_rows = grads[...]
    att_grad = dot_nt(grad_rows, jnp.where(first, own[0], other[0])).astype(jnp.bfloat16)
    query_rows, value_rows = queries[...], values[...]
    key_parts, value_parts = [], []
    for head in range(query_rows.shape[1] // HS):
        at = slice(head * HS, (head + 1) * HS)
        weights = probs[head]
        grad_scores = scores_grad(weights, att_grad[:, at], value_rows[:, at])
        key_parts.append(dot_tn(grad_scores, query_rows[:, at]) * SCALING)
        value_parts.append(dot_tn(weights.astype(jnp.bfloat16), att_grad[:, at]))
    products = [
        dot_tn(side_by_side(key_parts), normed[...]),
        dot_tn(side_by_side(value_parts), normed[...]),
        dot_tn(context[...], grad_rows),
    ]
    store_terms(products, term)


def chunks_kernel(core, enc_term, enc_sent, dec_term, dec_sent, tiles):
    first = core[0] == 0
    rows, cols = enc_term.shape
    high = rows // 8
    for block in range(cols // 128):
        at = slice(block * 128, (block + 1) * 128)
        kept = jnp.where(first, enc_term[:, at], dec_term[:, at])
        received = jnp.where(first, enc_sent[:, at], dec_sent[:, at])
        total = kept.astype(jnp.float32) + received.astype(jnp.float32)
        part = total.reshape(high, 8, 128)
        tiles[block * high : (block + 1) * high] = part.astype(jnp.bfloat16)


def sum_copies_kernel(pieces, copies):
    summed = pieces[0].astype(jnp.float32)
    for index in range(1, pieces.shape[0]):
        summed = summed + pieces[index].astype(jnp.float32)
    block = summed.astype(jnp.bfloat16)
    for copy in range(copies.shape[0]):
        copies[copy] = block


def pick_copies_kernel(core, blocks, copies):
    block = jnp.where(core[0] == 0, blocks[0], blocks[1])
    for copy in range(copies.shape[0]):
        copies[copy] = block


def from_chunks_kernel(tiles, gradient):
    rows, cols = gradient.shape
    high = rows // 8
    for block in range(cols // 128):
        part = tiles[block * high : (block + 1) * high].astype(jnp.float32)
        gradient[:, block * 128 : (block + 1) * 128] = part.reshape(rows, 128)


def call(kernel, outs, scalars, arrays, blocks=None, scratch=(), kept=(), read=()):
    blocks = blocks or {}

    def spec(index, array):
        shape, at = blocks.get(index, (array.shape, (0,) * array.ndim))
        return pl.BlockSpec(shape, lambda i: at)

    def out(index, shape, dtype):
        return pltpu.HBM(shape, dtype) if index in kept else jax.ShapeDtypeStruct(shape, dtype)

    arrays = [
        pltpu.with_memory_space_constraint(array, pltpu.HBM) if index in read else array
        for index, array in enumerate(arrays)
    ]
    result = pl.pallas_call(
        kernel,
        grid=(1,),
        out_shape=[out(index, *what) for index, what in enumerate(outs)],
        in_specs=[pl.BlockSpec(memory_space=pltpu.SMEM) for _ in scalars]
        + [spec(index, array) for index, array in enumerate(arrays)],
        out_specs=[
            pl.BlockSpec(shape, functools.partial(lambda n, i: (0,) * n, len(shape)))
            for shape, _ in outs
        ],
        scratch_shapes=list(scratch),
        compiler_params=pltpu.CompilerParams(vmem_limit_bytes=48 << 20),
    )(*scalars, *arrays)
    return result[0] if len(outs) == 1 else result


def swap(block):
    return lax.ppermute(block, "segment", [(0, 1), (1, 0)])


def shards(
    frames, dec_states, out_grad, frame_lengths, token_lengths, weights, norm_gains, norm_biases
):
    bf16, f32 = jnp.bfloat16, jnp.float32
    core = lax.axis_index("segment")
    first = core == 0
    own = weights[0]
    shard_rows, features = frames.shape[1:]
    mp = lax.axis_size("mp")
    dp = lax.axis_size("dp")
    head_cols = own.shape[1]
    heads = head_cols // HS
    rows = shard_rows * mp
    count = dec_states.shape[1]
    near_groups = [[x * 8 + y * 2 + b for x in range(4) for b in range(2)] for y in range(4)]
    far_groups = [[x * 8 + y * 2 + b for y in range(4)] for x in range(4) for b in range(2)]
    near, far = len(near_groups[0]), len(far_groups[0])

    def exchange(blocks, axis="mp", groups=None):
        return lax.all_to_all(blocks, axis, 0, 0, axis_index_groups=groups)

    core_id = core.astype(jnp.int32).reshape(1)
    place = lax.axis_index("mp").astype(jnp.int32).reshape(1)

    out_sent = lax.ppermute(own[3, HS:], "segment", [(0, 1)])
    copies = call(
        pick_copies_kernel, [((mp, shard_rows, features), bf16)], (core_id,), (frames,)
    )
    out_part = jnp.where(first, own[3, :HS], out_sent)
    out_part = lax.all_gather(out_part, "mp", axis=0, tiled=True)
    enc_full = exchange(copies).reshape(rows, features)
    other = swap(own)

    token_queries, token_grads = call(
        token_kernel,
        [((count, head_cols), bf16)] * 2,
        (core_id,),
        (dec_states, out_grad, own, other, norm_gains, norm_biases),
        kept=(0, 1),
        read=(0, 1, 2, 3),
    )
    weight_block = ((3, head_cols, features), (0, 0, 0))
    normed, queries, values, context, context_copies, probs = call(
        enc_forward_kernel,
        [
            ((rows, features), bf16),
            ((rows, head_cols), bf16),
            ((rows, head_cols), bf16),
            ((rows, head_cols), bf16),
            ((mp, rows, head_cols), bf16),
            ((heads, rows, rows), f32),
        ],
        (core_id, frame_lengths),
        (enc_full, own, other, norm_gains, norm_biases),
        {1: weight_block, 2: weight_block},
        kept=(0, 1, 2, 3, 5),
        read=(1,),
    )
    context_full, out_part = lax.optimization_barrier((exchange(context_copies), out_part))
    out_rest = swap(out_part)
    half_states = call(
        half_states_kernel,
        [((rows, features), f32)],
        (core_id,),
        (enc_full, context_full, out_part),
        read=(2,),
    )
    partial, states, state_normed, dec_key_grad, dec_value_grad, dec_context = call(
        dec_kernel,
        [
            ((rows, features), bf16),
            ((shard_rows, features), bf16),
            ((rows, features), bf16),
            ((rows, head_cols), bf16),
            ((rows, head_cols), bf16),
            ((count, head_cols), bf16),
        ],
        (core_id, place, frame_lengths, token_lengths),
        (
            half_states, context_full, out_rest, own, other, token_queries, token_grads,
            norm_gains, norm_biases,
        ),
        scratch=[pltpu.VMEM((rows, features), f32)],
        kept=(1, 2, 3, 4, 5),
        read=(3, 4, 5, 6),
    )
    pieces = exchange(partial.reshape(mp, shard_rows, features))
    whole = [((3 * head_cols, features), bf16)]
    dec_term = call(
        dec_terms_kernel,
        whole,
        (core_id,),
        (dec_key_grad, dec_value_grad, dec_context, state_normed, out_grad),
        kept=(0,),
        read=(0, 1, 2, 3, 4),
    )
    grads = call(
        norm_backward_kernel,
        [((mp, shard_rows, features), bf16)],
        (),
        (pieces, states, norm_gains),
        read=(1,),
    )
    grads_full = exchange(grads).reshape(rows, features)
    last_block = ((1, head_cols, features), (3, 0, 0))
    enc_term = call(
        enc_backward_kernel,
        whole,
        (core_id,),
        (grads_full, own, other, queries, values, probs, context, normed),
        {1: last_block, 2: last_block},
        read=(1, 2, 3, 4, 5, 6, 7),
    )
    dec_sent = lax.ppermute(dec_term, "segment", [(0, 1)])
    enc_sent = lax.ppermute(enc_term, "segment", [(1, 0)])
    size = 3 * head_cols * features // 1024
    each = size // near
    tiles = call(
        chunks_kernel,
        [((size, 8, 128), bf16)],
        (core_id,),
        (enc_term, enc_sent, dec_term, dec_sent),
        read=(2,),
    )
    parts = exchange(tiles.reshape(near, each, 8, 128), "dp", near_groups)
    parts = call(sum_copies_kernel, [((far, each, 8, 128), bf16)], (), (parts,))
    parts = exchange(parts, "dp", far_groups)
    parts = call(sum_copies_kernel, [((near, each, 8, 128), bf16)], (), (parts,))
    parts = exchange(parts, "dp", near_groups).reshape(size, 8, 128)
    gradient = call(from_chunks_kernel, [((3 * head_cols, features), f32)], (), (parts,))
    return gradient.reshape(1, 3, head_cols, features)


def solution(mesh):
    placed = (
        P(None, ("dp", "mp"), None),
        P(None, "dp", None),
        P(None, "dp", None),
        P(None, "dp", None),
        P(None, "dp", None),
        P("segment", None, "mp", None),
        P(),
        P(),
    )
    return jax.shard_map(
        shards,
        mesh=mesh,
        in_specs=placed,
        out_specs=P("segment", None, "mp", None),
        check_vma=False,
    )
```

```python
import functools
import math

import jax
import jax.numpy as jnp
from jax import lax
from jax.experimental import pallas as pl
from jax.experimental.pallas import tpu as pltpu
from jax.sharding import PartitionSpec as P

HS = 64
SCALING = 1.0 / math.sqrt(HS)
EPSILON = 1e-05
ROWS_DIMS = (((0,), (0,)), ((), ()))
FEAT_DIMS = (((1,), (1,)), ((), ()))


def dot_nn(a, b):
    return lax.dot_general(a, b, (((1,), (0,)), ((), ())), preferred_element_type=jnp.float32)


def dot_nt(a, b):
    return lax.dot_general(a, b, FEAT_DIMS, preferred_element_type=jnp.float32)


def dot_tn(a, b):
    return lax.dot_general(a, b, ROWS_DIMS, preferred_element_type=jnp.float32)


def row_stats(values):
    center = values - jnp.mean(values, axis=-1, keepdims=True)
    variance = jnp.mean(center * center, axis=-1, keepdims=True)
    return center, lax.rsqrt(variance + EPSILON)


def layer_norm(values, norm_gain, offset):
    center, inverse = row_stats(values.astype(jnp.float32))
    return (center * inverse * norm_gain + offset).astype(jnp.bfloat16)


def ids_along(lengths_ref, row, shape, axis):
    places = lax.broadcasted_iota(jnp.int32, shape, axis)
    bound = 0
    ids = jnp.zeros(shape, jnp.int32)
    for piece in range(lengths_ref.shape[2]):
        bound = bound + lengths_ref[row, 0, piece]
        ids = ids + (places >= bound).astype(jnp.int32)
    return ids


def softmax(queries, keys, allowed):
    scores = jnp.where(allowed, dot_nt(queries, keys) * SCALING, -1e30)
    raised = jnp.exp(scores - jnp.max(scores, axis=-1, keepdims=True))
    return raised / jnp.sum(raised, axis=-1, keepdims=True)


def scores_grad(probs, grad_context, values):
    grad_probs = dot_nt(grad_context, values)
    inner = jnp.sum(grad_probs * probs, axis=-1, keepdims=True)
    return (probs * (grad_probs - inner)).astype(jnp.bfloat16)


def side_by_side(parts):
    return jnp.concatenate(parts, axis=1).astype(jnp.bfloat16)


def enc_forward_kernel(
    core, lengths, x, own, other, gains, biases, normed, queries, values, context, copies, probs
):
    first = core[0] == 0
    rows = x.shape[0]
    normed_rows = layer_norm(x[...], gains[0:1, :], biases[0:1, :])
    normed[...] = normed_rows
    projected = []
    for kind in range(3):
        matrix = jnp.where(first, own[kind], other[kind])
        projected.append(dot_nt(normed_rows, matrix).astype(jnp.bfloat16))
    queries[...] = projected[0]
    values[...] = projected[2]
    allowed = ids_along(lengths, core[0], (rows, 1), 0) == ids_along(lengths, core[0], (1, rows), 1)
    parts = []
    for head in range(queries.shape[1] // HS):
        at = slice(head * HS, (head + 1) * HS)
        weights = softmax(projected[0][:, at], projected[1][:, at], allowed)
        probs[head] = weights
        parts.append(dot_nn(weights.astype(jnp.bfloat16), projected[2][:, at]))
    block = side_by_side(parts)
    context[...] = block
    for copy in range(copies.shape[0]):
        copies[copy] = block


def token_kernel(core, tokens, upstream, own, other, gains, biases, queries, grad_context):
    first = core[0] == 0
    own_tokens = jnp.where(first, tokens[0], tokens[1])
    normed_tokens = layer_norm(own_tokens, gains[1:2, :], biases[1:2, :])
    matrix = jnp.where(first, other[0], own[0])
    queries[...] = dot_nt(normed_tokens, matrix).astype(jnp.bfloat16)
    matrix = jnp.where(first, other[3], own[3])
    own_upstream = jnp.where(first, upstream[0], upstream[1])
    grad_context[...] = dot_nt(own_upstream, matrix).astype(jnp.bfloat16)


def half_context(context, second):
    heads = []
    for device in range(context.shape[0]):
        block = context[device]
        heads.append(jnp.where(second, block[:, HS:], block[:, :HS]))
    return jnp.concatenate(heads, axis=1)


def half_states_kernel(core, x, context, out_part, states):
    left = half_context(context, core[0] == 1)
    states[...] = x[...].astype(jnp.float32) + dot_nn(left, out_part[...])


def dec_kernel(
    core, place, frame_lens, token_lens, half_states, context, out_rest, own, other, token_queries,
    token_grads, gains, biases, partial, states, normed, key_grad, value_grad, dec_context, scratch,
):
    first = core[0] == 0
    rows = half_states.shape[0]
    left = half_context(context, core[0] == 0)
    scratch[...] = half_states[...] + dot_nn(left, out_rest[...])
    all_states = scratch[...].astype(jnp.bfloat16)
    shard = states.shape[0]
    start = pl.multiple_of(place[0] * shard, shard)
    states[...] = scratch[pl.ds(start, shard), :].astype(jnp.bfloat16)
    normed_rows = layer_norm(all_states, gains[2:3, :], biases[2:3, :])
    normed[...] = normed_rows
    matrix = [jnp.where(first, other[kind], own[kind]) for kind in (1, 2)]
    queries = token_queries[...]
    grad_context = token_grads[...]
    keys = dot_nt(normed_rows, matrix[0]).astype(jnp.bfloat16)
    values = dot_nt(normed_rows, matrix[1]).astype(jnp.bfloat16)
    count = queries.shape[0]
    token_ids = ids_along(token_lens, core[0], (count, 1), 0)
    allowed = token_ids == ids_along(frame_lens, core[0], (1, rows), 1)
    key_parts, value_parts, context_parts = [], [], []
    for head in range(queries.shape[1] // HS):
        at = slice(head * HS, (head + 1) * HS)
        weights = softmax(queries[:, at], keys[:, at], allowed)
        rounded = weights.astype(jnp.bfloat16)
        context_parts.append(dot_nn(rounded, values[:, at]))
        grad_scores = scores_grad(weights, grad_context[:, at], values[:, at])
        key_parts.append(dot_tn(grad_scores, queries[:, at]) * SCALING)
        value_parts.append(dot_tn(rounded, grad_context[:, at]))
    key_block, value_block = side_by_side(key_parts), side_by_side(value_parts)
    key_grad[...] = key_block
    value_grad[...] = value_block
    dec_context[...] = side_by_side(context_parts)
    partial[...] = (dot_nn(key_block, matrix[0]) + dot_nn(value_block, matrix[1])).astype(
        jnp.bfloat16
    )


def store_terms(products, term):
    high = products[0].shape[0]
    for index, product in enumerate(products):
        term[index * high : (index + 1) * high, :] = product.astype(jnp.bfloat16)


def dec_terms_kernel(core, key_grad, value_grad, context, normed, upstream, term):
    products = [
        dot_tn(key_grad[...], normed[...]),
        dot_tn(value_grad[...], normed[...]),
        dot_tn(context[...], jnp.where(core[0] == 0, upstream[0], upstream[1])),
    ]
    store_terms(products, term)


def norm_backward_kernel(pieces, states, gains, grads):
    summed = pieces[0].astype(jnp.float32)
    for index in range(1, pieces.shape[0]):
        summed = summed + pieces[index].astype(jnp.float32)
    center, inverse = row_stats(states[...].astype(jnp.float32))
    normed = center * inverse
    scaled = summed * gains[2:3, :]
    result = inverse * (
        scaled
        - jnp.mean(scaled, axis=-1, keepdims=True)
        - normed * jnp.mean(scaled * normed, axis=-1, keepdims=True)
    )
    block = result.astype(jnp.bfloat16)
    for copy in range(grads.shape[0]):
        grads[copy] = block


def enc_backward_kernel(
    core, grads, own, other, queries, values, probs, context, normed, term
):
    first = core[0] == 0
    grad_rows = grads[...]
    att_grad = dot_nt(grad_rows, jnp.where(first, own[0], other[0])).astype(jnp.bfloat16)
    query_rows, value_rows = queries[...], values[...]
    key_parts, value_parts = [], []
    for head in range(query_rows.shape[1] // HS):
        at = slice(head * HS, (head + 1) * HS)
        weights = probs[head]
        grad_scores = scores_grad(weights, att_grad[:, at], value_rows[:, at])
        key_parts.append(dot_tn(grad_scores, query_rows[:, at]) * SCALING)
        value_parts.append(dot_tn(weights.astype(jnp.bfloat16), att_grad[:, at]))
    products = [
        dot_tn(side_by_side(key_parts), normed[...]),
        dot_tn(side_by_side(value_parts), normed[...]),
        dot_tn(context[...], grad_rows),
    ]
    store_terms(products, term)


def chunks_kernel(core, enc_term, enc_sent, dec_term, dec_sent, tiles):
    first = core[0] == 0
    rows, cols = enc_term.shape
    high = rows // 8
    for block in range(cols // 128):
        at = slice(block * 128, (block + 1) * 128)
        kept = jnp.where(first, enc_term[:, at], dec_term[:, at])
        received = jnp.where(first, enc_sent[:, at], dec_sent[:, at])
        total = kept.astype(jnp.float32) + received.astype(jnp.float32)
        part = total.reshape(high, 8, 128)
        tiles[block * high : (block + 1) * high] = part.astype(jnp.bfloat16)


def sum_copies_kernel(pieces, copies):
    summed = pieces[0].astype(jnp.float32)
    for index in range(1, pieces.shape[0]):
        summed = summed + pieces[index].astype(jnp.float32)
    block = summed.astype(jnp.bfloat16)
    for copy in range(copies.shape[0]):
        copies[copy] = block


def pick_copies_kernel(core, blocks, copies):
    block = jnp.where(core[0] == 0, blocks[0], blocks[1])
    for copy in range(copies.shape[0]):
        copies[copy] = block


def from_chunks_kernel(tiles, gradient):
    rows, cols = gradient.shape
    high = rows // 8
    for block in range(cols // 128):
        part = tiles[block * high : (block + 1) * high].astype(jnp.float32)
        gradient[:, block * 128 : (block + 1) * 128] = part.reshape(rows, 128)


def call(
    kernel, outs, scalars, arrays, blocks=None, scratch=(), kept=(), read=(), cost=None
):
    blocks = blocks or {}

    def spec(index, array):
        shape, at = blocks.get(index, (array.shape, (0,) * array.ndim))
        return pl.BlockSpec(shape, lambda i: at)

    def out(index, shape, dtype):
        return pltpu.HBM(shape, dtype) if index in kept else jax.ShapeDtypeStruct(shape, dtype)

    arrays = [
        pltpu.with_memory_space_constraint(array, pltpu.HBM) if index in read else array
        for index, array in enumerate(arrays)
    ]
    result = pl.pallas_call(
        kernel,
        grid=(1,),
        out_shape=[out(index, *what) for index, what in enumerate(outs)],
        in_specs=[pl.BlockSpec(memory_space=pltpu.SMEM) for _ in scalars]
        + [spec(index, array) for index, array in enumerate(arrays)],
        out_specs=[
            pl.BlockSpec(shape, functools.partial(lambda n, i: (0,) * n, len(shape)))
            for shape, _ in outs
        ],
        scratch_shapes=list(scratch),
        cost_estimate=cost,
        compiler_params=pltpu.CompilerParams(vmem_limit_bytes=48 << 20),
    )(*scalars, *arrays)
    return result[0] if len(outs) == 1 else result


def swap(block):
    return lax.ppermute(block, "segment", [(0, 1), (1, 0)])


def shards(
    frames, dec_states, out_grad, frame_lengths, token_lengths, weights, norm_gains, norm_biases
):
    bf16, f32 = jnp.bfloat16, jnp.float32
    core = lax.axis_index("segment")
    first = core == 0
    own = weights[0]
    shard_rows, features = frames.shape[1:]
    mp = lax.axis_size("mp")
    dp = lax.axis_size("dp")
    head_cols = own.shape[1]
    heads = head_cols // HS
    rows = shard_rows * mp
    count = dec_states.shape[1]
    near_groups = [[x * 8 + y * 2 + b for x in range(4) for b in range(2)] for y in range(4)]
    far_groups = [[x * 8 + y * 2 + b for y in range(4)] for x in range(4) for b in range(2)]
    near, far = len(near_groups[0]), len(far_groups[0])

    def exchange(blocks, axis="mp", groups=None):
        return lax.all_to_all(blocks, axis, 0, 0, axis_index_groups=groups)

    core_id = core.astype(jnp.int32).reshape(1)
    place = lax.axis_index("mp").astype(jnp.int32).reshape(1)

    other = swap(own)
    copies = call(
        pick_copies_kernel, [((mp, shard_rows, features), bf16)], (core_id,), (frames,)
    )
    out_part = jnp.where(first, own[3, :HS], other[3, HS:])
    out_part = lax.all_gather(out_part, "mp", axis=0, tiled=True)
    enc_full = exchange(copies).reshape(rows, features)

    token_queries, token_grads = call(
        token_kernel,
        [((count, head_cols), bf16)] * 2,
        (core_id,),
        (dec_states, out_grad, own, other, norm_gains, norm_biases),
        kept=(0, 1),
        read=(0, 1, 2, 3),
    )
    weight_block = ((3, head_cols, features), (0, 0, 0))
    normed, queries, values, context, context_copies, probs = call(
        enc_forward_kernel,
        [
            ((rows, features), bf16),
            ((rows, head_cols), bf16),
            ((rows, head_cols), bf16),
            ((rows, head_cols), bf16),
            ((mp, rows, head_cols), bf16),
            ((heads, rows, rows), f32),
        ],
        (core_id, frame_lengths),
        (enc_full, own, other, norm_gains, norm_biases),
        {1: weight_block, 2: weight_block},
        kept=(0, 1, 2, 3, 5),
        read=(1,),
        cost=pl.CostEstimate(flops=3_000_000_000, transcendentals=0, bytes_accessed=0),
    )
    context_full, out_part, token_queries, token_grads = lax.optimization_barrier(
        (exchange(context_copies), out_part, token_queries, token_grads)
    )
    out_rest = swap(out_part)
    half_states = call(
        half_states_kernel,
        [((rows, features), f32)],
        (core_id,),
        (enc_full, context_full, out_part),
        read=(2,),
    )
    partial, states, state_normed, dec_key_grad, dec_value_grad, dec_context = call(
        dec_kernel,
        [
            ((rows, features), bf16),
            ((shard_rows, features), bf16),
            ((rows, features), bf16),
            ((rows, head_cols), bf16),
            ((rows, head_cols), bf16),
            ((count, head_cols), bf16),
        ],
        (core_id, place, frame_lengths, token_lengths),
        (
            half_states, context_full, out_rest, own, other, token_queries, token_grads,
            norm_gains, norm_biases,
        ),
        scratch=[pltpu.VMEM((rows, features), f32)],
        kept=(1, 2, 3, 4, 5),
        read=(3, 4, 5, 6),
    )
    pieces = exchange(partial.reshape(mp, shard_rows, features))
    whole = [((3 * head_cols, features), bf16)]
    dec_term = call(
        dec_terms_kernel,
        whole,
        (core_id,),
        (dec_key_grad, dec_value_grad, dec_context, state_normed, out_grad),
        kept=(0,),
        read=(0, 1, 2, 3, 4),
    )
    grads = call(
        norm_backward_kernel,
        [((mp, shard_rows, features), bf16)],
        (),
        (pieces, states, norm_gains),
        read=(1,),
    )
    grads_full = exchange(grads).reshape(rows, features)
    last_block = ((1, head_cols, features), (3, 0, 0))
    enc_term = call(
        enc_backward_kernel,
        whole,
        (core_id,),
        (grads_full, own, other, queries, values, probs, context, normed),
        {1: last_block, 2: last_block},
        read=(1, 2, 3, 4, 5, 6, 7),
    )
    dec_sent = lax.ppermute(dec_term, "segment", [(0, 1)])
    enc_sent = lax.ppermute(enc_term, "segment", [(1, 0)])
    size = 3 * head_cols * features // 1024
    each = size // near
    tiles = call(
        chunks_kernel,
        [((size, 8, 128), bf16)],
        (core_id,),
        (enc_term, enc_sent, dec_term, dec_sent),
        read=(2,),
    )
    parts = exchange(tiles.reshape(near, each, 8, 128), "dp", near_groups)
    parts = call(sum_copies_kernel, [((far, each, 8, 128), bf16)], (), (parts,))
    parts = exchange(parts, "dp", far_groups)
    parts = call(sum_copies_kernel, [((near, each, 8, 128), bf16)], (), (parts,))
    parts = exchange(parts, "dp", near_groups).reshape(size, 8, 128)
    gradient = call(from_chunks_kernel, [((3 * head_cols, features), f32)], (), (parts,))
    return gradient.reshape(1, 3, head_cols, features)


def solution(mesh):
    placed = (
        P(None, ("dp", "mp"), None),
        P(None, "dp", None),
        P(None, "dp", None),
        P(None, "dp", None),
        P(None, "dp", None),
        P("segment", None, "mp", None),
        P(),
        P(),
    )
    return jax.shard_map(
        shards,
        mesh=mesh,
        in_specs=placed,
        out_specs=P("segment", None, "mp", None),
        check_vma=False,
    )
```

```python
import functools
import math

import jax
import jax.numpy as jnp
from jax import lax
from jax.experimental import pallas as pl
from jax.experimental.pallas import tpu as pltpu
from jax.sharding import PartitionSpec as P

HS = 64
SCALING = 1.0 / math.sqrt(HS)
EPSILON = 1e-05
ROWS_DIMS = (((0,), (0,)), ((), ()))
FEAT_DIMS = (((1,), (1,)), ((), ()))


def dot_nn(a, b):
    return lax.dot_general(a, b, (((1,), (0,)), ((), ())), preferred_element_type=jnp.float32)


def dot_nt(a, b):
    return lax.dot_general(a, b, FEAT_DIMS, preferred_element_type=jnp.float32)


def dot_tn(a, b):
    return lax.dot_general(a, b, ROWS_DIMS, preferred_element_type=jnp.float32)


def row_stats(values):
    center = values - jnp.mean(values, axis=-1, keepdims=True)
    variance = jnp.mean(center * center, axis=-1, keepdims=True)
    return center, lax.rsqrt(variance + EPSILON)


def layer_norm(values, norm_gain, offset):
    center, inverse = row_stats(values.astype(jnp.float32))
    return (center * inverse * norm_gain + offset).astype(jnp.bfloat16)


def ids_along(lengths_ref, row, shape, axis):
    places = lax.broadcasted_iota(jnp.int32, shape, axis)
    bound = 0
    ids = jnp.zeros(shape, jnp.int32)
    for piece in range(lengths_ref.shape[2]):
        bound = bound + lengths_ref[row, 0, piece]
        ids = ids + (places >= bound).astype(jnp.int32)
    return ids


def softmax(queries, keys, allowed):
    scores = jnp.where(allowed, dot_nt(queries, keys) * SCALING, -1e30)
    raised = jnp.exp(scores - jnp.max(scores, axis=-1, keepdims=True))
    return raised / jnp.sum(raised, axis=-1, keepdims=True)


def scores_grad(probs, grad_context, values):
    grad_probs = dot_nt(grad_context, values)
    inner = jnp.sum(grad_probs * probs, axis=-1, keepdims=True)
    return (probs * (grad_probs - inner)).astype(jnp.bfloat16)


def side_by_side(parts):
    return jnp.concatenate(parts, axis=1).astype(jnp.bfloat16)


def enc_forward_kernel(
    core, lengths, x, own, other, gains, biases, normed, queries, values, context, copies, probs
):
    first = core[0] == 0
    rows = x.shape[0]
    normed_rows = layer_norm(x[...], gains[0:1, :], biases[0:1, :])
    normed[...] = normed_rows
    projected = []
    for kind in range(3):
        matrix = jnp.where(first, own[kind], other[kind])
        projected.append(dot_nt(normed_rows, matrix).astype(jnp.bfloat16))
    queries[...] = projected[0]
    values[...] = projected[2]
    allowed = ids_along(lengths, core[0], (rows, 1), 0) == ids_along(lengths, core[0], (1, rows), 1)
    parts = []
    for head in range(queries.shape[1] // HS):
        at = slice(head * HS, (head + 1) * HS)
        weights = softmax(projected[0][:, at], projected[1][:, at], allowed)
        probs[head] = weights
        parts.append(dot_nn(weights.astype(jnp.bfloat16), projected[2][:, at]))
    block = side_by_side(parts)
    context[...] = block
    for copy in range(copies.shape[0]):
        copies[copy] = block


def token_kernel(core, tokens, upstream, own, other, gains, biases, queries, grad_context):
    first = core[0] == 0
    own_tokens = jnp.where(first, tokens[0], tokens[1])
    normed_tokens = layer_norm(own_tokens, gains[1:2, :], biases[1:2, :])
    matrix = jnp.where(first, other[0], own[0])
    queries[...] = dot_nt(normed_tokens, matrix).astype(jnp.bfloat16)
    matrix = jnp.where(first, other[3], own[3])
    own_upstream = jnp.where(first, upstream[0], upstream[1])
    grad_context[...] = dot_nt(own_upstream, matrix).astype(jnp.bfloat16)


def half_context(context, second):
    heads = []
    devices = context.shape[0]
    for device in range(devices):
        block = jnp.where(second, context[devices - 1 - device], context[device])
        heads.append(jnp.where(second, block[:, HS:], block[:, :HS]))
    return jnp.concatenate(heads, axis=1)


def half_states_kernel(core, x, context, out_part, states):
    left = half_context(context, core[0] == 1)
    states[...] = x[...].astype(jnp.float32) + dot_nn(left, out_part[...])


def dec_kernel(
    core, place, frame_lens, token_lens, half_states, context, out_rest, own, other, token_queries,
    token_grads, gains, biases, partial, states, normed, key_grad, value_grad, dec_context, scratch,
):
    first = core[0] == 0
    rows = half_states.shape[0]
    left = half_context(context, core[0] == 0)
    scratch[...] = half_states[...] + dot_nn(left, out_rest[...])
    all_states = scratch[...].astype(jnp.bfloat16)
    shard = states.shape[0]
    start = pl.multiple_of(place[0] * shard, shard)
    states[...] = scratch[pl.ds(start, shard), :].astype(jnp.bfloat16)
    normed_rows = layer_norm(all_states, gains[2:3, :], biases[2:3, :])
    normed[...] = normed_rows
    matrix = [jnp.where(first, other[kind], own[kind]) for kind in (1, 2)]
    queries = token_queries[...]
    grad_context = token_grads[...]
    keys = dot_nt(normed_rows, matrix[0]).astype(jnp.bfloat16)
    values = dot_nt(normed_rows, matrix[1]).astype(jnp.bfloat16)
    count = queries.shape[0]
    token_ids = ids_along(token_lens, core[0], (count, 1), 0)
    allowed = token_ids == ids_along(frame_lens, core[0], (1, rows), 1)
    key_parts, value_parts, context_parts = [], [], []
    for head in range(queries.shape[1] // HS):
        at = slice(head * HS, (head + 1) * HS)
        weights = softmax(queries[:, at], keys[:, at], allowed)
        rounded = weights.astype(jnp.bfloat16)
        context_parts.append(dot_nn(rounded, values[:, at]))
        grad_scores = scores_grad(weights, grad_context[:, at], values[:, at])
        key_parts.append(dot_tn(grad_scores, queries[:, at]) * SCALING)
        value_parts.append(dot_tn(rounded, grad_context[:, at]))
    key_block, value_block = side_by_side(key_parts), side_by_side(value_parts)
    key_grad[...] = key_block
    value_grad[...] = value_block
    dec_context[...] = side_by_side(context_parts)
    partial[...] = (dot_nn(key_block, matrix[0]) + dot_nn(value_block, matrix[1])).astype(
        jnp.bfloat16
    )


def store_terms(products, term):
    high = products[0].shape[0]
    for index, product in enumerate(products):
        term[index * high : (index + 1) * high, :] = product.astype(jnp.bfloat16)


def dec_terms_kernel(core, key_grad, value_grad, context, normed, upstream, term):
    products = [
        dot_tn(key_grad[...], normed[...]),
        dot_tn(value_grad[...], normed[...]),
        dot_tn(context[...], jnp.where(core[0] == 0, upstream[0], upstream[1])),
    ]
    store_terms(products, term)


def norm_backward_kernel(pieces, states, gains, grads):
    summed = pieces[0].astype(jnp.float32)
    for index in range(1, pieces.shape[0]):
        summed = summed + pieces[index].astype(jnp.float32)
    center, inverse = row_stats(states[...].astype(jnp.float32))
    normed = center * inverse
    scaled = summed * gains[2:3, :]
    result = inverse * (
        scaled
        - jnp.mean(scaled, axis=-1, keepdims=True)
        - normed * jnp.mean(scaled * normed, axis=-1, keepdims=True)
    )
    block = result.astype(jnp.bfloat16)
    for copy in range(grads.shape[0]):
        grads[copy] = block


def enc_backward_kernel(
    core, grads, own, other, queries, values, probs, context, normed, term
):
    first = core[0] == 0
    grad_rows = grads[...]
    att_grad = dot_nt(grad_rows, jnp.where(first, own[0], other[0])).astype(jnp.bfloat16)
    query_rows, value_rows = queries[...], values[...]
    key_parts, value_parts = [], []
    for head in range(query_rows.shape[1] // HS):
        at = slice(head * HS, (head + 1) * HS)
        weights = probs[head]
        grad_scores = scores_grad(weights, att_grad[:, at], value_rows[:, at])
        key_parts.append(dot_tn(grad_scores, query_rows[:, at]) * SCALING)
        value_parts.append(dot_tn(weights.astype(jnp.bfloat16), att_grad[:, at]))
    products = [
        dot_tn(side_by_side(key_parts), normed[...]),
        dot_tn(side_by_side(value_parts), normed[...]),
        dot_tn(context[...], grad_rows),
    ]
    store_terms(products, term)


def chunks_kernel(core, enc_term, enc_sent, dec_term, dec_sent, tiles):
    first = core[0] == 0
    rows, cols = enc_term.shape
    high = rows // 8
    for block in range(cols // 128):
        at = slice(block * 128, (block + 1) * 128)
        kept = jnp.where(first, enc_term[:, at], dec_term[:, at])
        received = jnp.where(first, enc_sent[:, at], dec_sent[:, at])
        total = kept.astype(jnp.float32) + received.astype(jnp.float32)
        part = total.reshape(high, 8, 128)
        tiles[block * high : (block + 1) * high] = part.astype(jnp.bfloat16)


def sum_copies_kernel(pieces, copies):
    summed = pieces[0].astype(jnp.float32)
    for index in range(1, pieces.shape[0]):
        summed = summed + pieces[index].astype(jnp.float32)
    block = summed.astype(jnp.bfloat16)
    for copy in range(copies.shape[0]):
        copies[copy] = block


def pick_copies_kernel(core, blocks, copies):
    block = jnp.where(core[0] == 0, blocks[0], blocks[1])
    for copy in range(copies.shape[0]):
        copies[copy] = block


def from_chunks_kernel(tiles, gradient):
    rows, cols = gradient.shape
    high = rows // 8
    for block in range(cols // 128):
        part = tiles[block * high : (block + 1) * high].astype(jnp.float32)
        gradient[:, block * 128 : (block + 1) * 128] = part.reshape(rows, 128)


def call(
    kernel, outs, scalars, arrays, blocks=None, scratch=(), kept=(), read=(), cost=None
):
    blocks = blocks or {}

    def spec(index, array):
        shape, at = blocks.get(index, (array.shape, (0,) * array.ndim))
        return pl.BlockSpec(shape, lambda i: at)

    def out(index, shape, dtype):
        return pltpu.HBM(shape, dtype) if index in kept else jax.ShapeDtypeStruct(shape, dtype)

    arrays = [
        pltpu.with_memory_space_constraint(array, pltpu.HBM) if index in read else array
        for index, array in enumerate(arrays)
    ]
    result = pl.pallas_call(
        kernel,
        grid=(1,),
        out_shape=[out(index, *what) for index, what in enumerate(outs)],
        in_specs=[pl.BlockSpec(memory_space=pltpu.SMEM) for _ in scalars]
        + [spec(index, array) for index, array in enumerate(arrays)],
        out_specs=[
            pl.BlockSpec(shape, functools.partial(lambda n, i: (0,) * n, len(shape)))
            for shape, _ in outs
        ],
        scratch_shapes=list(scratch),
        cost_estimate=cost,
        compiler_params=pltpu.CompilerParams(vmem_limit_bytes=48 << 20),
    )(*scalars, *arrays)
    return result[0] if len(outs) == 1 else result


def swap(block):
    return lax.ppermute(block, "segment", [(0, 1), (1, 0)])


def shards(
    frames, dec_states, out_grad, frame_lengths, token_lengths, weights, norm_gains, norm_biases
):
    bf16, f32 = jnp.bfloat16, jnp.float32
    core = lax.axis_index("segment")
    first = core == 0
    own = weights[0]
    shard_rows, features = frames.shape[1:]
    mp = lax.axis_size("mp")
    dp = lax.axis_size("dp")
    head_cols = own.shape[1]
    heads = head_cols // HS
    rows = shard_rows * mp
    count = dec_states.shape[1]
    near_groups = [[x * 8 + y * 2 + b for x in range(4) for b in range(2)] for y in range(4)]
    far_groups = [[x * 8 + y * 2 + b for y in range(4)] for x in range(4) for b in range(2)]
    near, far = len(near_groups[0]), len(far_groups[0])

    def exchange(blocks, axis="mp", groups=None):
        return lax.all_to_all(blocks, axis, 0, 0, axis_index_groups=groups)

    core_id = core.astype(jnp.int32).reshape(1)
    place = lax.axis_index("mp").astype(jnp.int32).reshape(1)

    copies = call(
        pick_copies_kernel,
        [((mp, shard_rows, features), bf16)],
        (core_id,),
        (frames,),
        read=(0,),
    )
    copies, own = lax.optimization_barrier((copies, own))
    other = swap(own)
    out_part = jnp.where(first, own[3, :HS], other[3, HS:])
    both_orders = [list(range(mp)), list(range(2 * mp - 1, mp - 1, -1))]
    out_part = lax.all_gather(
        out_part, ("segment", "mp"), axis=0, tiled=True, axis_index_groups=both_orders
    )
    enc_full = exchange(copies).reshape(rows, features)

    token_queries, token_grads = call(
        token_kernel,
        [((count, head_cols), bf16)] * 2,
        (core_id,),
        (dec_states, out_grad, own, other, norm_gains, norm_biases),
        kept=(0, 1),
        read=(0, 1, 2, 3),
    )
    weight_block = ((3, head_cols, features), (0, 0, 0))
    normed, queries, values, context, context_copies, probs = call(
        enc_forward_kernel,
        [
            ((rows, features), bf16),
            ((rows, head_cols), bf16),
            ((rows, head_cols), bf16),
            ((rows, head_cols), bf16),
            ((mp, rows, head_cols), bf16),
            ((heads, rows, rows), f32),
        ],
        (core_id, frame_lengths),
        (enc_full, own, other, norm_gains, norm_biases),
        {1: weight_block, 2: weight_block},
        kept=(0, 1, 2, 3, 4, 5),
        cost=pl.CostEstimate(flops=3_000_000_000, transcendentals=0, bytes_accessed=0),
    )
    context_full, out_part, token_queries, token_grads = lax.optimization_barrier(
        (exchange(context_copies), out_part, token_queries, token_grads)
    )
    out_rest = swap(out_part)
    half_states = call(
        half_states_kernel,
        [((rows, features), f32)],
        (core_id,),
        (enc_full, context_full, out_part),
        read=(2,),
    )
    partial, states, state_normed, dec_key_grad, dec_value_grad, dec_context = call(
        dec_kernel,
        [
            ((rows, features), bf16),
            ((shard_rows, features), bf16),
            ((rows, features), bf16),
            ((rows, head_cols), bf16),
            ((rows, head_cols), bf16),
            ((count, head_cols), bf16),
        ],
        (core_id, place, frame_lengths, token_lengths),
        (
            half_states, context_full, out_rest, own, other, token_queries, token_grads,
            norm_gains, norm_biases,
        ),
        scratch=[pltpu.VMEM((rows, features), f32)],
        kept=(1, 2, 3, 4, 5),
        read=(3, 4, 5, 6),
    )
    pieces = exchange(partial.reshape(mp, shard_rows, features))
    whole = [((3 * head_cols, features), bf16)]
    dec_term = call(
        dec_terms_kernel,
        whole,
        (core_id,),
        (dec_key_grad, dec_value_grad, dec_context, state_normed, out_grad),
        kept=(0,),
        read=(0, 1, 2, 3, 4),
    )
    grads = call(
        norm_backward_kernel,
        [((mp, shard_rows, features), bf16)],
        (),
        (pieces, states, norm_gains),
        read=(1,),
    )
    grads_full = exchange(grads).reshape(rows, features)
    last_block = ((1, head_cols, features), (3, 0, 0))
    enc_term = call(
        enc_backward_kernel,
        whole,
        (core_id,),
        (grads_full, own, other, queries, values, probs, context, normed),
        {1: last_block, 2: last_block},
        read=(1, 2, 3, 4, 5, 6, 7),
    )
    dec_sent = lax.ppermute(dec_term, "segment", [(0, 1)])
    enc_sent = lax.ppermute(enc_term, "segment", [(1, 0)])
    size = 3 * head_cols * features // 1024
    each = size // near
    tiles = call(
        chunks_kernel,
        [((size, 8, 128), bf16)],
        (core_id,),
        (enc_term, enc_sent, dec_term, dec_sent),
        read=(2,),
    )
    parts = exchange(tiles.reshape(near, each, 8, 128), "dp", near_groups)
    parts = call(sum_copies_kernel, [((far, each, 8, 128), bf16)], (), (parts,))
    parts = exchange(parts, "dp", far_groups)
    parts = call(sum_copies_kernel, [((near, each, 8, 128), bf16)], (), (parts,))
    parts = exchange(parts, "dp", near_groups).reshape(size, 8, 128)
    gradient = call(from_chunks_kernel, [((3 * head_cols, features), f32)], (), (parts,))
    return gradient.reshape(1, 3, head_cols, features)


def solution(mesh):
    placed = (
        P(None, ("dp", "mp"), None),
        P(None, "dp", None),
        P(None, "dp", None),
        P(None, "dp", None),
        P(None, "dp", None),
        P("segment", None, "mp", None),
        P(),
        P(),
    )
    return jax.shard_map(
        shards,
        mesh=mesh,
        in_specs=placed,
        out_specs=P("segment", None, "mp", None),
        check_vma=False,
    )
```

```python
import functools
import math

import jax
import jax.numpy as jnp
from jax import lax
from jax.experimental import pallas as pl
from jax.experimental.pallas import tpu as pltpu
from jax.sharding import PartitionSpec as P

HS = 64
SCALING = 1.0 / math.sqrt(HS)
EPSILON = 1e-05
ROWS_DIMS = (((0,), (0,)), ((), ()))
FEAT_DIMS = (((1,), (1,)), ((), ()))


def dot_nn(a, b):
    return lax.dot_general(a, b, (((1,), (0,)), ((), ())), preferred_element_type=jnp.float32)


def dot_nt(a, b):
    return lax.dot_general(a, b, FEAT_DIMS, preferred_element_type=jnp.float32)


def dot_tn(a, b):
    return lax.dot_general(a, b, ROWS_DIMS, preferred_element_type=jnp.float32)


def row_stats(values):
    center = values - jnp.mean(values, axis=-1, keepdims=True)
    variance = jnp.mean(center * center, axis=-1, keepdims=True)
    return center, lax.rsqrt(variance + EPSILON)


def layer_norm(values, norm_gain, offset):
    center, inverse = row_stats(values.astype(jnp.float32))
    return (center * inverse * norm_gain + offset).astype(jnp.bfloat16)


def ids_along(lengths_ref, row, shape, axis):
    places = lax.broadcasted_iota(jnp.int32, shape, axis)
    bound = 0
    ids = jnp.zeros(shape, jnp.int32)
    for piece in range(lengths_ref.shape[2]):
        bound = bound + lengths_ref[row, 0, piece]
        ids = ids + (places >= bound).astype(jnp.int32)
    return ids


def softmax(queries, keys, allowed):
    scores = jnp.where(allowed, dot_nt(queries, keys) * SCALING, -1e30)
    raised = jnp.exp(scores - jnp.max(scores, axis=-1, keepdims=True))
    return raised / jnp.sum(raised, axis=-1, keepdims=True)


def scores_grad(probs, grad_context, values):
    grad_probs = dot_nt(grad_context, values)
    inner = jnp.sum(grad_probs * probs, axis=-1, keepdims=True)
    return (probs * (grad_probs - inner)).astype(jnp.bfloat16)


def side_by_side(parts):
    return jnp.concatenate(parts, axis=1).astype(jnp.bfloat16)


def enc_forward_kernel(
    core, lengths, x, own, other, gains, biases, normed, queries, values, context, copies, probs
):
    first = core[0] == 0
    rows = x.shape[0]
    normed_rows = layer_norm(x[...], gains[0:1, :], biases[0:1, :])
    normed[...] = normed_rows
    projected = []
    for kind in range(3):
        matrix = jnp.where(first, own[kind], other[kind])
        projected.append(dot_nt(normed_rows, matrix).astype(jnp.bfloat16))
    queries[...] = projected[0]
    values[...] = projected[2]
    allowed = ids_along(lengths, core[0], (rows, 1), 0) == ids_along(lengths, core[0], (1, rows), 1)
    parts = []
    for head in range(queries.shape[1] // HS):
        at = slice(head * HS, (head + 1) * HS)
        weights = softmax(projected[0][:, at], projected[1][:, at], allowed)
        probs[head] = weights
        parts.append(dot_nn(weights.astype(jnp.bfloat16), projected[2][:, at]))
    block = side_by_side(parts)
    context[...] = block
    for copy in range(copies.shape[0]):
        copies[copy] = block


def token_kernel(core, tokens, upstream, own, other, gains, biases, queries, grad_context):
    first = core[0] == 0
    own_tokens = jnp.where(first, tokens[0], tokens[1])
    normed_tokens = layer_norm(own_tokens, gains[1:2, :], biases[1:2, :])
    matrix = jnp.where(first, other[0], own[0])
    queries[...] = dot_nt(normed_tokens, matrix).astype(jnp.bfloat16)
    matrix = jnp.where(first, other[3], own[3])
    own_upstream = jnp.where(first, upstream[0], upstream[1])
    grad_context[...] = dot_nt(own_upstream, matrix).astype(jnp.bfloat16)


def dec_kernel(
    core, place, frame_lens, token_lens, x, context, own, other, token_queries, token_grads,
    gains, biases, *refs,
):
    devices = context.shape[0]
    out_shards, refs = refs[:devices], refs[devices:]
    partial, states, normed, key_grad, value_grad, dec_context, scratch = refs
    first = core[0] == 0
    rows = x.shape[0]
    summed = x[...].astype(jnp.float32)
    for index in range(0, devices, 2):
        pair = range(index, index + 2)
        left = [context[(place[0] + devices - back) % devices] for back in pair]
        right = [out_shards[back][...] for back in pair]
        summed = summed + dot_nn(jnp.concatenate(left, axis=1), jnp.concatenate(right, axis=0))
    scratch[...] = summed
    all_states = scratch[...].astype(jnp.bfloat16)
    shard = states.shape[0]
    start = pl.multiple_of(place[0] * shard, shard)
    states[...] = scratch[pl.ds(start, shard), :].astype(jnp.bfloat16)
    normed_rows = layer_norm(all_states, gains[2:3, :], biases[2:3, :])
    normed[...] = normed_rows
    matrix = [jnp.where(first, other[kind], own[kind]) for kind in (1, 2)]
    queries = token_queries[...]
    grad_context = token_grads[...]
    keys = dot_nt(normed_rows, matrix[0]).astype(jnp.bfloat16)
    values = dot_nt(normed_rows, matrix[1]).astype(jnp.bfloat16)
    count = queries.shape[0]
    token_ids = ids_along(token_lens, core[0], (count, 1), 0)
    allowed = token_ids == ids_along(frame_lens, core[0], (1, rows), 1)
    key_parts, value_parts, context_parts = [], [], []
    for head in range(queries.shape[1] // HS):
        at = slice(head * HS, (head + 1) * HS)
        weights = softmax(queries[:, at], keys[:, at], allowed)
        rounded = weights.astype(jnp.bfloat16)
        context_parts.append(dot_nn(rounded, values[:, at]))
        grad_scores = scores_grad(weights, grad_context[:, at], values[:, at])
        key_parts.append(dot_tn(grad_scores, queries[:, at]) * SCALING)
        value_parts.append(dot_tn(rounded, grad_context[:, at]))
    key_block, value_block = side_by_side(key_parts), side_by_side(value_parts)
    key_grad[...] = key_block
    value_grad[...] = value_block
    dec_context[...] = side_by_side(context_parts)
    partial[...] = (dot_nn(key_block, matrix[0]) + dot_nn(value_block, matrix[1])).astype(
        jnp.bfloat16
    )


def store_terms(products, term):
    high = products[0].shape[0]
    for index, product in enumerate(products):
        term[index * high : (index + 1) * high, :] = product.astype(jnp.bfloat16)


def dec_terms_kernel(core, key_grad, value_grad, context, normed, upstream, term):
    products = [
        dot_tn(key_grad[...], normed[...]),
        dot_tn(value_grad[...], normed[...]),
        dot_tn(context[...], jnp.where(core[0] == 0, upstream[0], upstream[1])),
    ]
    store_terms(products, term)


def norm_backward_kernel(pieces, states, gains, grads):
    summed = pieces[0].astype(jnp.float32)
    for index in range(1, pieces.shape[0]):
        summed = summed + pieces[index].astype(jnp.float32)
    center, inverse = row_stats(states[...].astype(jnp.float32))
    normed = center * inverse
    scaled = summed * gains[2:3, :]
    result = inverse * (
        scaled
        - jnp.mean(scaled, axis=-1, keepdims=True)
        - normed * jnp.mean(scaled * normed, axis=-1, keepdims=True)
    )
    block = result.astype(jnp.bfloat16)
    for copy in range(grads.shape[0]):
        grads[copy] = block


def enc_backward_kernel(
    core, grads, own, other, queries, values, probs, context, normed, term
):
    first = core[0] == 0
    grad_rows = grads[...]
    att_grad = dot_nt(grad_rows, jnp.where(first, own[0], other[0])).astype(jnp.bfloat16)
    query_rows, value_rows = queries[...], values[...]
    key_parts, value_parts = [], []
    for head in range(query_rows.shape[1] // HS):
        at = slice(head * HS, (head + 1) * HS)
        weights = probs[head]
        grad_scores = scores_grad(weights, att_grad[:, at], value_rows[:, at])
        key_parts.append(dot_tn(grad_scores, query_rows[:, at]) * SCALING)
        value_parts.append(dot_tn(weights.astype(jnp.bfloat16), att_grad[:, at]))
    products = [
        dot_tn(side_by_side(key_parts), normed[...]),
        dot_tn(side_by_side(value_parts), normed[...]),
        dot_tn(context[...], grad_rows),
    ]
    store_terms(products, term)


def chunks_kernel(core, enc_term, enc_sent, dec_term, dec_sent, tiles):
    first = core[0] == 0
    rows, cols = enc_term.shape
    high = rows // 8
    for block in range(cols // 128):
        at = slice(block * 128, (block + 1) * 128)
        kept = jnp.where(first, enc_term[:, at], dec_term[:, at])
        received = jnp.where(first, enc_sent[:, at], dec_sent[:, at])
        total = kept.astype(jnp.float32) + received.astype(jnp.float32)
        part = total.reshape(high, 8, 128)
        tiles[block * high : (block + 1) * high] = part.astype(jnp.bfloat16)


def sum_copies_kernel(pieces, copies):
    summed = pieces[0].astype(jnp.float32)
    for index in range(1, pieces.shape[0]):
        summed = summed + pieces[index].astype(jnp.float32)
    block = summed.astype(jnp.bfloat16)
    for copy in range(copies.shape[0]):
        copies[copy] = block


def pick_copies_kernel(core, blocks, copies):
    block = jnp.where(core[0] == 0, blocks[0], blocks[1])
    for copy in range(copies.shape[0]):
        copies[copy] = block


def from_chunks_kernel(tiles, gradient):
    rows, cols = gradient.shape
    high = rows // 8
    for block in range(cols // 128):
        part = tiles[block * high : (block + 1) * high].astype(jnp.float32)
        gradient[:, block * 128 : (block + 1) * 128] = part.reshape(rows, 128)


def call(
    kernel, outs, scalars, arrays, blocks=None, scratch=(), kept=(), read=(), cost=None
):
    blocks = blocks or {}

    def spec(index, array):
        shape, at = blocks.get(index, (array.shape, (0,) * array.ndim))
        return pl.BlockSpec(shape, lambda i: at)

    def out(index, shape, dtype):
        return pltpu.HBM(shape, dtype) if index in kept else jax.ShapeDtypeStruct(shape, dtype)

    arrays = [
        pltpu.with_memory_space_constraint(array, pltpu.HBM) if index in read else array
        for index, array in enumerate(arrays)
    ]
    result = pl.pallas_call(
        kernel,
        grid=(1,),
        out_shape=[out(index, *what) for index, what in enumerate(outs)],
        in_specs=[pl.BlockSpec(memory_space=pltpu.SMEM) for _ in scalars]
        + [spec(index, array) for index, array in enumerate(arrays)],
        out_specs=[
            pl.BlockSpec(shape, functools.partial(lambda n, i: (0,) * n, len(shape)))
            for shape, _ in outs
        ],
        scratch_shapes=list(scratch),
        cost_estimate=cost,
        compiler_params=pltpu.CompilerParams(vmem_limit_bytes=48 << 20),
    )(*scalars, *arrays)
    return result[0] if len(outs) == 1 else result


def swap(block):
    return lax.ppermute(block, "segment", [(0, 1), (1, 0)])


def shards(
    frames, dec_states, out_grad, frame_lengths, token_lengths, weights, norm_gains, norm_biases
):
    bf16, f32 = jnp.bfloat16, jnp.float32
    core = lax.axis_index("segment")
    first = core == 0
    own = weights[0]
    shard_rows, features = frames.shape[1:]
    mp = lax.axis_size("mp")
    dp = lax.axis_size("dp")
    head_cols = own.shape[1]
    heads = head_cols // HS
    rows = shard_rows * mp
    count = dec_states.shape[1]
    near_groups = [[x * 8 + y * 2 + b for x in range(4) for b in range(2)] for y in range(4)]
    far_groups = [[x * 8 + y * 2 + b for y in range(4)] for x in range(4) for b in range(2)]
    near, far = len(near_groups[0]), len(far_groups[0])

    def exchange(blocks, axis="mp", groups=None):
        return lax.all_to_all(blocks, axis, 0, 0, axis_index_groups=groups)

    core_id = core.astype(jnp.int32).reshape(1)
    place = lax.axis_index("mp").astype(jnp.int32).reshape(1)

    copies = call(
        pick_copies_kernel,
        [((mp, shard_rows, features), bf16)],
        (core_id,),
        (frames,),
        kept=(0,),
        read=(0,),
    )
    copies, own = lax.optimization_barrier((copies, own))
    other = swap(own)
    shard = jnp.where(first, own[3], other[3])
    forward, backward = [shard], [shard]
    for _ in range(mp // 2):
        forward.append(lax.ppermute(forward[-1], "mp", [(i, (i + 1) % mp) for i in range(mp)]))
    for _ in range(mp - mp // 2 - 1):
        backward.append(lax.ppermute(backward[-1], "mp", [(i, (i - 1) % mp) for i in range(mp)]))
    out_shards = forward + backward[:0:-1]
    enc_full = exchange(copies).reshape(rows, features)

    token_queries, token_grads = call(
        token_kernel,
        [((count, head_cols), bf16)] * 2,
        (core_id,),
        (dec_states, out_grad, own, other, norm_gains, norm_biases),
        kept=(0, 1),
        read=(0, 1, 2, 3),
    )
    weight_block = ((3, head_cols, features), (0, 0, 0))
    normed, queries, values, context, context_copies, probs = call(
        enc_forward_kernel,
        [
            ((rows, features), bf16),
            ((rows, head_cols), bf16),
            ((rows, head_cols), bf16),
            ((rows, head_cols), bf16),
            ((mp, rows, head_cols), bf16),
            ((heads, rows, rows), f32),
        ],
        (core_id, frame_lengths),
        (enc_full, own, other, norm_gains, norm_biases),
        {1: weight_block, 2: weight_block},
        kept=(0, 1, 2, 3, 4, 5),
        cost=pl.CostEstimate(flops=3_000_000_000, transcendentals=0, bytes_accessed=0),
    )
    context_full, token_queries, token_grads, out_shards = lax.optimization_barrier(
        (exchange(context_copies), token_queries, token_grads, out_shards)
    )
    partial, states, state_normed, dec_key_grad, dec_value_grad, dec_context = call(
        dec_kernel,
        [
            ((rows, features), bf16),
            ((shard_rows, features), bf16),
            ((rows, features), bf16),
            ((rows, head_cols), bf16),
            ((rows, head_cols), bf16),
            ((count, head_cols), bf16),
        ],
        (core_id, place, frame_lengths, token_lengths),
        (
            enc_full, context_full, own, other, token_queries, token_grads,
            norm_gains, norm_biases, *out_shards,
        ),
        scratch=[pltpu.VMEM((rows, features), f32)],
        kept=(1, 2, 3, 4, 5),
        read=(2, 3, 4, 5),
    )
    pieces = exchange(partial.reshape(mp, shard_rows, features))
    whole = [((3 * head_cols, features), bf16)]
    dec_term = call(
        dec_terms_kernel,
        whole,
        (core_id,),
        (dec_key_grad, dec_value_grad, dec_context, state_normed, out_grad),
        kept=(0,),
        read=(0, 1, 2, 3, 4),
    )
    grads = call(
        norm_backward_kernel,
        [((mp, shard_rows, features), bf16)],
        (),
        (pieces, states, norm_gains),
        read=(1,),
    )
    grads_full = exchange(grads).reshape(rows, features)
    last_block = ((1, head_cols, features), (3, 0, 0))
    enc_term = call(
        enc_backward_kernel,
        whole,
        (core_id,),
        (grads_full, own, other, queries, values, probs, context, normed),
        {1: last_block, 2: last_block},
        read=(1, 2, 3, 4, 5, 6, 7),
    )
    dec_sent = lax.ppermute(dec_term, "segment", [(0, 1)])
    enc_sent = lax.ppermute(enc_term, "segment", [(1, 0)])
    size = 3 * head_cols * features // 1024
    each = size // near
    tiles = call(
        chunks_kernel,
        [((size, 8, 128), bf16)],
        (core_id,),
        (enc_term, enc_sent, dec_term, dec_sent),
        read=(2,),
    )
    parts = exchange(tiles.reshape(near, each, 8, 128), "dp", near_groups)
    parts = call(sum_copies_kernel, [((far, each, 8, 128), bf16)], (), (parts,))
    parts = exchange(parts, "dp", far_groups)
    parts = call(sum_copies_kernel, [((near, each, 8, 128), bf16)], (), (parts,))
    parts = exchange(parts, "dp", near_groups).reshape(size, 8, 128)
    gradient = call(from_chunks_kernel, [((3 * head_cols, features), f32)], (), (parts,))
    return gradient.reshape(1, 3, head_cols, features)


def solution(mesh):
    placed = (
        P(None, ("dp", "mp"), None),
        P(None, "dp", None),
        P(None, "dp", None),
        P(None, "dp", None),
        P(None, "dp", None),
        P("segment", None, "mp", None),
        P(),
        P(),
    )
    return jax.shard_map(
        shards,
        mesh=mesh,
        in_specs=placed,
        out_specs=P("segment", None, "mp", None),
        check_vma=False,
    )
```

```python
import functools
import math

import jax
import jax.numpy as jnp
from jax import lax
from jax.experimental import pallas as pl
from jax.experimental.pallas import tpu as pltpu
from jax.sharding import PartitionSpec as P

HS = 64
SCALING = 1.0 / math.sqrt(HS)
EPSILON = 1e-05
ROWS_DIMS = (((0,), (0,)), ((), ()))
FEAT_DIMS = (((1,), (1,)), ((), ()))


def dot_nn(a, b):
    return lax.dot_general(a, b, (((1,), (0,)), ((), ())), preferred_element_type=jnp.float32)


def dot_nt(a, b):
    return lax.dot_general(a, b, FEAT_DIMS, preferred_element_type=jnp.float32)


def dot_tn(a, b):
    return lax.dot_general(a, b, ROWS_DIMS, preferred_element_type=jnp.float32)


def row_stats(values):
    center = values - jnp.mean(values, axis=-1, keepdims=True)
    variance = jnp.mean(center * center, axis=-1, keepdims=True)
    return center, lax.rsqrt(variance + EPSILON)


def layer_norm(values, norm_gain, offset):
    center, inverse = row_stats(values.astype(jnp.float32))
    return (center * inverse * norm_gain + offset).astype(jnp.bfloat16)


def ids_along(lengths_ref, row, shape, axis):
    places = lax.broadcasted_iota(jnp.int32, shape, axis)
    bound = 0
    ids = jnp.zeros(shape, jnp.int32)
    for piece in range(lengths_ref.shape[2]):
        bound = bound + lengths_ref[row, 0, piece]
        ids = ids + (places >= bound).astype(jnp.int32)
    return ids


def softmax(queries, keys, allowed):
    scores = jnp.where(allowed, dot_nt(queries, keys) * SCALING, -1e30)
    raised = jnp.exp(scores - jnp.max(scores, axis=-1, keepdims=True))
    return raised / jnp.sum(raised, axis=-1, keepdims=True)


def scores_grad(probs, grad_context, values):
    grad_probs = dot_nt(grad_context, values)
    inner = jnp.sum(grad_probs * probs, axis=-1, keepdims=True)
    return (probs * (grad_probs - inner)).astype(jnp.bfloat16)


def side_by_side(parts):
    return jnp.concatenate(parts, axis=1).astype(jnp.bfloat16)


def enc_forward_kernel(
    core, lengths, x, own, other, gains, biases, normed, queries, values, context, copies, probs
):
    first = core[0] == 0
    rows = x.shape[0]
    normed_rows = layer_norm(x[...], gains[0:1, :], biases[0:1, :])
    normed[...] = normed_rows
    projected = []
    for kind in range(3):
        matrix = jnp.where(first, own[kind], other[kind])
        projected.append(dot_nt(normed_rows, matrix).astype(jnp.bfloat16))
    queries[...] = projected[0]
    values[...] = projected[2]
    allowed = ids_along(lengths, core[0], (rows, 1), 0) == ids_along(lengths, core[0], (1, rows), 1)
    parts = []
    for head in range(queries.shape[1] // HS):
        at = slice(head * HS, (head + 1) * HS)
        weights = softmax(projected[0][:, at], projected[1][:, at], allowed)
        probs[head] = weights
        parts.append(dot_nn(weights.astype(jnp.bfloat16), projected[2][:, at]))
    block = side_by_side(parts)
    context[...] = block
    for copy in range(copies.shape[0]):
        copies[copy] = block


def token_kernel(core, tokens, upstream, own, other, gains, biases, queries, grad_context):
    first = core[0] == 0
    own_tokens = jnp.where(first, tokens[0], tokens[1])
    normed_tokens = layer_norm(own_tokens, gains[1:2, :], biases[1:2, :])
    matrix = jnp.where(first, other[0], own[0])
    queries[...] = dot_nt(normed_tokens, matrix).astype(jnp.bfloat16)
    matrix = jnp.where(first, other[3], own[3])
    own_upstream = jnp.where(first, upstream[0], upstream[1])
    grad_context[...] = dot_nt(own_upstream, matrix).astype(jnp.bfloat16)


def dec_kernel(
    core, place, frame_lens, token_lens, x, context, own, other, token_queries, token_grads,
    gains, biases, *refs,
):
    devices = context.shape[0]
    out_shards, refs = refs[:devices], refs[devices:]
    partial, states, normed, key_grad, value_grad, dec_context, scratch = refs
    first = core[0] == 0
    rows = x.shape[0]
    steps = devices // 2
    passed, swapped = out_shards[: steps + 1], out_shards[steps + 1 :]

    def context_at(back):
        return context[(place[0] + jnp.where(first, devices - back, back)) % devices]

    pairs = [(0, passed[0], steps, passed[steps])]
    for back in range(1, steps):
        pairs.append((back, passed[back], devices - back, swapped[back - 1]))
    summed = x[...].astype(jnp.float32)
    for back, shard, far_back, far_shard in pairs:
        left = jnp.concatenate([context_at(back), context_at(far_back)], axis=1)
        right = jnp.concatenate([shard[...], far_shard[...]], axis=0)
        summed = summed + dot_nn(left, right)
    scratch[...] = summed
    all_states = scratch[...].astype(jnp.bfloat16)
    shard = states.shape[0]
    start = pl.multiple_of(place[0] * shard, shard)
    states[...] = scratch[pl.ds(start, shard), :].astype(jnp.bfloat16)
    normed_rows = layer_norm(all_states, gains[2:3, :], biases[2:3, :])
    normed[...] = normed_rows
    matrix = [jnp.where(first, other[kind], own[kind]) for kind in (1, 2)]
    queries = token_queries[...]
    grad_context = token_grads[...]
    keys = dot_nt(normed_rows, matrix[0]).astype(jnp.bfloat16)
    values = dot_nt(normed_rows, matrix[1]).astype(jnp.bfloat16)
    count = queries.shape[0]
    token_ids = ids_along(token_lens, core[0], (count, 1), 0)
    allowed = token_ids == ids_along(frame_lens, core[0], (1, rows), 1)
    key_parts, value_parts, context_parts = [], [], []
    for head in range(queries.shape[1] // HS):
        at = slice(head * HS, (head + 1) * HS)
        weights = softmax(queries[:, at], keys[:, at], allowed)
        rounded = weights.astype(jnp.bfloat16)
        context_parts.append(dot_nn(rounded, values[:, at]))
        grad_scores = scores_grad(weights, grad_context[:, at], values[:, at])
        key_parts.append(dot_tn(grad_scores, queries[:, at]) * SCALING)
        value_parts.append(dot_tn(rounded, grad_context[:, at]))
    key_block, value_block = side_by_side(key_parts), side_by_side(value_parts)
    key_grad[...] = key_block
    value_grad[...] = value_block
    dec_context[...] = side_by_side(context_parts)
    partial[...] = (dot_nn(key_block, matrix[0]) + dot_nn(value_block, matrix[1])).astype(
        jnp.bfloat16
    )


def store_terms(products, term):
    high = products[0].shape[0]
    for index, product in enumerate(products):
        term[index * high : (index + 1) * high, :] = product.astype(jnp.bfloat16)


def dec_terms_kernel(core, key_grad, value_grad, context, normed, upstream, term):
    products = [
        dot_tn(key_grad[...], normed[...]),
        dot_tn(value_grad[...], normed[...]),
        dot_tn(context[...], jnp.where(core[0] == 0, upstream[0], upstream[1])),
    ]
    store_terms(products, term)


def norm_backward_kernel(pieces, states, gains, grads):
    summed = pieces[0].astype(jnp.float32)
    for index in range(1, pieces.shape[0]):
        summed = summed + pieces[index].astype(jnp.float32)
    center, inverse = row_stats(states[...].astype(jnp.float32))
    normed = center * inverse
    scaled = summed * gains[2:3, :]
    result = inverse * (
        scaled
        - jnp.mean(scaled, axis=-1, keepdims=True)
        - normed * jnp.mean(scaled * normed, axis=-1, keepdims=True)
    )
    block = result.astype(jnp.bfloat16)
    for copy in range(grads.shape[0]):
        grads[copy] = block


def enc_backward_kernel(
    core, grads, own, other, queries, values, probs, context, normed, term
):
    first = core[0] == 0
    grad_rows = grads[...]
    att_grad = dot_nt(grad_rows, jnp.where(first, own[0], other[0])).astype(jnp.bfloat16)
    query_rows, value_rows = queries[...], values[...]
    key_parts, value_parts = [], []
    for head in range(query_rows.shape[1] // HS):
        at = slice(head * HS, (head + 1) * HS)
        weights = probs[head]
        grad_scores = scores_grad(weights, att_grad[:, at], value_rows[:, at])
        key_parts.append(dot_tn(grad_scores, query_rows[:, at]) * SCALING)
        value_parts.append(dot_tn(weights.astype(jnp.bfloat16), att_grad[:, at]))
    products = [
        dot_tn(side_by_side(key_parts), normed[...]),
        dot_tn(side_by_side(value_parts), normed[...]),
        dot_tn(context[...], grad_rows),
    ]
    store_terms(products, term)


def chunks_kernel(core, enc_term, enc_sent, dec_term, dec_sent, tiles):
    first = core[0] == 0
    rows, cols = enc_term.shape
    high = rows // 8
    for block in range(cols // 128):
        at = slice(block * 128, (block + 1) * 128)
        kept = jnp.where(first, enc_term[:, at], dec_term[:, at])
        received = jnp.where(first, enc_sent[:, at], dec_sent[:, at])
        total = kept.astype(jnp.float32) + received.astype(jnp.float32)
        part = total.reshape(high, 8, 128)
        tiles[block * high : (block + 1) * high] = part.astype(jnp.bfloat16)


def sum_copies_kernel(pieces, copies):
    summed = pieces[0].astype(jnp.float32)
    for index in range(1, pieces.shape[0]):
        summed = summed + pieces[index].astype(jnp.float32)
    block = summed.astype(jnp.bfloat16)
    for copy in range(copies.shape[0]):
        copies[copy] = block


def pick_copies_kernel(core, blocks, copies):
    block = jnp.where(core[0] == 0, blocks[0], blocks[1])
    for copy in range(copies.shape[0]):
        copies[copy] = block


def from_chunks_kernel(tiles, gradient):
    rows, cols = gradient.shape
    high = rows // 8
    for block in range(cols // 128):
        part = tiles[block * high : (block + 1) * high].astype(jnp.float32)
        gradient[:, block * 128 : (block + 1) * 128] = part.reshape(rows, 128)


def call(
    kernel, outs, scalars, arrays, blocks=None, scratch=(), kept=(), read=(), cost=None
):
    blocks = blocks or {}

    def spec(index, array):
        shape, at = blocks.get(index, (array.shape, (0,) * array.ndim))
        return pl.BlockSpec(shape, lambda i: at)

    def out(index, shape, dtype):
        return pltpu.HBM(shape, dtype) if index in kept else jax.ShapeDtypeStruct(shape, dtype)

    arrays = [
        pltpu.with_memory_space_constraint(array, pltpu.HBM) if index in read else array
        for index, array in enumerate(arrays)
    ]
    result = pl.pallas_call(
        kernel,
        grid=(1,),
        out_shape=[out(index, *what) for index, what in enumerate(outs)],
        in_specs=[pl.BlockSpec(memory_space=pltpu.SMEM) for _ in scalars]
        + [spec(index, array) for index, array in enumerate(arrays)],
        out_specs=[
            pl.BlockSpec(shape, functools.partial(lambda n, i: (0,) * n, len(shape)))
            for shape, _ in outs
        ],
        scratch_shapes=list(scratch),
        cost_estimate=cost,
        compiler_params=pltpu.CompilerParams(vmem_limit_bytes=48 << 20),
    )(*scalars, *arrays)
    return result[0] if len(outs) == 1 else result


def swap(block):
    return lax.ppermute(block, "segment", [(0, 1), (1, 0)])


def shards(
    frames, dec_states, out_grad, frame_lengths, token_lengths, weights, norm_gains, norm_biases
):
    bf16, f32 = jnp.bfloat16, jnp.float32
    core = lax.axis_index("segment")
    first = core == 0
    own = weights[0]
    shard_rows, features = frames.shape[1:]
    mp = lax.axis_size("mp")
    dp = lax.axis_size("dp")
    head_cols = own.shape[1]
    heads = head_cols // HS
    rows = shard_rows * mp
    count = dec_states.shape[1]
    near_groups = [[x * 8 + y * 2 + b for x in range(4) for b in range(2)] for y in range(4)]
    far_groups = [[x * 8 + y * 2 + b for y in range(4)] for x in range(4) for b in range(2)]
    near, far = len(near_groups[0]), len(far_groups[0])

    def exchange(blocks, axis="mp", groups=None):
        return lax.all_to_all(blocks, axis, 0, 0, axis_index_groups=groups)

    core_id = core.astype(jnp.int32).reshape(1)
    place = lax.axis_index("mp").astype(jnp.int32).reshape(1)

    copies = call(
        pick_copies_kernel,
        [((mp, shard_rows, features), bf16)],
        (core_id,),
        (frames,),
        kept=(0,),
        read=(0,),
    )
    copies, own = lax.optimization_barrier((copies, own))
    other = swap(own)
    shard = jnp.where(first, own[3], other[3])
    step = [(i, (i + 1) % mp) for i in range(mp)] + [(mp + i, mp + (i - 1) % mp) for i in range(mp)]
    passed, swapped = [shard], []
    for index in range(mp // 2):
        passed.append(lax.ppermute(passed[-1], ("segment", "mp"), step))
        if index < mp // 2 - 1:
            swapped.append(swap(passed[-1]))
    out_shards = passed + swapped
    enc_full = exchange(copies).reshape(rows, features)

    token_queries, token_grads = call(
        token_kernel,
        [((count, head_cols), bf16)] * 2,
        (core_id,),
        (dec_states, out_grad, own, other, norm_gains, norm_biases),
        kept=(0, 1),
        read=(0, 1, 2, 3),
    )
    weight_block = ((3, head_cols, features), (0, 0, 0))
    normed, queries, values, context, context_copies, probs = call(
        enc_forward_kernel,
        [
            ((rows, features), bf16),
            ((rows, head_cols), bf16),
            ((rows, head_cols), bf16),
            ((rows, head_cols), bf16),
            ((mp, rows, head_cols), bf16),
            ((heads, rows, rows), f32),
        ],
        (core_id, frame_lengths),
        (enc_full, own, other, norm_gains, norm_biases),
        {1: weight_block, 2: weight_block},
        kept=(0, 1, 2, 3, 4, 5),
        cost=pl.CostEstimate(flops=3_000_000_000, transcendentals=0, bytes_accessed=0),
    )
    context_full, token_queries, token_grads, out_shards = lax.optimization_barrier(
        (exchange(context_copies), token_queries, token_grads, out_shards)
    )
    partial, states, state_normed, dec_key_grad, dec_value_grad, dec_context = call(
        dec_kernel,
        [
            ((rows, features), bf16),
            ((shard_rows, features), bf16),
            ((rows, features), bf16),
            ((rows, head_cols), bf16),
            ((rows, head_cols), bf16),
            ((count, head_cols), bf16),
        ],
        (core_id, place, frame_lengths, token_lengths),
        (
            enc_full, context_full, own, other, token_queries, token_grads,
            norm_gains, norm_biases, *out_shards,
        ),
        scratch=[pltpu.VMEM((rows, features), f32)],
        kept=(1, 2, 3, 4, 5),
        read=(2, 3, 4, 5),
    )
    pieces = exchange(partial.reshape(mp, shard_rows, features))
    whole = [((3 * head_cols, features), bf16)]
    dec_term = call(
        dec_terms_kernel,
        whole,
        (core_id,),
        (dec_key_grad, dec_value_grad, dec_context, state_normed, out_grad),
        kept=(0,),
        read=(0, 1, 2, 3, 4),
    )
    grads = call(
        norm_backward_kernel,
        [((mp, shard_rows, features), bf16)],
        (),
        (pieces, states, norm_gains),
        read=(1,),
    )
    grads_full = exchange(grads).reshape(rows, features)
    last_block = ((1, head_cols, features), (3, 0, 0))
    enc_term = call(
        enc_backward_kernel,
        whole,
        (core_id,),
        (grads_full, own, other, queries, values, probs, context, normed),
        {1: last_block, 2: last_block},
        read=(1, 2, 3, 4, 5, 6, 7),
    )
    dec_sent = lax.ppermute(dec_term, "segment", [(0, 1)])
    enc_sent = lax.ppermute(enc_term, "segment", [(1, 0)])
    size = 3 * head_cols * features // 1024
    each = size // near
    tiles = call(
        chunks_kernel,
        [((size, 8, 128), bf16)],
        (core_id,),
        (enc_term, enc_sent, dec_term, dec_sent),
        read=(2,),
    )
    parts = exchange(tiles.reshape(near, each, 8, 128), "dp", near_groups)
    parts = call(sum_copies_kernel, [((far, each, 8, 128), bf16)], (), (parts,))
    parts = exchange(parts, "dp", far_groups)
    parts = call(sum_copies_kernel, [((near, each, 8, 128), bf16)], (), (parts,))
    parts = exchange(parts, "dp", near_groups).reshape(size, 8, 128)
    gradient = call(from_chunks_kernel, [((3 * head_cols, features), f32)], (), (parts,))
    return gradient.reshape(1, 3, head_cols, features)


def solution(mesh):
    placed = (
        P(None, ("dp", "mp"), None),
        P(None, "dp", None),
        P(None, "dp", None),
        P(None, "dp", None),
        P(None, "dp", None),
        P("segment", None, "mp", None),
        P(),
        P(),
    )
    return jax.shard_map(
        shards,
        mesh=mesh,
        in_specs=placed,
        out_specs=P("segment", None, "mp", None),
        check_vma=False,
    )
```

```python
import functools
import math

import jax
import jax.numpy as jnp
from jax import lax
from jax.experimental import pallas as pl
from jax.experimental.pallas import tpu as pltpu
from jax.sharding import PartitionSpec as P

HS = 64
SCALING = 1.0 / math.sqrt(HS)
EPSILON = 1e-05
ROWS_DIMS = (((0,), (0,)), ((), ()))
FEAT_DIMS = (((1,), (1,)), ((), ()))


def dot_nn(a, b):
    return lax.dot_general(a, b, (((1,), (0,)), ((), ())), preferred_element_type=jnp.float32)


def dot_nt(a, b):
    return lax.dot_general(a, b, FEAT_DIMS, preferred_element_type=jnp.float32)


def dot_tn(a, b):
    return lax.dot_general(a, b, ROWS_DIMS, preferred_element_type=jnp.float32)


def row_stats(values):
    center = values - jnp.mean(values, axis=-1, keepdims=True)
    variance = jnp.mean(center * center, axis=-1, keepdims=True)
    return center, lax.rsqrt(variance + EPSILON)


def layer_norm(values, norm_gain, offset):
    center, inverse = row_stats(values.astype(jnp.float32))
    return (center * inverse * norm_gain + offset).astype(jnp.bfloat16)


def ids_along(lengths_ref, row, shape, axis):
    places = lax.broadcasted_iota(jnp.int32, shape, axis)
    bound = 0
    ids = jnp.zeros(shape, jnp.int32)
    for piece in range(lengths_ref.shape[2]):
        bound = bound + lengths_ref[row, 0, piece]
        ids = ids + (places >= bound).astype(jnp.int32)
    return ids


def softmax(queries, keys, allowed):
    scores = jnp.where(allowed, dot_nt(queries, keys) * SCALING, -1e30)
    raised = jnp.exp(scores - jnp.max(scores, axis=-1, keepdims=True))
    return raised / jnp.sum(raised, axis=-1, keepdims=True)


def scores_grad(probs, grad_context, values):
    grad_probs = dot_nt(grad_context, values)
    inner = jnp.sum(grad_probs * probs, axis=-1, keepdims=True)
    return (probs * (grad_probs - inner)).astype(jnp.bfloat16)


def side_by_side(parts):
    return jnp.concatenate(parts, axis=1).astype(jnp.bfloat16)


def enc_forward_kernel(
    core, lengths, x, own, other, gains, biases, normed, queries, values, context, copies, probs
):
    first = core[0] == 0
    rows = x.shape[0]
    normed_rows = layer_norm(x[...], gains[0:1, :], biases[0:1, :])
    normed[...] = normed_rows
    projected = []
    for kind in range(3):
        matrix = jnp.where(first, own[kind], other[kind])
        projected.append(dot_nt(normed_rows, matrix).astype(jnp.bfloat16))
    queries[...] = projected[0]
    values[...] = projected[2]
    allowed = ids_along(lengths, core[0], (rows, 1), 0) == ids_along(lengths, core[0], (1, rows), 1)
    parts = []
    for head in range(queries.shape[1] // HS):
        at = slice(head * HS, (head + 1) * HS)
        weights = softmax(projected[0][:, at], projected[1][:, at], allowed)
        probs[head] = weights
        parts.append(dot_nn(weights.astype(jnp.bfloat16), projected[2][:, at]))
    block = side_by_side(parts)
    context[...] = block
    for copy in range(copies.shape[0]):
        copies[copy] = block


def token_kernel(core, tokens, upstream, own, other, gains, biases, queries, grad_context):
    first = core[0] == 0
    own_tokens = jnp.where(first, tokens[0], tokens[1])
    normed_tokens = layer_norm(own_tokens, gains[1:2, :], biases[1:2, :])
    matrix = jnp.where(first, other[0], own[0])
    queries[...] = dot_nt(normed_tokens, matrix).astype(jnp.bfloat16)
    matrix = jnp.where(first, other[3], own[3])
    own_upstream = jnp.where(first, upstream[0], upstream[1])
    grad_context[...] = dot_nt(own_upstream, matrix).astype(jnp.bfloat16)


def dec_kernel(
    core, place, frame_lens, token_lens, x, context, own_key, own_value, other_key, other_value,
    token_queries, token_grads, gains, biases, *refs,
):
    devices = context.shape[0]
    out_shards, refs = refs[:devices], refs[devices:]
    partial, states, normed, key_grad, value_grad, dec_context, scratch = refs
    first = core[0] == 0
    rows = x.shape[0]
    steps = devices // 2
    passed, swapped = out_shards[: steps + 1], out_shards[steps + 1 :]

    def context_at(back):
        return context[(place[0] + jnp.where(first, devices - back, back)) % devices]

    pairs = [(0, passed[0], steps, passed[steps])]
    for back in range(1, steps):
        pairs.append((back, passed[back], devices - back, swapped[back - 1]))
    summed = x[...].astype(jnp.float32)
    for back, shard, far_back, far_shard in pairs:
        left = jnp.concatenate([context_at(back), context_at(far_back)], axis=1)
        right = jnp.concatenate([shard[...], far_shard[...]], axis=0)
        summed = summed + dot_nn(left, right)
    scratch[...] = summed
    all_states = scratch[...].astype(jnp.bfloat16)
    shard = states.shape[0]
    start = pl.multiple_of(place[0] * shard, shard)
    states[...] = scratch[pl.ds(start, shard), :].astype(jnp.bfloat16)
    normed_rows = layer_norm(all_states, gains[2:3, :], biases[2:3, :])
    normed[...] = normed_rows
    matrix = [
        jnp.where(first, other_key[0], own_key[0]),
        jnp.where(first, other_value[0], own_value[0]),
    ]
    queries = token_queries[...]
    grad_context = token_grads[...]
    keys = dot_nt(normed_rows, matrix[0]).astype(jnp.bfloat16)
    values = dot_nt(normed_rows, matrix[1]).astype(jnp.bfloat16)
    count = queries.shape[0]
    token_ids = ids_along(token_lens, core[0], (count, 1), 0)
    allowed = token_ids == ids_along(frame_lens, core[0], (1, rows), 1)
    key_parts, value_parts, context_parts = [], [], []
    for head in range(queries.shape[1] // HS):
        at = slice(head * HS, (head + 1) * HS)
        weights = softmax(queries[:, at], keys[:, at], allowed)
        rounded = weights.astype(jnp.bfloat16)
        context_parts.append(dot_nn(rounded, values[:, at]))
        grad_scores = scores_grad(weights, grad_context[:, at], values[:, at])
        key_parts.append(dot_tn(grad_scores, queries[:, at]) * SCALING)
        value_parts.append(dot_tn(rounded, grad_context[:, at]))
    key_block, value_block = side_by_side(key_parts), side_by_side(value_parts)
    key_grad[...] = key_block
    value_grad[...] = value_block
    dec_context[...] = side_by_side(context_parts)
    partial[...] = (dot_nn(key_block, matrix[0]) + dot_nn(value_block, matrix[1])).astype(
        jnp.bfloat16
    )


def store_terms(products, term):
    high = products[0].shape[0]
    for index, product in enumerate(products):
        term[index * high : (index + 1) * high, :] = product.astype(jnp.bfloat16)


def dec_terms_kernel(core, key_grad, value_grad, context, normed, upstream, term):
    products = [
        dot_tn(key_grad[...], normed[...]),
        dot_tn(value_grad[...], normed[...]),
        dot_tn(context[...], jnp.where(core[0] == 0, upstream[0], upstream[1])),
    ]
    store_terms(products, term)


def norm_backward_kernel(pieces, states, gains, grads):
    summed = pieces[0].astype(jnp.float32)
    for index in range(1, pieces.shape[0]):
        summed = summed + pieces[index].astype(jnp.float32)
    center, inverse = row_stats(states[...].astype(jnp.float32))
    normed = center * inverse
    scaled = summed * gains[2:3, :]
    result = inverse * (
        scaled
        - jnp.mean(scaled, axis=-1, keepdims=True)
        - normed * jnp.mean(scaled * normed, axis=-1, keepdims=True)
    )
    block = result.astype(jnp.bfloat16)
    for copy in range(grads.shape[0]):
        grads[copy] = block


def enc_backward_kernel(
    core, grads, own, other, queries, values, probs, context, normed, term
):
    first = core[0] == 0
    grad_rows = grads[...]
    att_grad = dot_nt(grad_rows, jnp.where(first, own[0], other[0])).astype(jnp.bfloat16)
    query_rows, value_rows = queries[...], values[...]
    key_parts, value_parts = [], []
    for head in range(query_rows.shape[1] // HS):
        at = slice(head * HS, (head + 1) * HS)
        weights = probs[head]
        grad_scores = scores_grad(weights, att_grad[:, at], value_rows[:, at])
        key_parts.append(dot_tn(grad_scores, query_rows[:, at]) * SCALING)
        value_parts.append(dot_tn(weights.astype(jnp.bfloat16), att_grad[:, at]))
    products = [
        dot_tn(side_by_side(key_parts), normed[...]),
        dot_tn(side_by_side(value_parts), normed[...]),
        dot_tn(context[...], grad_rows),
    ]
    store_terms(products, term)


def chunks_kernel(core, enc_term, enc_sent, dec_term, dec_sent, tiles):
    first = core[0] == 0
    rows, cols = enc_term.shape
    high = rows // 8
    for block in range(cols // 128):
        at = slice(block * 128, (block + 1) * 128)
        kept = jnp.where(first, enc_term[:, at], dec_term[:, at])
        received = jnp.where(first, enc_sent[:, at], dec_sent[:, at])
        total = kept.astype(jnp.float32) + received.astype(jnp.float32)
        part = total.reshape(high, 8, 128)
        tiles[block * high : (block + 1) * high] = part.astype(jnp.bfloat16)


def sum_copies_kernel(pieces, copies):
    summed = pieces[0].astype(jnp.float32)
    for index in range(1, pieces.shape[0]):
        summed = summed + pieces[index].astype(jnp.float32)
    block = summed.astype(jnp.bfloat16)
    for copy in range(copies.shape[0]):
        copies[copy] = block


def pick_copies_kernel(core, blocks, copies):
    block = jnp.where(core[0] == 0, blocks[0], blocks[1])
    for copy in range(copies.shape[0]):
        copies[copy] = block


def from_chunks_kernel(tiles, gradient):
    rows, cols = gradient.shape
    high = rows // 8
    for block in range(cols // 128):
        part = tiles[block * high : (block + 1) * high].astype(jnp.float32)
        gradient[:, block * 128 : (block + 1) * 128] = part.reshape(rows, 128)


def call(
    kernel, outs, scalars, arrays, blocks=None, scratch=(), kept=(), read=(), cost=None
):
    blocks = blocks or {}

    def spec(index, array):
        shape, at = blocks.get(index, (array.shape, (0,) * array.ndim))
        return pl.BlockSpec(shape, lambda i: at)

    def out(index, shape, dtype):
        return pltpu.HBM(shape, dtype) if index in kept else jax.ShapeDtypeStruct(shape, dtype)

    arrays = [
        pltpu.with_memory_space_constraint(array, pltpu.HBM) if index in read else array
        for index, array in enumerate(arrays)
    ]
    result = pl.pallas_call(
        kernel,
        grid=(1,),
        out_shape=[out(index, *what) for index, what in enumerate(outs)],
        in_specs=[pl.BlockSpec(memory_space=pltpu.SMEM) for _ in scalars]
        + [spec(index, array) for index, array in enumerate(arrays)],
        out_specs=[
            pl.BlockSpec(shape, functools.partial(lambda n, i: (0,) * n, len(shape)))
            for shape, _ in outs
        ],
        scratch_shapes=list(scratch),
        cost_estimate=cost,
        compiler_params=pltpu.CompilerParams(vmem_limit_bytes=48 << 20),
    )(*scalars, *arrays)
    return result[0] if len(outs) == 1 else result


def swap(block):
    return lax.ppermute(block, "segment", [(0, 1), (1, 0)])


def shards(
    frames, dec_states, out_grad, frame_lengths, token_lengths, weights, norm_gains, norm_biases
):
    bf16, f32 = jnp.bfloat16, jnp.float32
    core = lax.axis_index("segment")
    first = core == 0
    own = weights[0]
    shard_rows, features = frames.shape[1:]
    mp = lax.axis_size("mp")
    dp = lax.axis_size("dp")
    head_cols = own.shape[1]
    heads = head_cols // HS
    rows = shard_rows * mp
    count = dec_states.shape[1]
    near_groups = [[x * 8 + y * 2 + b for x in range(4) for b in range(2)] for y in range(4)]
    far_groups = [[x * 8 + y * 2 + b for y in range(4)] for x in range(4) for b in range(2)]
    near, far = len(near_groups[0]), len(far_groups[0])

    def exchange(blocks, axis="mp", groups=None):
        return lax.all_to_all(blocks, axis, 0, 0, axis_index_groups=groups)

    core_id = core.astype(jnp.int32).reshape(1)
    place = lax.axis_index("mp").astype(jnp.int32).reshape(1)

    copies = call(
        pick_copies_kernel,
        [((mp, shard_rows, features), bf16)],
        (core_id,),
        (frames,),
        kept=(0,),
        read=(0,),
    )
    copies, own = lax.optimization_barrier((copies, own))
    other = swap(own)
    shard = jnp.where(first, own[3], other[3])
    def passing(block, hop):
        up = [(i, (i + hop) % mp) for i in range(mp)]
        down = [(mp + i, mp + (i - hop) % mp) for i in range(mp)]
        return lax.ppermute(block, ("segment", "mp"), up + down)

    passed, swapped = [shard], []
    for index in range(mp // 2 - 1):
        passed.append(passing(passed[-1], 1))
        swapped.append(swap(passed[-1]))
    passed.append(passing(passed[-2], 2))
    out_shards = passed + swapped
    enc_full = exchange(copies).reshape(rows, features)

    token_queries, token_grads = call(
        token_kernel,
        [((count, head_cols), bf16)] * 2,
        (core_id,),
        (dec_states, out_grad, own, other, norm_gains, norm_biases),
        kept=(0, 1),
        read=(0, 1, 2, 3),
    )
    enc_full, token_queries, token_grads = lax.optimization_barrier(
        (enc_full, token_queries, token_grads)
    )
    weight_block = ((3, head_cols, features), (0, 0, 0))
    normed, queries, values, context, context_copies, probs = call(
        enc_forward_kernel,
        [
            ((rows, features), bf16),
            ((rows, head_cols), bf16),
            ((rows, head_cols), bf16),
            ((rows, head_cols), bf16),
            ((mp, rows, head_cols), bf16),
            ((heads, rows, rows), f32),
        ],
        (core_id, frame_lengths),
        (enc_full, own, other, norm_gains, norm_biases),
        {1: weight_block, 2: weight_block},
        kept=(0, 1, 2, 3, 4, 5),
        cost=pl.CostEstimate(flops=3_000_000_000, transcendentals=0, bytes_accessed=0),
    )
    context_full, out_shards = lax.optimization_barrier((exchange(context_copies), out_shards))
    key_block = ((1, head_cols, features), (1, 0, 0))
    value_block = ((1, head_cols, features), (2, 0, 0))
    partial, states, state_normed, dec_key_grad, dec_value_grad, dec_context = call(
        dec_kernel,
        [
            ((rows, features), bf16),
            ((shard_rows, features), bf16),
            ((rows, features), bf16),
            ((rows, head_cols), bf16),
            ((rows, head_cols), bf16),
            ((count, head_cols), bf16),
        ],
        (core_id, place, frame_lengths, token_lengths),
        (
            enc_full, context_full, own, own, other, other, token_queries, token_grads,
            norm_gains, norm_biases, *out_shards,
        ),
        {2: key_block, 3: value_block, 4: key_block, 5: value_block},
        scratch=[pltpu.VMEM((rows, features), f32)],
        kept=(1, 2, 3, 4, 5),
        read=(2, 3, 4, 5, 6, 7),
    )
    pieces = exchange(partial.reshape(mp, shard_rows, features))
    whole = [((3 * head_cols, features), bf16)]
    dec_term = call(
        dec_terms_kernel,
        whole,
        (core_id,),
        (dec_key_grad, dec_value_grad, dec_context, state_normed, out_grad),
        kept=(0,),
        read=(0, 1, 2, 3, 4),
    )
    grads = call(
        norm_backward_kernel,
        [((mp, shard_rows, features), bf16)],
        (),
        (pieces, states, norm_gains),
        read=(1,),
    )
    grads_full = exchange(grads).reshape(rows, features)
    last_block = ((1, head_cols, features), (3, 0, 0))
    enc_term = call(
        enc_backward_kernel,
        whole,
        (core_id,),
        (grads_full, own, other, queries, values, probs, context, normed),
        {1: last_block, 2: last_block},
        read=(1, 2, 3, 4, 5, 6, 7),
    )
    dec_sent = lax.ppermute(dec_term, "segment", [(0, 1)])
    enc_sent = lax.ppermute(enc_term, "segment", [(1, 0)])
    size = 3 * head_cols * features // 1024
    each = size // near
    tiles = call(
        chunks_kernel,
        [((size, 8, 128), bf16)],
        (core_id,),
        (enc_term, enc_sent, dec_term, dec_sent),
        read=(2,),
    )
    parts = exchange(tiles.reshape(near, each, 8, 128), "dp", near_groups)
    parts = call(sum_copies_kernel, [((far, each, 8, 128), bf16)], (), (parts,))
    parts = exchange(parts, "dp", far_groups)
    parts = call(sum_copies_kernel, [((near, each, 8, 128), bf16)], (), (parts,))
    parts = exchange(parts, "dp", near_groups).reshape(size, 8, 128)
    gradient = call(from_chunks_kernel, [((3 * head_cols, features), f32)], (), (parts,))
    return gradient.reshape(1, 3, head_cols, features)


def solution(mesh):
    placed = (
        P(None, ("dp", "mp"), None),
        P(None, "dp", None),
        P(None, "dp", None),
        P(None, "dp", None),
        P(None, "dp", None),
        P("segment", None, "mp", None),
        P(),
        P(),
    )
    return jax.shard_map(
        shards,
        mesh=mesh,
        in_specs=placed,
        out_specs=P("segment", None, "mp", None),
        check_vma=False,
    )
```

```python
import functools
import math

import jax
import jax.numpy as jnp
from jax import lax
from jax.experimental import pallas as pl
from jax.experimental.pallas import tpu as pltpu
from jax.sharding import PartitionSpec as P

HS = 64
SCALING = 1.0 / math.sqrt(HS)
EPSILON = 1e-05
ROWS_DIMS = (((0,), (0,)), ((), ()))
FEAT_DIMS = (((1,), (1,)), ((), ()))


def dot_nn(a, b):
    return lax.dot_general(a, b, (((1,), (0,)), ((), ())), preferred_element_type=jnp.float32)


def dot_nt(a, b):
    return lax.dot_general(a, b, FEAT_DIMS, preferred_element_type=jnp.float32)


def dot_tn(a, b):
    return lax.dot_general(a, b, ROWS_DIMS, preferred_element_type=jnp.float32)


def row_stats(values):
    center = values - jnp.mean(values, axis=-1, keepdims=True)
    variance = jnp.mean(center * center, axis=-1, keepdims=True)
    return center, lax.rsqrt(variance + EPSILON)


def layer_norm(values, norm_gain, offset):
    center, inverse = row_stats(values.astype(jnp.float32))
    return (center * inverse * norm_gain + offset).astype(jnp.bfloat16)


def ids_along(lengths_ref, row, shape, axis):
    places = lax.broadcasted_iota(jnp.int32, shape, axis)
    bound = 0
    ids = jnp.zeros(shape, jnp.int32)
    for piece in range(lengths_ref.shape[2]):
        bound = bound + lengths_ref[row, 0, piece]
        ids = ids + (places >= bound).astype(jnp.int32)
    return ids


def softmax(queries, keys, allowed):
    scores = jnp.where(allowed, dot_nt(queries, keys) * SCALING, -1e30)
    raised = jnp.exp(scores - jnp.max(scores, axis=-1, keepdims=True))
    return raised / jnp.sum(raised, axis=-1, keepdims=True)


def scores_grad(probs, grad_context, values):
    grad_probs = dot_nt(grad_context, values)
    inner = jnp.sum(grad_probs * probs, axis=-1, keepdims=True)
    return (probs * (grad_probs - inner)).astype(jnp.bfloat16)


def side_by_side(parts):
    return jnp.concatenate(parts, axis=1).astype(jnp.bfloat16)


def enc_forward_kernel(
    core, lengths, x, own, other, gains, biases, normed, queries, values, context, copies, probs
):
    first = core[0] == 0
    rows = x.shape[0]
    normed_rows = layer_norm(x[...], gains[0:1, :], biases[0:1, :])
    normed[...] = normed_rows
    projected = []
    for kind in range(3):
        matrix = jnp.where(first, own[kind], other[kind])
        projected.append(dot_nt(normed_rows, matrix).astype(jnp.bfloat16))
    queries[...] = projected[0]
    values[...] = projected[2]
    allowed = ids_along(lengths, core[0], (rows, 1), 0) == ids_along(lengths, core[0], (1, rows), 1)
    parts = []
    for head in range(queries.shape[1] // HS):
        at = slice(head * HS, (head + 1) * HS)
        weights = softmax(projected[0][:, at], projected[1][:, at], allowed)
        probs[head] = weights
        parts.append(dot_nn(weights.astype(jnp.bfloat16), projected[2][:, at]))
    block = side_by_side(parts)
    context[...] = block
    for copy in range(copies.shape[0]):
        copies[copy] = block


def token_kernel(core, tokens, upstream, own, other, gains, biases, queries, grad_context):
    first = core[0] == 0
    own_tokens = jnp.where(first, tokens[0], tokens[1])
    normed_tokens = layer_norm(own_tokens, gains[1:2, :], biases[1:2, :])
    matrix = jnp.where(first, other[0], own[0])
    queries[...] = dot_nt(normed_tokens, matrix).astype(jnp.bfloat16)
    matrix = jnp.where(first, other[3], own[3])
    own_upstream = jnp.where(first, upstream[0], upstream[1])
    grad_context[...] = dot_nt(own_upstream, matrix).astype(jnp.bfloat16)


def dec_kernel(
    core, place, frame_lens, token_lens, x, context, own_key, own_value, other_key, other_value,
    token_queries, token_grads, gains, biases, *refs,
):
    devices = context.shape[0]
    out_shards, refs = refs[:devices], refs[devices:]
    partial, states, normed, key_grad, value_grad, dec_context, scratch = refs
    first = core[0] == 0
    rows = x.shape[0]
    steps = devices // 2
    passed, swapped = out_shards[: steps + 1], out_shards[steps + 1 :]

    def context_at(back):
        return context[(place[0] + jnp.where(first, devices - back, back)) % devices]

    pairs = [(0, passed[0], steps, passed[steps])]
    for back in range(1, steps):
        pairs.append((back, passed[back], devices - back, swapped[back - 1]))
    summed = x[...].astype(jnp.float32)
    for back, shard, far_back, far_shard in pairs:
        left = jnp.concatenate([context_at(back), context_at(far_back)], axis=1)
        right = jnp.concatenate([shard[...], far_shard[...]], axis=0)
        summed = summed + dot_nn(left, right)
    scratch[...] = summed
    all_states = scratch[...].astype(jnp.bfloat16)
    shard = states.shape[0]
    start = pl.multiple_of(place[0] * shard, shard)
    states[...] = scratch[pl.ds(start, shard), :].astype(jnp.bfloat16)
    normed_rows = layer_norm(all_states, gains[2:3, :], biases[2:3, :])
    normed[...] = normed_rows
    matrix = [
        jnp.where(first, other_key[0], own_key[0]),
        jnp.where(first, other_value[0], own_value[0]),
    ]
    queries = token_queries[...]
    grad_context = token_grads[...]
    keys = dot_nt(normed_rows, matrix[0]).astype(jnp.bfloat16)
    values = dot_nt(normed_rows, matrix[1]).astype(jnp.bfloat16)
    count = queries.shape[0]
    token_ids = ids_along(token_lens, core[0], (count, 1), 0)
    allowed = token_ids == ids_along(frame_lens, core[0], (1, rows), 1)
    key_parts, value_parts, context_parts = [], [], []
    for head in range(queries.shape[1] // HS):
        at = slice(head * HS, (head + 1) * HS)
        weights = softmax(queries[:, at], keys[:, at], allowed)
        rounded = weights.astype(jnp.bfloat16)
        context_parts.append(dot_nn(rounded, values[:, at]))
        grad_scores = scores_grad(weights, grad_context[:, at], values[:, at])
        key_parts.append(dot_tn(grad_scores, queries[:, at]) * SCALING)
        value_parts.append(dot_tn(rounded, grad_context[:, at]))
    key_block, value_block = side_by_side(key_parts), side_by_side(value_parts)
    key_grad[...] = key_block
    value_grad[...] = value_block
    dec_context[...] = side_by_side(context_parts)
    partial[...] = (dot_nn(key_block, matrix[0]) + dot_nn(value_block, matrix[1])).astype(
        jnp.bfloat16
    )


def store_terms(products, term):
    high = products[0].shape[0]
    for index, product in enumerate(products):
        term[index * high : (index + 1) * high, :] = product.astype(jnp.bfloat16)


def dec_terms_kernel(core, key_grad, value_grad, context, normed, upstream, term):
    products = [
        dot_tn(key_grad[...], normed[...]),
        dot_tn(value_grad[...], normed[...]),
        dot_tn(context[...], jnp.where(core[0] == 0, upstream[0], upstream[1])),
    ]
    store_terms(products, term)


def norm_backward_kernel(pieces, states, gains, grads):
    summed = pieces[0].astype(jnp.float32)
    for index in range(1, pieces.shape[0]):
        summed = summed + pieces[index].astype(jnp.float32)
    center, inverse = row_stats(states[...].astype(jnp.float32))
    normed = center * inverse
    scaled = summed * gains[2:3, :]
    result = inverse * (
        scaled
        - jnp.mean(scaled, axis=-1, keepdims=True)
        - normed * jnp.mean(scaled * normed, axis=-1, keepdims=True)
    )
    block = result.astype(jnp.bfloat16)
    for copy in range(grads.shape[0]):
        grads[copy] = block


def enc_backward_kernel(
    core, grads, own, other, queries, values, probs, context, normed, term
):
    first = core[0] == 0
    grad_rows = grads[...]
    att_grad = dot_nt(grad_rows, jnp.where(first, own[0], other[0])).astype(jnp.bfloat16)
    query_rows, value_rows = queries[...], values[...]
    key_parts, value_parts = [], []
    for head in range(query_rows.shape[1] // HS):
        at = slice(head * HS, (head + 1) * HS)
        weights = probs[head]
        grad_scores = scores_grad(weights, att_grad[:, at], value_rows[:, at])
        key_parts.append(dot_tn(grad_scores, query_rows[:, at]) * SCALING)
        value_parts.append(dot_tn(weights.astype(jnp.bfloat16), att_grad[:, at]))
    products = [
        dot_tn(side_by_side(key_parts), normed[...]),
        dot_tn(side_by_side(value_parts), normed[...]),
        dot_tn(context[...], grad_rows),
    ]
    store_terms(products, term)


def chunks_kernel(core, enc_term, enc_sent, dec_term, dec_sent, tiles):
    first = core[0] == 0
    rows, cols = enc_term.shape
    high = rows // 8
    for block in range(cols // 128):
        at = slice(block * 128, (block + 1) * 128)
        kept = jnp.where(first, enc_term[:, at], dec_term[:, at])
        received = jnp.where(first, enc_sent[:, at], dec_sent[:, at])
        total = kept.astype(jnp.float32) + received.astype(jnp.float32)
        part = total.reshape(high, 8, 128)
        tiles[block * high : (block + 1) * high] = part.astype(jnp.bfloat16)


def sum_copies_kernel(pieces, copies):
    summed = pieces[0].astype(jnp.float32)
    for index in range(1, pieces.shape[0]):
        summed = summed + pieces[index].astype(jnp.float32)
    block = summed.astype(jnp.bfloat16)
    for copy in range(copies.shape[0]):
        copies[copy] = block


def pick_copies_kernel(core, blocks, copies):
    block = jnp.where(core[0] == 0, blocks[0], blocks[1])
    for copy in range(copies.shape[0]):
        copies[copy] = block


def from_chunks_kernel(tiles, gradient):
    rows, cols = gradient.shape
    high = rows // 8
    for block in range(cols // 128):
        part = tiles[block * high : (block + 1) * high].astype(jnp.float32)
        gradient[:, block * 128 : (block + 1) * 128] = part.reshape(rows, 128)


def call(
    kernel, outs, scalars, arrays, blocks=None, scratch=(), kept=(), read=(), cost=None
):
    blocks = blocks or {}

    def spec(index, array):
        shape, at = blocks.get(index, (array.shape, (0,) * array.ndim))
        return pl.BlockSpec(shape, lambda i: at)

    def out(index, shape, dtype):
        return pltpu.HBM(shape, dtype) if index in kept else jax.ShapeDtypeStruct(shape, dtype)

    arrays = [
        pltpu.with_memory_space_constraint(array, pltpu.HBM) if index in read else array
        for index, array in enumerate(arrays)
    ]
    result = pl.pallas_call(
        kernel,
        grid=(1,),
        out_shape=[out(index, *what) for index, what in enumerate(outs)],
        in_specs=[pl.BlockSpec(memory_space=pltpu.SMEM) for _ in scalars]
        + [spec(index, array) for index, array in enumerate(arrays)],
        out_specs=[
            pl.BlockSpec(shape, functools.partial(lambda n, i: (0,) * n, len(shape)))
            for shape, _ in outs
        ],
        scratch_shapes=list(scratch),
        cost_estimate=cost,
        compiler_params=pltpu.CompilerParams(vmem_limit_bytes=48 << 20),
    )(*scalars, *arrays)
    return result[0] if len(outs) == 1 else result


def swap(block):
    return lax.ppermute(block, "segment", [(0, 1), (1, 0)])


def shards(
    frames, dec_states, out_grad, frame_lengths, token_lengths, weights, norm_gains, norm_biases
):
    bf16, f32 = jnp.bfloat16, jnp.float32
    core = lax.axis_index("segment")
    first = core == 0
    own = weights[0]
    shard_rows, features = frames.shape[1:]
    mp = lax.axis_size("mp")
    dp = lax.axis_size("dp")
    head_cols = own.shape[1]
    heads = head_cols // HS
    rows = shard_rows * mp
    count = dec_states.shape[1]
    near_groups = [[x * 8 + y * 2 + b for x in range(4) for b in range(2)] for y in range(4)]
    far_groups = [[x * 8 + y * 2 + b for y in range(4)] for x in range(4) for b in range(2)]
    near, far = len(near_groups[0]), len(far_groups[0])

    def exchange(blocks, axis="mp", groups=None):
        return lax.all_to_all(blocks, axis, 0, 0, axis_index_groups=groups)

    core_id = core.astype(jnp.int32).reshape(1)
    place = lax.axis_index("mp").astype(jnp.int32).reshape(1)

    copies = call(
        pick_copies_kernel,
        [((mp, shard_rows, features), bf16)],
        (core_id,),
        (frames,),
        kept=(0,),
        read=(0,),
    )
    copies, own = lax.optimization_barrier((copies, own))
    other = swap(own)
    shard = jnp.where(first, own[3], other[3])
    def passing(block, hop):
        up = [(i, (i + hop) % mp) for i in range(mp)]
        down = [(mp + i, mp + (i - hop) % mp) for i in range(mp)]
        return lax.ppermute(block, ("segment", "mp"), up + down)

    passed = [shard]
    for _ in range(mp // 2 - 1):
        passed.append(passing(passed[-1], 1))
    passed.append(passing(passed[-2], 2))
    swapped = [swap(block) for block in passed[1:-1]]
    out_shards = passed + swapped
    enc_full = exchange(copies).reshape(rows, features)

    token_queries, token_grads = call(
        token_kernel,
        [((count, head_cols), bf16)] * 2,
        (core_id,),
        (dec_states, out_grad, own, other, norm_gains, norm_biases),
        kept=(0, 1),
        read=(0, 1),
    )
    enc_full, token_queries, token_grads = lax.optimization_barrier(
        (enc_full, token_queries, token_grads)
    )
    weight_block = ((3, head_cols, features), (0, 0, 0))
    normed, queries, values, context, context_copies, probs = call(
        enc_forward_kernel,
        [
            ((rows, features), bf16),
            ((rows, head_cols), bf16),
            ((rows, head_cols), bf16),
            ((rows, head_cols), bf16),
            ((mp, rows, head_cols), bf16),
            ((heads, rows, rows), f32),
        ],
        (core_id, frame_lengths),
        (enc_full, own, other, norm_gains, norm_biases),
        {1: weight_block, 2: weight_block},
        kept=(0, 1, 2, 3, 4, 5),
        cost=pl.CostEstimate(flops=3_000_000_000, transcendentals=0, bytes_accessed=0),
    )
    context_full = exchange(context_copies)
    key_block = ((1, head_cols, features), (1, 0, 0))
    value_block = ((1, head_cols, features), (2, 0, 0))
    partial, states, state_normed, dec_key_grad, dec_value_grad, dec_context = call(
        dec_kernel,
        [
            ((rows, features), bf16),
            ((shard_rows, features), bf16),
            ((rows, features), bf16),
            ((rows, head_cols), bf16),
            ((rows, head_cols), bf16),
            ((count, head_cols), bf16),
        ],
        (core_id, place, frame_lengths, token_lengths),
        (
            enc_full, context_full, own, own, other, other, token_queries, token_grads,
            norm_gains, norm_biases, *out_shards,
        ),
        {2: key_block, 3: value_block, 4: key_block, 5: value_block},
        scratch=[pltpu.VMEM((rows, features), f32)],
        kept=(1, 2, 3, 4, 5),
        read=(2, 3, 4, 5, 6, 7, 17),
    )
    pieces = exchange(partial.reshape(mp, shard_rows, features))
    whole = [((3 * head_cols, features), bf16)]
    dec_term = call(
        dec_terms_kernel,
        whole,
        (core_id,),
        (dec_key_grad, dec_value_grad, dec_context, state_normed, out_grad),
        kept=(0,),
        read=(0, 1, 2, 3, 4),
    )
    grads = call(
        norm_backward_kernel,
        [((mp, shard_rows, features), bf16)],
        (),
        (pieces, states, norm_gains),
        read=(1,),
    )
    grads_full = exchange(grads).reshape(rows, features)
    last_block = ((1, head_cols, features), (3, 0, 0))
    enc_term = call(
        enc_backward_kernel,
        whole,
        (core_id,),
        (grads_full, own, other, queries, values, probs, context, normed),
        {1: last_block, 2: last_block},
        read=(1, 2, 3, 4, 5, 6, 7),
    )
    dec_sent = lax.ppermute(dec_term, "segment", [(0, 1)])
    enc_sent = lax.ppermute(enc_term, "segment", [(1, 0)])
    size = 3 * head_cols * features // 1024
    each = size // near
    tiles = call(
        chunks_kernel,
        [((size, 8, 128), bf16)],
        (core_id,),
        (enc_term, enc_sent, dec_term, dec_sent),
        read=(2,),
    )
    parts = exchange(tiles.reshape(near, each, 8, 128), "dp", near_groups)
    parts = call(sum_copies_kernel, [((far, each, 8, 128), bf16)], (), (parts,))
    parts = exchange(parts, "dp", far_groups)
    parts = call(sum_copies_kernel, [((near, each, 8, 128), bf16)], (), (parts,))
    parts = exchange(parts, "dp", near_groups).reshape(size, 8, 128)
    gradient = call(from_chunks_kernel, [((3 * head_cols, features), f32)], (), (parts,))
    return gradient.reshape(1, 3, head_cols, features)


def solution(mesh):
    placed = (
        P(None, ("dp", "mp"), None),
        P(None, "dp", None),
        P(None, "dp", None),
        P(None, "dp", None),
        P(None, "dp", None),
        P("segment", None, "mp", None),
        P(),
        P(),
    )
    return jax.shard_map(
        shards,
        mesh=mesh,
        in_specs=placed,
        out_specs=P("segment", None, "mp", None),
        check_vma=False,
    )
```

```python
import functools
import math

import jax
import jax.numpy as jnp
from jax import lax
from jax.experimental import pallas as pl
from jax.experimental.pallas import tpu as pltpu
from jax.sharding import PartitionSpec as P

HS = 64
SCALING = 1.0 / math.sqrt(HS)
EPSILON = 1e-05
ROWS_DIMS = (((0,), (0,)), ((), ()))
FEAT_DIMS = (((1,), (1,)), ((), ()))


def dot_nn(a, b):
    return lax.dot_general(a, b, (((1,), (0,)), ((), ())), preferred_element_type=jnp.float32)


def dot_nt(a, b):
    return lax.dot_general(a, b, FEAT_DIMS, preferred_element_type=jnp.float32)


def dot_tn(a, b):
    return lax.dot_general(a, b, ROWS_DIMS, preferred_element_type=jnp.float32)


def row_stats(values):
    center = values - jnp.mean(values, axis=-1, keepdims=True)
    variance = jnp.mean(center * center, axis=-1, keepdims=True)
    return center, lax.rsqrt(variance + EPSILON)


def layer_norm(values, norm_gain, offset):
    center, inverse = row_stats(values.astype(jnp.float32))
    return (center * inverse * norm_gain + offset).astype(jnp.bfloat16)


def ids_along(lengths_ref, row, shape, axis):
    places = lax.broadcasted_iota(jnp.int32, shape, axis)
    bound = 0
    ids = jnp.zeros(shape, jnp.int32)
    for piece in range(lengths_ref.shape[2]):
        bound = bound + lengths_ref[row, 0, piece]
        ids = ids + (places >= bound).astype(jnp.int32)
    return ids


def softmax(queries, keys, allowed):
    scores = jnp.where(allowed, dot_nt(queries, keys) * SCALING, -1e30)
    raised = jnp.exp(scores - jnp.max(scores, axis=-1, keepdims=True))
    return raised / jnp.sum(raised, axis=-1, keepdims=True)


def scores_grad(probs, grad_context, values):
    grad_probs = dot_nt(grad_context, values)
    inner = jnp.sum(grad_probs * probs, axis=-1, keepdims=True)
    return (probs * (grad_probs - inner)).astype(jnp.bfloat16)


def side_by_side(parts):
    return jnp.concatenate(parts, axis=1).astype(jnp.bfloat16)


def enc_forward_kernel(
    core, lengths, x, own, other, gains, biases, normed, queries, values, context, copies, probs
):
    first = core[0] == 0
    rows = x.shape[0]
    normed_rows = layer_norm(x[...], gains[0:1, :], biases[0:1, :])
    normed[...] = normed_rows
    projected = []
    for kind in range(3):
        matrix = jnp.where(first, own[kind], other[kind])
        projected.append(dot_nt(normed_rows, matrix).astype(jnp.bfloat16))
    queries[...] = projected[0]
    values[...] = projected[2]
    allowed = ids_along(lengths, core[0], (rows, 1), 0) == ids_along(lengths, core[0], (1, rows), 1)
    parts = []
    for head in range(queries.shape[1] // HS):
        at = slice(head * HS, (head + 1) * HS)
        weights = softmax(projected[0][:, at], projected[1][:, at], allowed)
        probs[head] = weights
        parts.append(dot_nn(weights.astype(jnp.bfloat16), projected[2][:, at]))
    block = side_by_side(parts)
    context[...] = block
    for copy in range(copies.shape[0]):
        copies[copy] = block


def token_kernel(core, tokens, upstream, own, other, gains, biases, queries, grad_context):
    first = core[0] == 0
    own_tokens = jnp.where(first, tokens[0], tokens[1])
    normed_tokens = layer_norm(own_tokens, gains[1:2, :], biases[1:2, :])
    matrix = jnp.where(first, other[0], own[0])
    queries[...] = dot_nt(normed_tokens, matrix).astype(jnp.bfloat16)
    matrix = jnp.where(first, other[3], own[3])
    own_upstream = jnp.where(first, upstream[0], upstream[1])
    grad_context[...] = dot_nt(own_upstream, matrix).astype(jnp.bfloat16)


def dec_kernel(
    core, place, frame_lens, token_lens, x, context, own_key, own_value, other_key, other_value,
    token_queries, token_grads, gains, biases, *refs,
):
    devices = context.shape[0]
    out_shards, refs = refs[:devices], refs[devices:]
    partial, states, normed, key_grad, value_grad, dec_context, scratch = refs
    first = core[0] == 0
    rows = x.shape[0]
    steps = devices // 2
    passed, swapped = out_shards[: steps + 1], out_shards[steps + 1 :]

    def context_at(back):
        return context[(place[0] + jnp.where(first, devices - back, back)) % devices]

    pairs = [(0, passed[0], steps, passed[steps])]
    for back in range(1, steps):
        pairs.append((back, passed[back], devices - back, swapped[back - 1]))
    summed = x[...].astype(jnp.float32)
    for back, shard, far_back, far_shard in pairs:
        left = jnp.concatenate([context_at(back), context_at(far_back)], axis=1)
        right = jnp.concatenate([shard[...], far_shard[...]], axis=0)
        summed = summed + dot_nn(left, right)
    scratch[...] = summed
    all_states = scratch[...].astype(jnp.bfloat16)
    shard = states.shape[0]
    start = pl.multiple_of(place[0] * shard, shard)
    states[...] = scratch[pl.ds(start, shard), :].astype(jnp.bfloat16)
    normed_rows = layer_norm(all_states, gains[2:3, :], biases[2:3, :])
    normed[...] = normed_rows
    matrix = [
        jnp.where(first, other_key[0], own_key[0]),
        jnp.where(first, other_value[0], own_value[0]),
    ]
    queries = token_queries[...]
    grad_context = token_grads[...]
    keys = dot_nt(normed_rows, matrix[0]).astype(jnp.bfloat16)
    values = dot_nt(normed_rows, matrix[1]).astype(jnp.bfloat16)
    count = queries.shape[0]
    token_ids = ids_along(token_lens, core[0], (count, 1), 0)
    allowed = token_ids == ids_along(frame_lens, core[0], (1, rows), 1)
    key_parts, value_parts, context_parts = [], [], []
    for head in range(queries.shape[1] // HS):
        at = slice(head * HS, (head + 1) * HS)
        weights = softmax(queries[:, at], keys[:, at], allowed)
        rounded = weights.astype(jnp.bfloat16)
        context_parts.append(dot_nn(rounded, values[:, at]))
        grad_scores = scores_grad(weights, grad_context[:, at], values[:, at])
        key_parts.append(dot_tn(grad_scores, queries[:, at]) * SCALING)
        value_parts.append(dot_tn(rounded, grad_context[:, at]))
    key_block, value_block = side_by_side(key_parts), side_by_side(value_parts)
    key_grad[...] = key_block
    value_grad[...] = value_block
    dec_context[...] = side_by_side(context_parts)
    partial[...] = (dot_nn(key_block, matrix[0]) + dot_nn(value_block, matrix[1])).astype(
        jnp.bfloat16
    )


def store_terms(products, term):
    high = products[0].shape[0]
    for index, product in enumerate(products):
        term[index * high : (index + 1) * high, :] = product.astype(jnp.bfloat16)


def dec_terms_kernel(core, key_grad, value_grad, context, normed, upstream, term):
    products = [
        dot_tn(key_grad[...], normed[...]),
        dot_tn(value_grad[...], normed[...]),
        dot_tn(context[...], jnp.where(core[0] == 0, upstream[0], upstream[1])),
    ]
    store_terms(products, term)


def norm_backward_kernel(pieces, states, gains, grads):
    summed = pieces[0].astype(jnp.float32)
    for index in range(1, pieces.shape[0]):
        summed = summed + pieces[index].astype(jnp.float32)
    center, inverse = row_stats(states[...].astype(jnp.float32))
    normed = center * inverse
    scaled = summed * gains[2:3, :]
    result = inverse * (
        scaled
        - jnp.mean(scaled, axis=-1, keepdims=True)
        - normed * jnp.mean(scaled * normed, axis=-1, keepdims=True)
    )
    block = result.astype(jnp.bfloat16)
    for copy in range(grads.shape[0]):
        grads[copy] = block


def enc_backward_kernel(
    core, grads, own, other, queries, values, probs, context, normed, term
):
    first = core[0] == 0
    grad_rows = grads[...]
    att_grad = dot_nt(grad_rows, jnp.where(first, own[0], other[0])).astype(jnp.bfloat16)
    query_rows, value_rows = queries[...], values[...]
    key_parts, value_parts = [], []
    for head in range(query_rows.shape[1] // HS):
        at = slice(head * HS, (head + 1) * HS)
        weights = probs[head]
        grad_scores = scores_grad(weights, att_grad[:, at], value_rows[:, at])
        key_parts.append(dot_tn(grad_scores, query_rows[:, at]) * SCALING)
        value_parts.append(dot_tn(weights.astype(jnp.bfloat16), att_grad[:, at]))
    products = [
        dot_tn(side_by_side(key_parts), normed[...]),
        dot_tn(side_by_side(value_parts), normed[...]),
        dot_tn(context[...], grad_rows),
    ]
    store_terms(products, term)


def chunks_kernel(core, enc_term, enc_sent, dec_term, dec_sent, tiles):
    first = core[0] == 0
    rows, cols = enc_term.shape
    high = rows // 8
    for block in range(cols // 128):
        at = slice(block * 128, (block + 1) * 128)
        kept = jnp.where(first, enc_term[:, at], dec_term[:, at])
        received = jnp.where(first, enc_sent[:, at], dec_sent[:, at])
        total = kept.astype(jnp.float32) + received.astype(jnp.float32)
        part = total.reshape(high, 8, 128)
        tiles[block * high : (block + 1) * high] = part.astype(jnp.bfloat16)


def sum_copies_kernel(pieces, copies):
    summed = pieces[0].astype(jnp.float32)
    for index in range(1, pieces.shape[0]):
        summed = summed + pieces[index].astype(jnp.float32)
    block = summed.astype(jnp.bfloat16)
    for copy in range(copies.shape[0]):
        copies[copy] = block


def pick_copies_kernel(core, blocks, copies):
    block = jnp.where(core[0] == 0, blocks[0], blocks[1])
    for copy in range(copies.shape[0]):
        copies[copy] = block


def from_chunks_kernel(tiles, gradient):
    rows, cols = gradient.shape
    high = rows // 8
    for block in range(cols // 128):
        part = tiles[block * high : (block + 1) * high].astype(jnp.float32)
        gradient[:, block * 128 : (block + 1) * 128] = part.reshape(rows, 128)


def call(
    kernel, outs, scalars, arrays, blocks=None, scratch=(), kept=(), read=(), cost=None
):
    blocks = blocks or {}

    def spec(index, array):
        shape, at = blocks.get(index, (array.shape, (0,) * array.ndim))
        return pl.BlockSpec(shape, lambda i: at)

    def out(index, shape, dtype):
        return pltpu.HBM(shape, dtype) if index in kept else jax.ShapeDtypeStruct(shape, dtype)

    arrays = [
        pltpu.with_memory_space_constraint(array, pltpu.HBM) if index in read else array
        for index, array in enumerate(arrays)
    ]
    result = pl.pallas_call(
        kernel,
        grid=(1,),
        out_shape=[out(index, *what) for index, what in enumerate(outs)],
        in_specs=[pl.BlockSpec(memory_space=pltpu.SMEM) for _ in scalars]
        + [spec(index, array) for index, array in enumerate(arrays)],
        out_specs=[
            pl.BlockSpec(shape, functools.partial(lambda n, i: (0,) * n, len(shape)))
            for shape, _ in outs
        ],
        scratch_shapes=list(scratch),
        cost_estimate=cost,
        compiler_params=pltpu.CompilerParams(vmem_limit_bytes=48 << 20),
    )(*scalars, *arrays)
    return result[0] if len(outs) == 1 else result


def swap(block):
    return lax.ppermute(block, "segment", [(0, 1), (1, 0)])


def shards(
    frames, dec_states, out_grad, frame_lengths, token_lengths, weights, norm_gains, norm_biases
):
    bf16, f32 = jnp.bfloat16, jnp.float32
    core = lax.axis_index("segment")
    first = core == 0
    own = weights[0]
    shard_rows, features = frames.shape[1:]
    mp = lax.axis_size("mp")
    dp = lax.axis_size("dp")
    head_cols = own.shape[1]
    heads = head_cols // HS
    rows = shard_rows * mp
    count = dec_states.shape[1]
    near_groups = [[x * 8 + y * 2 + b for x in range(4) for b in range(2)] for y in range(4)]
    far_groups = [[x * 8 + y * 2 + b for y in range(4)] for x in range(4) for b in range(2)]
    near, far = len(near_groups[0]), len(far_groups[0])

    def exchange(blocks, axis="mp", groups=None):
        return lax.all_to_all(blocks, axis, 0, 0, axis_index_groups=groups)

    core_id = core.astype(jnp.int32).reshape(1)
    place = lax.axis_index("mp").astype(jnp.int32).reshape(1)

    copies = call(
        pick_copies_kernel,
        [((mp, shard_rows, features), bf16)],
        (core_id,),
        (frames,),
        kept=(0,),
        read=(0,),
    )
    copies, own = lax.optimization_barrier((copies, own))
    other = swap(own)
    shard = jnp.where(first, own[3], other[3])
    def passing(block, hop):
        up = [(i, (i + hop) % mp) for i in range(mp)]
        down = [(mp + i, mp + (i - hop) % mp) for i in range(mp)]
        return lax.ppermute(block, ("segment", "mp"), up + down)

    passed = [shard]
    for _ in range(mp // 2 - 1):
        passed.append(passing(passed[-1], 1))
    passed.append(passing(passed[-2], 2))
    swapped = [swap(block) for block in passed[1:-1]]
    out_shards = passed + swapped
    enc_full = exchange(copies).reshape(rows, features)

    token_queries, token_grads = call(
        token_kernel,
        [((count, head_cols), bf16)] * 2,
        (core_id,),
        (dec_states, out_grad, own, other, norm_gains, norm_biases),
        kept=(0, 1),
        read=(0, 1),
    )
    enc_full, token_queries, token_grads = lax.optimization_barrier(
        (enc_full, token_queries, token_grads)
    )
    weight_block = ((3, head_cols, features), (0, 0, 0))
    normed, queries, values, context, context_copies, probs = call(
        enc_forward_kernel,
        [
            ((rows, features), bf16),
            ((rows, head_cols), bf16),
            ((rows, head_cols), bf16),
            ((rows, head_cols), bf16),
            ((mp, rows, head_cols), bf16),
            ((heads, rows, rows), f32),
        ],
        (core_id, frame_lengths),
        (enc_full, own, other, norm_gains, norm_biases),
        {1: weight_block, 2: weight_block},
        kept=(0, 1, 2, 3, 4, 5),
        cost=pl.CostEstimate(flops=3_000_000_000, transcendentals=0, bytes_accessed=0),
    )
    context_full = exchange(context_copies)
    key_block = ((1, head_cols, features), (1, 0, 0))
    value_block = ((1, head_cols, features), (2, 0, 0))
    partial, states, state_normed, dec_key_grad, dec_value_grad, dec_context = call(
        dec_kernel,
        [
            ((rows, features), bf16),
            ((shard_rows, features), bf16),
            ((rows, features), bf16),
            ((rows, head_cols), bf16),
            ((rows, head_cols), bf16),
            ((count, head_cols), bf16),
        ],
        (core_id, place, frame_lengths, token_lengths),
        (
            enc_full, context_full, own, own, other, other, token_queries, token_grads,
            norm_gains, norm_biases, *out_shards,
        ),
        {2: key_block, 3: value_block, 4: key_block, 5: value_block},
        scratch=[pltpu.VMEM((rows, features), f32)],
        kept=(0, 1, 2, 3, 4, 5),
        read=(2, 3, 4, 5, 6, 7, 17),
    )
    whole = [((3 * head_cols, features), bf16)]
    dec_term = call(
        dec_terms_kernel,
        whole,
        (core_id,),
        (dec_key_grad, dec_value_grad, dec_context, state_normed, out_grad),
        kept=(0,),
        read=(0, 1, 2, 3, 4),
    )
    pieces, dec_term = lax.optimization_barrier(
        (exchange(partial.reshape(mp, shard_rows, features)), dec_term)
    )
    grads = call(
        norm_backward_kernel,
        [((mp, shard_rows, features), bf16)],
        (),
        (pieces, states, norm_gains),
        read=(1,),
    )
    grads_full = exchange(grads).reshape(rows, features)
    last_block = ((1, head_cols, features), (3, 0, 0))
    enc_term = call(
        enc_backward_kernel,
        whole,
        (core_id,),
        (grads_full, own, other, queries, values, probs, context, normed),
        {1: last_block, 2: last_block},
        read=(1, 2, 3, 4, 5, 6, 7),
    )
    dec_sent = lax.ppermute(dec_term, "segment", [(0, 1)])
    enc_sent = lax.ppermute(enc_term, "segment", [(1, 0)])
    size = 3 * head_cols * features // 1024
    each = size // near
    tiles = call(
        chunks_kernel,
        [((size, 8, 128), bf16)],
        (core_id,),
        (enc_term, enc_sent, dec_term, dec_sent),
        read=(2,),
    )
    parts = exchange(tiles.reshape(near, each, 8, 128), "dp", near_groups)
    parts = call(sum_copies_kernel, [((far, each, 8, 128), bf16)], (), (parts,))
    parts = exchange(parts, "dp", far_groups)
    parts = call(sum_copies_kernel, [((near, each, 8, 128), bf16)], (), (parts,))
    parts = exchange(parts, "dp", near_groups).reshape(size, 8, 128)
    gradient = call(from_chunks_kernel, [((3 * head_cols, features), f32)], (), (parts,))
    return gradient.reshape(1, 3, head_cols, features)


def solution(mesh):
    placed = (
        P(None, ("dp", "mp"), None),
        P(None, "dp", None),
        P(None, "dp", None),
        P(None, "dp", None),
        P(None, "dp", None),
        P("segment", None, "mp", None),
        P(),
        P(),
    )
    return jax.shard_map(
        shards,
        mesh=mesh,
        in_specs=placed,
        out_specs=P("segment", None, "mp", None),
        check_vma=False,
    )
```

```python
import functools
import math

import jax
import jax.numpy as jnp
from jax import lax
from jax.experimental import pallas as pl
from jax.experimental.pallas import tpu as pltpu
from jax.sharding import PartitionSpec as P

HS = 64
SCALING = 1.0 / math.sqrt(HS)
EPSILON = 1e-05
ROWS_DIMS = (((0,), (0,)), ((), ()))
FEAT_DIMS = (((1,), (1,)), ((), ()))


def dot_nn(a, b):
    return lax.dot_general(a, b, (((1,), (0,)), ((), ())), preferred_element_type=jnp.float32)


def dot_nt(a, b):
    return lax.dot_general(a, b, FEAT_DIMS, preferred_element_type=jnp.float32)


def dot_tn(a, b):
    return lax.dot_general(a, b, ROWS_DIMS, preferred_element_type=jnp.float32)


def row_stats(values):
    center = values - jnp.mean(values, axis=-1, keepdims=True)
    variance = jnp.mean(center * center, axis=-1, keepdims=True)
    return center, lax.rsqrt(variance + EPSILON)


def layer_norm(values, norm_gain, offset):
    center, inverse = row_stats(values.astype(jnp.float32))
    return (center * inverse * norm_gain + offset).astype(jnp.bfloat16)


def ids_along(lengths_ref, row, shape, axis):
    places = lax.broadcasted_iota(jnp.int32, shape, axis)
    bound = 0
    ids = jnp.zeros(shape, jnp.int32)
    for piece in range(lengths_ref.shape[2]):
        bound = bound + lengths_ref[row, 0, piece]
        ids = ids + (places >= bound).astype(jnp.int32)
    return ids


def softmax(queries, keys, allowed):
    scores = jnp.where(allowed, dot_nt(queries, keys) * SCALING, -1e30)
    raised = jnp.exp(scores - jnp.max(scores, axis=-1, keepdims=True))
    return raised / jnp.sum(raised, axis=-1, keepdims=True)


def scores_grad(probs, grad_context, values):
    grad_probs = dot_nt(grad_context, values)
    inner = jnp.sum(grad_probs * probs, axis=-1, keepdims=True)
    return (probs * (grad_probs - inner)).astype(jnp.bfloat16)


def side_by_side(parts):
    return jnp.concatenate(parts, axis=1).astype(jnp.bfloat16)


def enc_forward_kernel(
    core, lengths, x, own, other, gains, biases, normed, queries, values, context, copies, probs
):
    first = core[0] == 0
    rows = x.shape[0]
    normed_rows = layer_norm(x[...], gains[0:1, :], biases[0:1, :])
    normed[...] = normed_rows
    projected = []
    for kind in range(3):
        matrix = jnp.where(first, own[kind], other[kind])
        projected.append(dot_nt(normed_rows, matrix).astype(jnp.bfloat16))
    queries[...] = projected[0]
    values[...] = projected[2]
    allowed = ids_along(lengths, core[0], (rows, 1), 0) == ids_along(lengths, core[0], (1, rows), 1)
    parts = []
    for head in range(queries.shape[1] // HS):
        at = slice(head * HS, (head + 1) * HS)
        weights = softmax(projected[0][:, at], projected[1][:, at], allowed)
        probs[head] = weights
        parts.append(dot_nn(weights.astype(jnp.bfloat16), projected[2][:, at]))
    block = side_by_side(parts)
    context[...] = block
    for copy in range(copies.shape[0]):
        copies[copy] = block


def token_kernel(
    core, tokens, upstream, own, other, gains, biases, queries, grad_context, picked
):
    first = core[0] == 0
    own_tokens = jnp.where(first, tokens[0], tokens[1])
    normed_tokens = layer_norm(own_tokens, gains[1:2, :], biases[1:2, :])
    matrix = jnp.where(first, other[0], own[0])
    queries[...] = dot_nt(normed_tokens, matrix).astype(jnp.bfloat16)
    matrix = jnp.where(first, other[3], own[3])
    own_upstream = jnp.where(first, upstream[0], upstream[1])
    grad_context[...] = dot_nt(own_upstream, matrix).astype(jnp.bfloat16)
    for kind in (1, 2):
        picked[kind - 1] = jnp.where(first, other[kind], own[kind])


def dec_kernel(
    core, place, frame_lens, token_lens, x, context, weights, token_queries, token_grads, gains, biases,
    *refs,
):
    devices = context.shape[0]
    out_shards, refs = refs[:devices], refs[devices:]
    partial, states, normed, key_grad, value_grad, dec_context, scratch = refs
    first = core[0] == 0
    rows = x.shape[0]
    steps = devices // 2
    passed, swapped = out_shards[: steps + 1], out_shards[steps + 1 :]

    def context_at(back):
        return context[(place[0] + jnp.where(first, devices - back, back)) % devices]

    pairs = [(0, passed[0], steps, passed[steps])]
    for back in range(1, steps):
        pairs.append((back, passed[back], devices - back, swapped[back - 1]))
    summed = x[...].astype(jnp.float32)
    for back, shard, far_back, far_shard in pairs:
        left = jnp.concatenate([context_at(back), context_at(far_back)], axis=1)
        right = jnp.concatenate([shard[...], far_shard[...]], axis=0)
        summed = summed + dot_nn(left, right)
    scratch[...] = summed
    all_states = scratch[...].astype(jnp.bfloat16)
    shard = states.shape[0]
    start = pl.multiple_of(place[0] * shard, shard)
    states[...] = scratch[pl.ds(start, shard), :].astype(jnp.bfloat16)
    normed_rows = layer_norm(all_states, gains[2:3, :], biases[2:3, :])
    normed[...] = normed_rows
    matrix = [weights[0], weights[1]]
    queries = token_queries[...]
    grad_context = token_grads[...]
    keys = dot_nt(normed_rows, matrix[0]).astype(jnp.bfloat16)
    values = dot_nt(normed_rows, matrix[1]).astype(jnp.bfloat16)
    count = queries.shape[0]
    token_ids = ids_along(token_lens, core[0], (count, 1), 0)
    allowed = token_ids == ids_along(frame_lens, core[0], (1, rows), 1)
    key_parts, value_parts, context_parts = [], [], []
    for head in range(queries.shape[1] // HS):
        at = slice(head * HS, (head + 1) * HS)
        probs = softmax(queries[:, at], keys[:, at], allowed)
        rounded = probs.astype(jnp.bfloat16)
        context_parts.append(dot_nn(rounded, values[:, at]))
        grad_scores = scores_grad(probs, grad_context[:, at], values[:, at])
        key_parts.append(dot_tn(grad_scores, queries[:, at]) * SCALING)
        value_parts.append(dot_tn(rounded, grad_context[:, at]))
    key_block, value_block = side_by_side(key_parts), side_by_side(value_parts)
    key_grad[...] = key_block
    value_grad[...] = value_block
    dec_context[...] = side_by_side(context_parts)
    partial[...] = (dot_nn(key_block, matrix[0]) + dot_nn(value_block, matrix[1])).astype(
        jnp.bfloat16
    )


def store_terms(products, term):
    high = products[0].shape[0]
    for index, product in enumerate(products):
        term[index * high : (index + 1) * high, :] = product.astype(jnp.bfloat16)


def dec_terms_kernel(core, key_grad, value_grad, context, normed, upstream, term):
    products = [
        dot_tn(key_grad[...], normed[...]),
        dot_tn(value_grad[...], normed[...]),
        dot_tn(context[...], jnp.where(core[0] == 0, upstream[0], upstream[1])),
    ]
    store_terms(products, term)


def norm_backward_kernel(pieces, states, gains, grads):
    summed = pieces[0].astype(jnp.float32)
    for index in range(1, pieces.shape[0]):
        summed = summed + pieces[index].astype(jnp.float32)
    center, inverse = row_stats(states[...].astype(jnp.float32))
    normed = center * inverse
    scaled = summed * gains[2:3, :]
    result = inverse * (
        scaled
        - jnp.mean(scaled, axis=-1, keepdims=True)
        - normed * jnp.mean(scaled * normed, axis=-1, keepdims=True)
    )
    block = result.astype(jnp.bfloat16)
    for copy in range(grads.shape[0]):
        grads[copy] = block


def enc_backward_kernel(
    grads, out_shard, queries, values, probs, context, normed, term
):
    grad_rows = grads[...]
    att_grad = dot_nt(grad_rows, out_shard[...]).astype(jnp.bfloat16)
    query_rows, value_rows = queries[...], values[...]
    key_parts, value_parts = [], []
    for head in range(query_rows.shape[1] // HS):
        at = slice(head * HS, (head + 1) * HS)
        weights = probs[head]
        grad_scores = scores_grad(weights, att_grad[:, at], value_rows[:, at])
        key_parts.append(dot_tn(grad_scores, query_rows[:, at]) * SCALING)
        value_parts.append(dot_tn(weights.astype(jnp.bfloat16), att_grad[:, at]))
    products = [
        dot_tn(side_by_side(key_parts), normed[...]),
        dot_tn(side_by_side(value_parts), normed[...]),
        dot_tn(context[...], grad_rows),
    ]
    store_terms(products, term)


def chunks_kernel(core, enc_term, enc_sent, dec_term, dec_sent, tiles):
    first = core[0] == 0
    rows, cols = enc_term.shape
    high = rows // 8
    for block in range(cols // 128):
        at = slice(block * 128, (block + 1) * 128)
        kept = jnp.where(first, enc_term[:, at], dec_term[:, at])
        received = jnp.where(first, enc_sent[:, at], dec_sent[:, at])
        total = kept.astype(jnp.float32) + received.astype(jnp.float32)
        part = total.reshape(high, 8, 128)
        tiles[block * high : (block + 1) * high] = part.astype(jnp.bfloat16)


def sum_copies_kernel(pieces, copies):
    summed = pieces[0].astype(jnp.float32)
    for index in range(1, pieces.shape[0]):
        summed = summed + pieces[index].astype(jnp.float32)
    block = summed.astype(jnp.bfloat16)
    for copy in range(copies.shape[0]):
        copies[copy] = block


def pick_copies_kernel(core, blocks, copies):
    block = jnp.where(core[0] == 0, blocks[0], blocks[1])
    for copy in range(copies.shape[0]):
        copies[copy] = block


def from_chunks_kernel(tiles, gradient):
    rows, cols = gradient.shape
    high = rows // 8
    for block in range(cols // 128):
        part = tiles[block * high : (block + 1) * high].astype(jnp.float32)
        gradient[:, block * 128 : (block + 1) * 128] = part.reshape(rows, 128)


def call(
    kernel, outs, scalars, arrays, blocks=None, scratch=(), kept=(), read=(), cost=None
):
    blocks = blocks or {}

    def spec(index, array):
        shape, at = blocks.get(index, (array.shape, (0,) * array.ndim))
        return pl.BlockSpec(shape, lambda i: at)

    def out(index, shape, dtype):
        return pltpu.HBM(shape, dtype) if index in kept else jax.ShapeDtypeStruct(shape, dtype)

    arrays = [
        pltpu.with_memory_space_constraint(array, pltpu.HBM) if index in read else array
        for index, array in enumerate(arrays)
    ]
    result = pl.pallas_call(
        kernel,
        grid=(1,),
        out_shape=[out(index, *what) for index, what in enumerate(outs)],
        in_specs=[pl.BlockSpec(memory_space=pltpu.SMEM) for _ in scalars]
        + [spec(index, array) for index, array in enumerate(arrays)],
        out_specs=[
            pl.BlockSpec(shape, functools.partial(lambda n, i: (0,) * n, len(shape)))
            for shape, _ in outs
        ],
        scratch_shapes=list(scratch),
        cost_estimate=cost,
        compiler_params=pltpu.CompilerParams(vmem_limit_bytes=48 << 20),
    )(*scalars, *arrays)
    return result[0] if len(outs) == 1 else result


def swap(block):
    return lax.ppermute(block, "segment", [(0, 1), (1, 0)])


def shards(
    frames, dec_states, out_grad, frame_lengths, token_lengths, weights, norm_gains, norm_biases
):
    bf16, f32 = jnp.bfloat16, jnp.float32
    core = lax.axis_index("segment")
    first = core == 0
    own = weights[0]
    shard_rows, features = frames.shape[1:]
    mp = lax.axis_size("mp")
    dp = lax.axis_size("dp")
    head_cols = own.shape[1]
    heads = head_cols // HS
    rows = shard_rows * mp
    count = dec_states.shape[1]
    near_groups = [[x * 8 + y * 2 + b for x in range(4) for b in range(2)] for y in range(4)]
    far_groups = [[x * 8 + y * 2 + b for y in range(4)] for x in range(4) for b in range(2)]
    near, far = len(near_groups[0]), len(far_groups[0])

    def exchange(blocks, axis="mp", groups=None):
        return lax.all_to_all(blocks, axis, 0, 0, axis_index_groups=groups)

    core_id = core.astype(jnp.int32).reshape(1)
    place = lax.axis_index("mp").astype(jnp.int32).reshape(1)

    copies = call(
        pick_copies_kernel,
        [((mp, shard_rows, features), bf16)],
        (core_id,),
        (frames,),
        kept=(0,),
        read=(0,),
    )
    copies, own = lax.optimization_barrier((copies, own))
    other = swap(own)
    shard = jnp.where(first, own[3], other[3])
    def passing(block, hop):
        up = [(i, (i + hop) % mp) for i in range(mp)]
        down = [(mp + i, mp + (i - hop) % mp) for i in range(mp)]
        return lax.ppermute(block, ("segment", "mp"), up + down)

    passed = [shard]
    for _ in range(mp // 2 - 1):
        passed.append(passing(passed[-1], 1))
    passed.append(passing(passed[-2], 2))
    swapped = [swap(block) for block in passed[1:-1]]
    out_shards = passed + swapped
    enc_full = exchange(copies).reshape(rows, features)

    token_queries, token_grads, dec_weights = call(
        token_kernel,
        [((count, head_cols), bf16)] * 2 + [((2, head_cols, features), bf16)],
        (core_id,),
        (dec_states, out_grad, own, other, norm_gains, norm_biases),
        kept=(0, 1, 2),
        read=(0, 1),
    )
    enc_full, token_queries, token_grads, dec_weights = lax.optimization_barrier(
        (enc_full, token_queries, token_grads, dec_weights)
    )
    weight_block = ((3, head_cols, features), (0, 0, 0))
    normed, queries, values, context, context_copies, probs = call(
        enc_forward_kernel,
        [
            ((rows, features), bf16),
            ((rows, head_cols), bf16),
            ((rows, head_cols), bf16),
            ((rows, head_cols), bf16),
            ((mp, rows, head_cols), bf16),
            ((heads, rows, rows), f32),
        ],
        (core_id, frame_lengths),
        (enc_full, own, other, norm_gains, norm_biases),
        {1: weight_block, 2: weight_block},
        kept=(0, 1, 2, 3, 4, 5),
        cost=pl.CostEstimate(flops=3_000_000_000, transcendentals=0, bytes_accessed=0),
    )
    context_full = exchange(context_copies)
    partial, states, state_normed, dec_key_grad, dec_value_grad, dec_context = call(
        dec_kernel,
        [
            ((rows, features), bf16),
            ((shard_rows, features), bf16),
            ((rows, features), bf16),
            ((rows, head_cols), bf16),
            ((rows, head_cols), bf16),
            ((count, head_cols), bf16),
        ],
        (core_id, place, frame_lengths, token_lengths),
        (
            enc_full, context_full, dec_weights, token_queries, token_grads,
            norm_gains, norm_biases, *out_shards,
        ),
        scratch=[pltpu.VMEM((rows, features), f32)],
        kept=(2, 3, 4, 5),
        read=(2, 3, 4, 14),
    )
    pieces = exchange(partial.reshape(mp, shard_rows, features))
    whole = [((3 * head_cols, features), bf16)]
    dec_term = call(
        dec_terms_kernel,
        whole,
        (core_id,),
        (dec_key_grad, dec_value_grad, dec_context, state_normed, out_grad),
        kept=(0,),
        read=(0, 1, 2, 3, 4),
    )
    grads = call(
        norm_backward_kernel,
        [((mp, shard_rows, features), bf16)],
        (),
        (pieces, states, norm_gains),
    )
    grads_full = exchange(grads).reshape(rows, features)
    enc_term = call(
        enc_backward_kernel,
        whole,
        (),
        (grads_full, shard, queries, values, probs, context, normed),
        read=(1, 2, 3, 4, 5, 6),
    )
    dec_sent = lax.ppermute(dec_term, "segment", [(0, 1)])
    enc_sent = lax.ppermute(enc_term, "segment", [(1, 0)])
    size = 3 * head_cols * features // 1024
    each = size // near
    tiles = call(
        chunks_kernel,
        [((size, 8, 128), bf16)],
        (core_id,),
        (enc_term, enc_sent, dec_term, dec_sent),
        read=(2,),
    )
    parts = exchange(tiles.reshape(near, each, 8, 128), "dp", near_groups)
    parts = call(sum_copies_kernel, [((far, each, 8, 128), bf16)], (), (parts,))
    parts = exchange(parts, "dp", far_groups)
    parts = call(sum_copies_kernel, [((near, each, 8, 128), bf16)], (), (parts,))
    parts = exchange(parts, "dp", near_groups).reshape(size, 8, 128)
    gradient = call(from_chunks_kernel, [((3 * head_cols, features), f32)], (), (parts,))
    return gradient.reshape(1, 3, head_cols, features)


def solution(mesh):
    placed = (
        P(None, ("dp", "mp"), None),
        P(None, "dp", None),
        P(None, "dp", None),
        P(None, "dp", None),
        P(None, "dp", None),
        P("segment", None, "mp", None),
        P(),
        P(),
    )
    return jax.shard_map(
        shards,
        mesh=mesh,
        in_specs=placed,
        out_specs=P("segment", None, "mp", None),
        check_vma=False,
    )
```

```python
import functools
import math

import jax
import jax.numpy as jnp
from jax import lax
from jax.experimental import pallas as pl
from jax.experimental.pallas import tpu as pltpu
from jax.sharding import PartitionSpec as P

HS = 64
SCALING = 1.0 / math.sqrt(HS)
EPSILON = 1e-05
ROWS_DIMS = (((0,), (0,)), ((), ()))
FEAT_DIMS = (((1,), (1,)), ((), ()))


def dot_nn(a, b):
    return lax.dot_general(a, b, (((1,), (0,)), ((), ())), preferred_element_type=jnp.float32)


def dot_nt(a, b):
    return lax.dot_general(a, b, FEAT_DIMS, preferred_element_type=jnp.float32)


def dot_tn(a, b):
    return lax.dot_general(a, b, ROWS_DIMS, preferred_element_type=jnp.float32)


def row_stats(values):
    center = values - jnp.mean(values, axis=-1, keepdims=True)
    variance = jnp.mean(center * center, axis=-1, keepdims=True)
    return center, lax.rsqrt(variance + EPSILON)


def layer_norm(values, norm_gain, offset):
    center, inverse = row_stats(values.astype(jnp.float32))
    return (center * inverse * norm_gain + offset).astype(jnp.bfloat16)


def ids_along(lengths_ref, row, shape, axis):
    places = lax.broadcasted_iota(jnp.int32, shape, axis)
    bound = 0
    ids = jnp.zeros(shape, jnp.int32)
    for piece in range(lengths_ref.shape[2]):
        bound = bound + lengths_ref[row, 0, piece]
        ids = ids + (places >= bound).astype(jnp.int32)
    return ids


def softmax(queries, keys, allowed):
    scores = jnp.where(allowed, dot_nt(queries, keys) * SCALING, -1e30)
    raised = jnp.exp(scores - jnp.max(scores, axis=-1, keepdims=True))
    return raised / jnp.sum(raised, axis=-1, keepdims=True)


def scores_grad(probs, grad_context, values):
    grad_probs = dot_nt(grad_context, values)
    inner = jnp.sum(grad_probs * probs, axis=-1, keepdims=True)
    return (probs * (grad_probs - inner)).astype(jnp.bfloat16)


def side_by_side(parts):
    return jnp.concatenate(parts, axis=1).astype(jnp.bfloat16)


def enc_forward_kernel(
    core, lengths, x, own, other, gains, biases, normed, queries, values, context, copies, probs
):
    first = core[0] == 0
    rows = x.shape[0]
    normed_rows = layer_norm(x[...], gains[0:1, :], biases[0:1, :])
    normed[...] = normed_rows
    projected = []
    for kind in range(3):
        matrix = jnp.where(first, own[kind], other[kind])
        projected.append(dot_nt(normed_rows, matrix).astype(jnp.bfloat16))
    queries[...] = projected[0]
    values[...] = projected[2]
    allowed = ids_along(lengths, core[0], (rows, 1), 0) == ids_along(lengths, core[0], (1, rows), 1)
    parts = []
    for head in range(queries.shape[1] // HS):
        at = slice(head * HS, (head + 1) * HS)
        weights = softmax(projected[0][:, at], projected[1][:, at], allowed)
        probs[head] = weights
        parts.append(dot_nn(weights.astype(jnp.bfloat16), projected[2][:, at]))
    block = side_by_side(parts)
    context[...] = block
    for copy in range(copies.shape[0]):
        copies[copy] = block


def token_kernel(
    core, tokens, upstream, own, other, gains, biases, queries, grad_context, picked
):
    first = core[0] == 0
    own_tokens = jnp.where(first, tokens[0], tokens[1])
    normed_tokens = layer_norm(own_tokens, gains[1:2, :], biases[1:2, :])
    matrix = jnp.where(first, other[0], own[0])
    queries[...] = dot_nt(normed_tokens, matrix).astype(jnp.bfloat16)
    matrix = jnp.where(first, other[3], own[3])
    own_upstream = jnp.where(first, upstream[0], upstream[1])
    grad_context[...] = dot_nt(own_upstream, matrix).astype(jnp.bfloat16)
    for kind in (1, 2):
        picked[kind - 1] = jnp.where(first, other[kind], own[kind])


def dec_kernel(
    core, place, frame_lens, token_lens, x, context, weights, token_queries, token_grads, gains, biases,
    *refs,
):
    devices = context.shape[0]
    out_shards, refs = refs[:devices], refs[devices:]
    partial, states, normed, key_grad, value_grad, dec_context, scratch = refs
    first = core[0] == 0
    rows = x.shape[0]
    steps = devices // 2
    passed, swapped = out_shards[: steps + 1], out_shards[steps + 1 :]

    def context_at(back):
        return context[(place[0] + jnp.where(first, devices - back, back)) % devices]

    pairs = [(0, passed[0], steps, passed[steps])]
    for back in range(1, steps):
        pairs.append((back, passed[back], devices - back, swapped[back - 1]))
    summed = x[...].astype(jnp.float32)
    for back, shard, far_back, far_shard in pairs:
        left = jnp.concatenate([context_at(back), context_at(far_back)], axis=1)
        right = jnp.concatenate([shard[...], far_shard[...]], axis=0)
        summed = summed + dot_nn(left, right)
    scratch[...] = summed
    all_states = scratch[...].astype(jnp.bfloat16)
    shard = states.shape[0]
    start = pl.multiple_of(place[0] * shard, shard)
    states[...] = scratch[pl.ds(start, shard), :].astype(jnp.bfloat16)
    normed_rows = layer_norm(all_states, gains[2:3, :], biases[2:3, :])
    normed[...] = normed_rows
    matrix = [weights[0], weights[1]]
    queries = token_queries[...]
    grad_context = token_grads[...]
    keys = dot_nt(normed_rows, matrix[0]).astype(jnp.bfloat16)
    values = dot_nt(normed_rows, matrix[1]).astype(jnp.bfloat16)
    count = queries.shape[0]
    token_ids = ids_along(token_lens, core[0], (count, 1), 0)
    allowed = token_ids == ids_along(frame_lens, core[0], (1, rows), 1)
    key_parts, value_parts, context_parts = [], [], []
    for head in range(queries.shape[1] // HS):
        at = slice(head * HS, (head + 1) * HS)
        probs = softmax(queries[:, at], keys[:, at], allowed)
        rounded = probs.astype(jnp.bfloat16)
        context_parts.append(dot_nn(rounded, values[:, at]))
        grad_scores = scores_grad(probs, grad_context[:, at], values[:, at])
        key_parts.append(dot_tn(grad_scores, queries[:, at]) * SCALING)
        value_parts.append(dot_tn(rounded, grad_context[:, at]))
    key_block, value_block = side_by_side(key_parts), side_by_side(value_parts)
    key_grad[...] = key_block
    value_grad[...] = value_block
    dec_context[...] = side_by_side(context_parts)
    partial[...] = (dot_nn(key_block, matrix[0]) + dot_nn(value_block, matrix[1])).astype(
        jnp.bfloat16
    )


def store_terms(products, term):
    high = products[0].shape[0]
    for index, product in enumerate(products):
        term[index * high : (index + 1) * high, :] = product.astype(jnp.bfloat16)


def dec_terms_kernel(core, key_grad, value_grad, context, normed, upstream, term):
    products = [
        dot_tn(key_grad[...], normed[...]),
        dot_tn(value_grad[...], normed[...]),
        dot_tn(context[...], jnp.where(core[0] == 0, upstream[0], upstream[1])),
    ]
    store_terms(products, term)


def norm_backward_kernel(pieces, states, gains, grads):
    summed = pieces[0].astype(jnp.float32)
    for index in range(1, pieces.shape[0]):
        summed = summed + pieces[index].astype(jnp.float32)
    center, inverse = row_stats(states[...].astype(jnp.float32))
    normed = center * inverse
    scaled = summed * gains[2:3, :]
    result = inverse * (
        scaled
        - jnp.mean(scaled, axis=-1, keepdims=True)
        - normed * jnp.mean(scaled * normed, axis=-1, keepdims=True)
    )
    block = result.astype(jnp.bfloat16)
    for copy in range(grads.shape[0]):
        grads[copy] = block


def enc_backward_kernel(
    grads, out_shard, queries, values, probs, context, normed, term
):
    grad_rows = grads[...]
    att_grad = dot_nt(grad_rows, out_shard[...]).astype(jnp.bfloat16)
    query_rows, value_rows = queries[...], values[...]
    key_parts, value_parts = [], []
    for head in range(query_rows.shape[1] // HS):
        at = slice(head * HS, (head + 1) * HS)
        weights = probs[head]
        grad_scores = scores_grad(weights, att_grad[:, at], value_rows[:, at])
        key_parts.append(dot_tn(grad_scores, query_rows[:, at]) * SCALING)
        value_parts.append(dot_tn(weights.astype(jnp.bfloat16), att_grad[:, at]))
    products = [
        dot_tn(side_by_side(key_parts), normed[...]),
        dot_tn(side_by_side(value_parts), normed[...]),
        dot_tn(context[...], grad_rows),
    ]
    store_terms(products, term)


def chunks_kernel(core, enc_term, enc_sent, dec_term, dec_sent, tiles):
    first = core[0] == 0
    rows, cols = enc_term.shape
    high = rows // 8
    for block in range(cols // 128):
        at = slice(block * 128, (block + 1) * 128)
        kept = jnp.where(first, enc_term[:, at], dec_term[:, at])
        received = jnp.where(first, enc_sent[:, at], dec_sent[:, at])
        total = kept.astype(jnp.float32) + received.astype(jnp.float32)
        part = total.reshape(high, 8, 128)
        tiles[block * high : (block + 1) * high] = part.astype(jnp.bfloat16)


def sum_copies_kernel(pieces, copies):
    summed = pieces[0].astype(jnp.float32)
    for index in range(1, pieces.shape[0]):
        summed = summed + pieces[index].astype(jnp.float32)
    block = summed.astype(jnp.bfloat16)
    for copy in range(copies.shape[0]):
        copies[copy] = block


def pick_copies_kernel(core, blocks, copies):
    block = jnp.where(core[0] == 0, blocks[0], blocks[1])
    for copy in range(copies.shape[0]):
        copies[copy] = block


def from_chunks_kernel(tiles, gradient):
    rows, cols = gradient.shape
    high = rows // 8
    for block in range(cols // 128):
        part = tiles[block * high : (block + 1) * high].astype(jnp.float32)
        gradient[:, block * 128 : (block + 1) * 128] = part.reshape(rows, 128)


def call(
    kernel, outs, scalars, arrays, blocks=None, scratch=(), kept=(), read=(), cost=None
):
    blocks = blocks or {}

    def spec(index, array):
        shape, at = blocks.get(index, (array.shape, (0,) * array.ndim))
        return pl.BlockSpec(shape, lambda i: at)

    def out(index, shape, dtype):
        return pltpu.HBM(shape, dtype) if index in kept else jax.ShapeDtypeStruct(shape, dtype)

    arrays = [
        pltpu.with_memory_space_constraint(array, pltpu.HBM) if index in read else array
        for index, array in enumerate(arrays)
    ]
    result = pl.pallas_call(
        kernel,
        grid=(1,),
        out_shape=[out(index, *what) for index, what in enumerate(outs)],
        in_specs=[pl.BlockSpec(memory_space=pltpu.SMEM) for _ in scalars]
        + [spec(index, array) for index, array in enumerate(arrays)],
        out_specs=[
            pl.BlockSpec(shape, functools.partial(lambda n, i: (0,) * n, len(shape)))
            for shape, _ in outs
        ],
        scratch_shapes=list(scratch),
        cost_estimate=cost,
        compiler_params=pltpu.CompilerParams(vmem_limit_bytes=48 << 20),
    )(*scalars, *arrays)
    return result[0] if len(outs) == 1 else result


def swap(block):
    return lax.ppermute(block, "segment", [(0, 1), (1, 0)])


def shards(
    frames, dec_states, out_grad, frame_lengths, token_lengths, weights, norm_gains, norm_biases
):
    bf16, f32 = jnp.bfloat16, jnp.float32
    core = lax.axis_index("segment")
    first = core == 0
    own = weights[0]
    shard_rows, features = frames.shape[1:]
    mp = lax.axis_size("mp")
    dp = lax.axis_size("dp")
    head_cols = own.shape[1]
    heads = head_cols // HS
    rows = shard_rows * mp
    count = dec_states.shape[1]
    near_groups = [[x * 8 + y * 2 + b for x in range(4) for b in range(2)] for y in range(4)]
    far_groups = [[x * 8 + y * 2 + b for y in range(4)] for x in range(4) for b in range(2)]
    near, far = len(near_groups[0]), len(far_groups[0])

    def exchange(blocks, axis="mp", groups=None):
        return lax.all_to_all(blocks, axis, 0, 0, axis_index_groups=groups)

    core_id = core.astype(jnp.int32).reshape(1)
    place = lax.axis_index("mp").astype(jnp.int32).reshape(1)

    copies = call(
        pick_copies_kernel,
        [((mp, shard_rows, features), bf16)],
        (core_id,),
        (frames,),
        kept=(0,),
        read=(0,),
    )
    copies, own = lax.optimization_barrier((copies, own))
    other = swap(own)
    shard = jnp.where(first, own[3], other[3])
    def passing(block, hop):
        up = [(i, (i + hop) % mp) for i in range(mp)]
        down = [(mp + i, mp + (i - hop) % mp) for i in range(mp)]
        return lax.ppermute(block, ("segment", "mp"), up + down)

    passed = [shard]
    for _ in range(mp // 2 - 1):
        passed.append(passing(passed[-1], 1))
    passed.append(passing(passed[-2], 2))
    swapped = [swap(block) for block in passed[1:-1]]
    out_shards = passed + swapped
    enc_full = exchange(copies).reshape(rows, features)

    token_queries, token_grads, dec_weights = call(
        token_kernel,
        [((count, head_cols), bf16)] * 2 + [((2, head_cols, features), bf16)],
        (core_id,),
        (dec_states, out_grad, own, other, norm_gains, norm_biases),
        kept=(0, 1, 2),
        read=(0, 1),
    )
    enc_full, token_queries, token_grads, dec_weights = lax.optimization_barrier(
        (enc_full, token_queries, token_grads, dec_weights)
    )
    weight_block = ((3, head_cols, features), (0, 0, 0))
    normed, queries, values, context, context_copies, probs = call(
        enc_forward_kernel,
        [
            ((rows, features), bf16),
            ((rows, head_cols), bf16),
            ((rows, head_cols), bf16),
            ((rows, head_cols), bf16),
            ((mp, rows, head_cols), bf16),
            ((heads, rows, rows), f32),
        ],
        (core_id, frame_lengths),
        (enc_full, own, other, norm_gains, norm_biases),
        {1: weight_block, 2: weight_block},
        kept=(0, 1, 2, 3, 4, 5),
        cost=pl.CostEstimate(flops=3_000_000_000, transcendentals=0, bytes_accessed=0),
    )
    context_full = exchange(context_copies)
    partial, states, state_normed, dec_key_grad, dec_value_grad, dec_context = call(
        dec_kernel,
        [
            ((rows, features), bf16),
            ((shard_rows, features), bf16),
            ((rows, features), bf16),
            ((rows, head_cols), bf16),
            ((rows, head_cols), bf16),
            ((count, head_cols), bf16),
        ],
        (core_id, place, frame_lengths, token_lengths),
        (
            enc_full, context_full, dec_weights, token_queries, token_grads,
            norm_gains, norm_biases, *out_shards,
        ),
        scratch=[pltpu.VMEM((rows, features), f32)],
        kept=(2, 3, 4, 5),
        read=(14,),
    )
    pieces = exchange(partial.reshape(mp, shard_rows, features))
    whole = [((3 * head_cols, features), bf16)]
    dec_term = call(
        dec_terms_kernel,
        whole,
        (core_id,),
        (dec_key_grad, dec_value_grad, dec_context, state_normed, out_grad),
        kept=(0,),
        read=(0, 1, 2, 3, 4),
    )
    grads = call(
        norm_backward_kernel,
        [((mp, shard_rows, features), bf16)],
        (),
        (pieces, states, norm_gains),
    )
    grads_full = exchange(grads).reshape(rows, features)
    enc_term = call(
        enc_backward_kernel,
        whole,
        (),
        (grads_full, shard, queries, values, probs, context, normed),
    )
    dec_sent = lax.ppermute(dec_term, "segment", [(0, 1)])
    enc_sent = lax.ppermute(enc_term, "segment", [(1, 0)])
    size = 3 * head_cols * features // 1024
    each = size // near
    tiles = call(
        chunks_kernel,
        [((size, 8, 128), bf16)],
        (core_id,),
        (enc_term, enc_sent, dec_term, dec_sent),
        read=(2,),
    )
    parts = exchange(tiles.reshape(near, each, 8, 128), "dp", near_groups)
    parts = call(sum_copies_kernel, [((far, each, 8, 128), bf16)], (), (parts,))
    parts = exchange(parts, "dp", far_groups)
    parts = call(sum_copies_kernel, [((near, each, 8, 128), bf16)], (), (parts,))
    parts = exchange(parts, "dp", near_groups).reshape(size, 8, 128)
    gradient = call(from_chunks_kernel, [((3 * head_cols, features), f32)], (), (parts,))
    return gradient.reshape(1, 3, head_cols, features)


def solution(mesh):
    placed = (
        P(None, ("dp", "mp"), None),
        P(None, "dp", None),
        P(None, "dp", None),
        P(None, "dp", None),
        P(None, "dp", None),
        P("segment", None, "mp", None),
        P(),
        P(),
    )
    return jax.shard_map(
        shards,
        mesh=mesh,
        in_specs=placed,
        out_specs=P("segment", None, "mp", None),
        check_vma=False,
    )
```

```python
import functools
import math

import jax
import jax.numpy as jnp
from jax import lax
from jax.experimental import pallas as pl
from jax.experimental.pallas import tpu as pltpu
from jax.sharding import PartitionSpec as P

HS = 64
SCALING = 1.0 / math.sqrt(HS)
EPSILON = 1e-05
ROWS_DIMS = (((0,), (0,)), ((), ()))
FEAT_DIMS = (((1,), (1,)), ((), ()))


def dot_nn(a, b):
    return lax.dot_general(a, b, (((1,), (0,)), ((), ())), preferred_element_type=jnp.float32)


def dot_nt(a, b):
    return lax.dot_general(a, b, FEAT_DIMS, preferred_element_type=jnp.float32)


def dot_tn(a, b):
    return lax.dot_general(a, b, ROWS_DIMS, preferred_element_type=jnp.float32)


def row_stats(values):
    center = values - jnp.mean(values, axis=-1, keepdims=True)
    variance = jnp.mean(center * center, axis=-1, keepdims=True)
    return center, lax.rsqrt(variance + EPSILON)


def layer_norm(values, norm_gain, offset):
    center, inverse = row_stats(values.astype(jnp.float32))
    return (center * inverse * norm_gain + offset).astype(jnp.bfloat16)


def ids_along(lengths_ref, row, shape, axis):
    places = lax.broadcasted_iota(jnp.int32, shape, axis)
    bound = 0
    ids = jnp.zeros(shape, jnp.int32)
    for piece in range(lengths_ref.shape[2]):
        bound = bound + lengths_ref[row, 0, piece]
        ids = ids + (places >= bound).astype(jnp.int32)
    return ids


def softmax(queries, keys, allowed):
    scores = jnp.where(allowed, dot_nt(queries, keys) * SCALING, -1e30)
    raised = jnp.exp(scores - jnp.max(scores, axis=-1, keepdims=True))
    return raised / jnp.sum(raised, axis=-1, keepdims=True)


def scores_grad(probs, grad_context, values):
    grad_probs = dot_nt(grad_context, values)
    inner = jnp.sum(grad_probs * probs, axis=-1, keepdims=True)
    return (probs * (grad_probs - inner)).astype(jnp.bfloat16)


def side_by_side(parts):
    return jnp.concatenate(parts, axis=1).astype(jnp.bfloat16)


def enc_forward_kernel(
    core, lengths, x, own, other, gains, biases, normed, queries, values, context, copies, probs
):
    first = core[0] == 0
    rows = x.shape[0]
    normed_rows = layer_norm(x[...], gains[0:1, :], biases[0:1, :])
    normed[...] = normed_rows
    projected = []
    for kind in range(3):
        matrix = jnp.where(first, own[kind], other[kind])
        projected.append(dot_nt(normed_rows, matrix).astype(jnp.bfloat16))
    queries[...] = projected[0]
    values[...] = projected[2]
    allowed = ids_along(lengths, core[0], (rows, 1), 0) == ids_along(lengths, core[0], (1, rows), 1)
    parts = []
    for head in range(queries.shape[1] // HS):
        at = slice(head * HS, (head + 1) * HS)
        weights = softmax(projected[0][:, at], projected[1][:, at], allowed)
        probs[head] = weights
        parts.append(dot_nn(weights.astype(jnp.bfloat16), projected[2][:, at]))
    block = side_by_side(parts)
    context[...] = block
    for copy in range(copies.shape[0]):
        copies[copy] = block


def token_kernel(
    core, tokens, upstream, own, other, gains, biases, queries, grad_context, picked
):
    first = core[0] == 0
    own_tokens = jnp.where(first, tokens[0], tokens[1])
    normed_tokens = layer_norm(own_tokens, gains[1:2, :], biases[1:2, :])
    matrix = jnp.where(first, other[0], own[0])
    queries[...] = dot_nt(normed_tokens, matrix).astype(jnp.bfloat16)
    matrix = jnp.where(first, other[3], own[3])
    own_upstream = jnp.where(first, upstream[0], upstream[1])
    grad_context[...] = dot_nt(own_upstream, matrix).astype(jnp.bfloat16)
    for kind in (1, 2):
        picked[kind - 1] = jnp.where(first, other[kind], own[kind])


def shard_products(core, place, context, pairs):
    first = core[0] == 0
    devices = context.shape[0]

    def context_at(back):
        return context[(place[0] + jnp.where(first, devices - back, back)) % devices]

    summed = 0.0
    for back, shard, far_back, far_shard in pairs:
        left = jnp.concatenate([context_at(back), context_at(far_back)], axis=1)
        right = jnp.concatenate([shard[...], far_shard[...]], axis=0)
        summed = summed + dot_nn(left, right)
    return summed


def half_states_kernel(core, place, x, context, *refs):
    states, shards_in = refs[-1], refs[:-1]
    devices = context.shape[0]
    count = len(shards_in) // 2
    pairs = [
        (back + 1, shards_in[back], devices - 1 - back, shards_in[count + back])
        for back in range(count)
    ]
    states[...] = x[...].astype(jnp.float32) + shard_products(core, place, context, pairs)


def dec_kernel(
    core, place, frame_lens, token_lens, half_states, context, weights, token_queries, token_grads,
    gains, biases, *refs,
):
    near, near_swapped, own_shard, far, partial, states, normed = refs[:7]
    key_grad, value_grad, dec_context, scratch = refs[7:]
    rows = half_states.shape[0]
    steps = context.shape[0] // 2
    pairs = [(0, own_shard, steps, far), (steps - 1, near, steps + 1, near_swapped)]
    summed = half_states[...] + shard_products(core, place, context, pairs)
    scratch[...] = summed
    all_states = scratch[...].astype(jnp.bfloat16)
    shard = states.shape[0]
    start = pl.multiple_of(place[0] * shard, shard)
    states[...] = scratch[pl.ds(start, shard), :].astype(jnp.bfloat16)
    normed_rows = layer_norm(all_states, gains[2:3, :], biases[2:3, :])
    normed[...] = normed_rows
    matrix = [weights[0], weights[1]]
    queries = token_queries[...]
    grad_context = token_grads[...]
    keys = dot_nt(normed_rows, matrix[0]).astype(jnp.bfloat16)
    values = dot_nt(normed_rows, matrix[1]).astype(jnp.bfloat16)
    count = queries.shape[0]
    token_ids = ids_along(token_lens, core[0], (count, 1), 0)
    allowed = token_ids == ids_along(frame_lens, core[0], (1, rows), 1)
    key_parts, value_parts, context_parts = [], [], []
    for head in range(queries.shape[1] // HS):
        at = slice(head * HS, (head + 1) * HS)
        probs = softmax(queries[:, at], keys[:, at], allowed)
        rounded = probs.astype(jnp.bfloat16)
        context_parts.append(dot_nn(rounded, values[:, at]))
        grad_scores = scores_grad(probs, grad_context[:, at], values[:, at])
        key_parts.append(dot_tn(grad_scores, queries[:, at]) * SCALING)
        value_parts.append(dot_tn(rounded, grad_context[:, at]))
    key_block, value_block = side_by_side(key_parts), side_by_side(value_parts)
    key_grad[...] = key_block
    value_grad[...] = value_block
    dec_context[...] = side_by_side(context_parts)
    partial[...] = (dot_nn(key_block, matrix[0]) + dot_nn(value_block, matrix[1])).astype(
        jnp.bfloat16
    )


def store_terms(products, term):
    high = products[0].shape[0]
    for index, product in enumerate(products):
        term[index * high : (index + 1) * high, :] = product.astype(jnp.bfloat16)


def dec_terms_kernel(core, key_grad, value_grad, context, normed, upstream, term):
    products = [
        dot_tn(key_grad[...], normed[...]),
        dot_tn(value_grad[...], normed[...]),
        dot_tn(context[...], jnp.where(core[0] == 0, upstream[0], upstream[1])),
    ]
    store_terms(products, term)


def norm_backward_kernel(pieces, states, gains, grads):
    summed = pieces[0].astype(jnp.float32)
    for index in range(1, pieces.shape[0]):
        summed = summed + pieces[index].astype(jnp.float32)
    center, inverse = row_stats(states[...].astype(jnp.float32))
    normed = center * inverse
    scaled = summed * gains[2:3, :]
    result = inverse * (
        scaled
        - jnp.mean(scaled, axis=-1, keepdims=True)
        - normed * jnp.mean(scaled * normed, axis=-1, keepdims=True)
    )
    block = result.astype(jnp.bfloat16)
    for copy in range(grads.shape[0]):
        grads[copy] = block


def enc_backward_kernel(
    grads, out_shard, queries, values, probs, context, normed, term
):
    grad_rows = grads[...]
    att_grad = dot_nt(grad_rows, out_shard[...]).astype(jnp.bfloat16)
    query_rows, value_rows = queries[...], values[...]
    key_parts, value_parts = [], []
    for head in range(query_rows.shape[1] // HS):
        at = slice(head * HS, (head + 1) * HS)
        weights = probs[head]
        grad_scores = scores_grad(weights, att_grad[:, at], value_rows[:, at])
        key_parts.append(dot_tn(grad_scores, query_rows[:, at]) * SCALING)
        value_parts.append(dot_tn(weights.astype(jnp.bfloat16), att_grad[:, at]))
    products = [
        dot_tn(side_by_side(key_parts), normed[...]),
        dot_tn(side_by_side(value_parts), normed[...]),
        dot_tn(context[...], grad_rows),
    ]
    store_terms(products, term)


def chunks_kernel(core, enc_term, enc_sent, dec_term, dec_sent, tiles):
    first = core[0] == 0
    rows, cols = enc_term.shape
    high = rows // 8
    for block in range(cols // 128):
        at = slice(block * 128, (block + 1) * 128)
        kept = jnp.where(first, enc_term[:, at], dec_term[:, at])
        received = jnp.where(first, enc_sent[:, at], dec_sent[:, at])
        total = kept.astype(jnp.float32) + received.astype(jnp.float32)
        part = total.reshape(high, 8, 128)
        tiles[block * high : (block + 1) * high] = part.astype(jnp.bfloat16)


def sum_copies_kernel(pieces, copies):
    summed = pieces[0].astype(jnp.float32)
    for index in range(1, pieces.shape[0]):
        summed = summed + pieces[index].astype(jnp.float32)
    block = summed.astype(jnp.bfloat16)
    for copy in range(copies.shape[0]):
        copies[copy] = block


def pick_copies_kernel(core, blocks, copies):
    block = jnp.where(core[0] == 0, blocks[0], blocks[1])
    for copy in range(copies.shape[0]):
        copies[copy] = block


def from_chunks_kernel(tiles, gradient):
    rows, cols = gradient.shape
    high = rows // 8
    for block in range(cols // 128):
        part = tiles[block * high : (block + 1) * high].astype(jnp.float32)
        gradient[:, block * 128 : (block + 1) * 128] = part.reshape(rows, 128)


def call(
    kernel, outs, scalars, arrays, blocks=None, scratch=(), kept=(), read=(), cost=None
):
    blocks = blocks or {}

    def spec(index, array):
        shape, at = blocks.get(index, (array.shape, (0,) * array.ndim))
        return pl.BlockSpec(shape, lambda i: at)

    def out(index, shape, dtype):
        return pltpu.HBM(shape, dtype) if index in kept else jax.ShapeDtypeStruct(shape, dtype)

    arrays = [
        pltpu.with_memory_space_constraint(array, pltpu.HBM) if index in read else array
        for index, array in enumerate(arrays)
    ]
    result = pl.pallas_call(
        kernel,
        grid=(1,),
        out_shape=[out(index, *what) for index, what in enumerate(outs)],
        in_specs=[pl.BlockSpec(memory_space=pltpu.SMEM) for _ in scalars]
        + [spec(index, array) for index, array in enumerate(arrays)],
        out_specs=[
            pl.BlockSpec(shape, functools.partial(lambda n, i: (0,) * n, len(shape)))
            for shape, _ in outs
        ],
        scratch_shapes=list(scratch),
        cost_estimate=cost,
        compiler_params=pltpu.CompilerParams(vmem_limit_bytes=48 << 20),
    )(*scalars, *arrays)
    return result[0] if len(outs) == 1 else result


def swap(block):
    return lax.ppermute(block, "segment", [(0, 1), (1, 0)])


def shards(
    frames, dec_states, out_grad, frame_lengths, token_lengths, weights, norm_gains, norm_biases
):
    bf16, f32 = jnp.bfloat16, jnp.float32
    core = lax.axis_index("segment")
    first = core == 0
    own = weights[0]
    shard_rows, features = frames.shape[1:]
    mp = lax.axis_size("mp")
    dp = lax.axis_size("dp")
    head_cols = own.shape[1]
    heads = head_cols // HS
    rows = shard_rows * mp
    count = dec_states.shape[1]
    near_groups = [[x * 8 + y * 2 + b for x in range(4) for b in range(2)] for y in range(4)]
    far_groups = [[x * 8 + y * 2 + b for y in range(4)] for x in range(4) for b in range(2)]
    near, far = len(near_groups[0]), len(far_groups[0])

    def exchange(blocks, axis="mp", groups=None):
        return lax.all_to_all(blocks, axis, 0, 0, axis_index_groups=groups)

    core_id = core.astype(jnp.int32).reshape(1)
    place = lax.axis_index("mp").astype(jnp.int32).reshape(1)

    copies = call(
        pick_copies_kernel,
        [((mp, shard_rows, features), bf16)],
        (core_id,),
        (frames,),
        kept=(0,),
        read=(0,),
    )
    copies, own = lax.optimization_barrier((copies, own))
    other = swap(own)
    shard = jnp.where(first, own[3], other[3])
    def passing(block, hop):
        up = [(i, (i + hop) % mp) for i in range(mp)]
        down = [(mp + i, mp + (i - hop) % mp) for i in range(mp)]
        return lax.ppermute(block, ("segment", "mp"), up + down)

    passed = [shard]
    for _ in range(mp // 2 - 1):
        passed.append(passing(passed[-1], 1))
    passed.append(passing(passed[-2], 2))
    swapped = [swap(block) for block in passed[1:-1]]
    enc_full = exchange(copies).reshape(rows, features)

    token_queries, token_grads, dec_weights = call(
        token_kernel,
        [((count, head_cols), bf16)] * 2 + [((2, head_cols, features), bf16)],
        (core_id,),
        (dec_states, out_grad, own, other, norm_gains, norm_biases),
        kept=(0, 1, 2),
        read=(0, 1),
    )
    enc_full, token_queries, token_grads, dec_weights = lax.optimization_barrier(
        (enc_full, token_queries, token_grads, dec_weights)
    )
    weight_block = ((3, head_cols, features), (0, 0, 0))
    normed, queries, values, context, context_copies, probs = call(
        enc_forward_kernel,
        [
            ((rows, features), bf16),
            ((rows, head_cols), bf16),
            ((rows, head_cols), bf16),
            ((rows, head_cols), bf16),
            ((mp, rows, head_cols), bf16),
            ((heads, rows, rows), f32),
        ],
        (core_id, frame_lengths),
        (enc_full, own, other, norm_gains, norm_biases),
        {1: weight_block, 2: weight_block},
        kept=(0, 1, 2, 3, 4, 5),
        cost=pl.CostEstimate(flops=3_000_000_000, transcendentals=0, bytes_accessed=0),
    )
    context_full = exchange(context_copies)
    half_states = call(
        half_states_kernel,
        [((rows, features), f32)],
        (core_id, place),
        (enc_full, context_full, *passed[1:-2], *swapped[:-1]),
    )
    partial, states, state_normed, dec_key_grad, dec_value_grad, dec_context = call(
        dec_kernel,
        [
            ((rows, features), bf16),
            ((shard_rows, features), bf16),
            ((rows, features), bf16),
            ((rows, head_cols), bf16),
            ((rows, head_cols), bf16),
            ((count, head_cols), bf16),
        ],
        (core_id, place, frame_lengths, token_lengths),
        (
            half_states, context_full, dec_weights, token_queries, token_grads,
            norm_gains, norm_biases, passed[-2], swapped[-1], shard, passed[-1],
        ),
        scratch=[pltpu.VMEM((rows, features), f32)],
        kept=(2, 3, 4, 5),
        read=(8,),
    )
    pieces = exchange(partial.reshape(mp, shard_rows, features))
    whole = [((3 * head_cols, features), bf16)]
    dec_term = call(
        dec_terms_kernel,
        whole,
        (core_id,),
        (dec_key_grad, dec_value_grad, dec_context, state_normed, out_grad),
        kept=(0,),
        read=(0, 1, 2, 3, 4),
    )
    grads = call(
        norm_backward_kernel,
        [((mp, shard_rows, features), bf16)],
        (),
        (pieces, states, norm_gains),
    )
    grads_full = exchange(grads).reshape(rows, features)
    enc_term = call(
        enc_backward_kernel,
        whole,
        (),
        (grads_full, shard, queries, values, probs, context, normed),
    )
    dec_sent = lax.ppermute(dec_term, "segment", [(0, 1)])
    enc_sent = lax.ppermute(enc_term, "segment", [(1, 0)])
    size = 3 * head_cols * features // 1024
    each = size // near
    tiles = call(
        chunks_kernel,
        [((size, 8, 128), bf16)],
        (core_id,),
        (enc_term, enc_sent, dec_term, dec_sent),
        read=(2,),
    )
    parts = exchange(tiles.reshape(near, each, 8, 128), "dp", near_groups)
    parts = call(sum_copies_kernel, [((far, each, 8, 128), bf16)], (), (parts,))
    parts = exchange(parts, "dp", far_groups)
    parts = call(sum_copies_kernel, [((near, each, 8, 128), bf16)], (), (parts,))
    parts = exchange(parts, "dp", near_groups).reshape(size, 8, 128)
    gradient = call(from_chunks_kernel, [((3 * head_cols, features), f32)], (), (parts,))
    return gradient.reshape(1, 3, head_cols, features)


def solution(mesh):
    placed = (
        P(None, ("dp", "mp"), None),
        P(None, "dp", None),
        P(None, "dp", None),
        P(None, "dp", None),
        P(None, "dp", None),
        P("segment", None, "mp", None),
        P(),
        P(),
    )
    return jax.shard_map(
        shards,
        mesh=mesh,
        in_specs=placed,
        out_specs=P("segment", None, "mp", None),
        check_vma=False,
    )
```

```python
import functools
import math

import jax
import jax.numpy as jnp
from jax import lax
from jax.experimental import pallas as pl
from jax.experimental.pallas import tpu as pltpu
from jax.sharding import PartitionSpec as P

HS = 64
SCALING = 1.0 / math.sqrt(HS)
EPSILON = 1e-05
ROWS_DIMS = (((0,), (0,)), ((), ()))
FEAT_DIMS = (((1,), (1,)), ((), ()))


def dot_nn(a, b):
    return lax.dot_general(a, b, (((1,), (0,)), ((), ())), preferred_element_type=jnp.float32)


def dot_nt(a, b):
    return lax.dot_general(a, b, FEAT_DIMS, preferred_element_type=jnp.float32)


def dot_tn(a, b):
    return lax.dot_general(a, b, ROWS_DIMS, preferred_element_type=jnp.float32)


def row_stats(values):
    center = values - jnp.mean(values, axis=-1, keepdims=True)
    variance = jnp.mean(center * center, axis=-1, keepdims=True)
    return center, lax.rsqrt(variance + EPSILON)


def layer_norm(values, norm_gain, offset):
    center, inverse = row_stats(values.astype(jnp.float32))
    return (center * inverse * norm_gain + offset).astype(jnp.bfloat16)


def ids_along(lengths_ref, row, shape, axis):
    places = lax.broadcasted_iota(jnp.int32, shape, axis)
    bound = 0
    ids = jnp.zeros(shape, jnp.int32)
    for piece in range(lengths_ref.shape[2]):
        bound = bound + lengths_ref[row, 0, piece]
        ids = ids + (places >= bound).astype(jnp.int32)
    return ids


def softmax(queries, keys, allowed):
    scores = jnp.where(allowed, dot_nt(queries, keys) * SCALING, -1e30)
    raised = jnp.exp(scores - jnp.max(scores, axis=-1, keepdims=True))
    return raised / jnp.sum(raised, axis=-1, keepdims=True)


def scores_grad(probs, grad_context, values):
    grad_probs = dot_nt(grad_context, values)
    inner = jnp.sum(grad_probs * probs, axis=-1, keepdims=True)
    return (probs * (grad_probs - inner)).astype(jnp.bfloat16)


def side_by_side(parts):
    return jnp.concatenate(parts, axis=1).astype(jnp.bfloat16)


def enc_attention(core, lengths, x, own, other, gains, biases):
    first = core[0] == 0
    rows = x.shape[0]
    normed = layer_norm(x[...], gains[0:1, :], biases[0:1, :])
    queries, keys, values = [
        dot_nt(normed, jnp.where(first, own[kind], other[kind])).astype(jnp.bfloat16)
        for kind in range(3)
    ]
    allowed = ids_along(lengths, core[0], (rows, 1), 0) == ids_along(lengths, core[0], (1, rows), 1)
    heads = [slice(at, at + HS) for at in range(0, queries.shape[1], HS)]
    probs = [softmax(queries[:, at], keys[:, at], allowed) for at in heads]
    return normed, queries, values, heads, probs


def enc_forward_kernel(core, lengths, x, own, other, gains, biases, copies):
    _, _, values, heads, probs = enc_attention(core, lengths, x, own, other, gains, biases)
    block = side_by_side(
        [
            dot_nn(weights.astype(jnp.bfloat16), values[:, at])
            for at, weights in zip(heads, probs, strict=True)
        ]
    )
    for copy in range(copies.shape[0]):
        copies[copy] = block


def enc_keep_kernel(
    core, lengths, x, own, other, gains, biases, copies, normed, queries, values, context, probs
):
    kept = enc_attention(core, lengths, x, own, other, gains, biases)
    normed[...], queries[...], values[...] = kept[:3]
    context[...] = copies[0]
    for head, weights in enumerate(kept[4]):
        probs[head] = weights


def token_kernel(
    core, tokens, upstream, own, other, gains, biases, queries, grad_context, picked
):
    first = core[0] == 0
    own_tokens = jnp.where(first, tokens[0], tokens[1])
    normed_tokens = layer_norm(own_tokens, gains[1:2, :], biases[1:2, :])
    matrix = jnp.where(first, other[0], own[0])
    queries[...] = dot_nt(normed_tokens, matrix).astype(jnp.bfloat16)
    matrix = jnp.where(first, other[3], own[3])
    own_upstream = jnp.where(first, upstream[0], upstream[1])
    grad_context[...] = dot_nt(own_upstream, matrix).astype(jnp.bfloat16)
    for kind in (1, 2):
        picked[kind - 1] = jnp.where(first, other[kind], own[kind])


def shard_products(core, place, context, pairs):
    first = core[0] == 0
    devices = context.shape[0]

    def context_at(back):
        return context[(place[0] + jnp.where(first, devices - back, back)) % devices]

    summed = 0.0
    for back, shard, far_back, far_shard in pairs:
        left = jnp.concatenate([context_at(back), context_at(far_back)], axis=1)
        right = jnp.concatenate([shard[...], far_shard[...]], axis=0)
        summed = summed + dot_nn(left, right)
    return summed


def half_states_kernel(core, place, x, context, *refs):
    states, shards_in = refs[-1], refs[:-1]
    devices = context.shape[0]
    count = len(shards_in) // 2
    pairs = [
        (back + 1, shards_in[back], devices - 1 - back, shards_in[count + back])
        for back in range(count)
    ]
    states[...] = x[...].astype(jnp.float32) + shard_products(core, place, context, pairs)


def dec_kernel(
    core, place, frame_lens, token_lens, half_states, context, weights, token_queries, token_grads,
    gains, biases, *refs,
):
    near, near_swapped, own_shard, far, partial, states, normed = refs[:7]
    key_grad, value_grad, dec_context, scratch = refs[7:]
    rows = half_states.shape[0]
    steps = context.shape[0] // 2
    pairs = [(0, own_shard, steps, far), (steps - 1, near, steps + 1, near_swapped)]
    summed = half_states[...] + shard_products(core, place, context, pairs)
    scratch[...] = summed
    all_states = scratch[...].astype(jnp.bfloat16)
    shard = states.shape[0]
    start = pl.multiple_of(place[0] * shard, shard)
    states[...] = scratch[pl.ds(start, shard), :].astype(jnp.bfloat16)
    normed_rows = layer_norm(all_states, gains[2:3, :], biases[2:3, :])
    normed[...] = normed_rows
    matrix = [weights[0], weights[1]]
    queries = token_queries[...]
    grad_context = token_grads[...]
    keys = dot_nt(normed_rows, matrix[0]).astype(jnp.bfloat16)
    values = dot_nt(normed_rows, matrix[1]).astype(jnp.bfloat16)
    count = queries.shape[0]
    token_ids = ids_along(token_lens, core[0], (count, 1), 0)
    allowed = token_ids == ids_along(frame_lens, core[0], (1, rows), 1)
    key_parts, value_parts, context_parts = [], [], []
    for head in range(queries.shape[1] // HS):
        at = slice(head * HS, (head + 1) * HS)
        probs = softmax(queries[:, at], keys[:, at], allowed)
        rounded = probs.astype(jnp.bfloat16)
        context_parts.append(dot_nn(rounded, values[:, at]))
        grad_scores = scores_grad(probs, grad_context[:, at], values[:, at])
        key_parts.append(dot_tn(grad_scores, queries[:, at]) * SCALING)
        value_parts.append(dot_tn(rounded, grad_context[:, at]))
    key_block, value_block = side_by_side(key_parts), side_by_side(value_parts)
    key_grad[...] = key_block
    value_grad[...] = value_block
    dec_context[...] = side_by_side(context_parts)
    partial[...] = (dot_nn(key_block, matrix[0]) + dot_nn(value_block, matrix[1])).astype(
        jnp.bfloat16
    )


def store_terms(products, term):
    high = products[0].shape[0]
    for index, product in enumerate(products):
        term[index * high : (index + 1) * high, :] = product.astype(jnp.bfloat16)


def dec_terms_kernel(core, key_grad, value_grad, context, normed, upstream, term):
    products = [
        dot_tn(key_grad[...], normed[...]),
        dot_tn(value_grad[...], normed[...]),
        dot_tn(context[...], jnp.where(core[0] == 0, upstream[0], upstream[1])),
    ]
    store_terms(products, term)


def norm_backward_kernel(pieces, states, gains, grads):
    summed = pieces[0].astype(jnp.float32)
    for index in range(1, pieces.shape[0]):
        summed = summed + pieces[index].astype(jnp.float32)
    center, inverse = row_stats(states[...].astype(jnp.float32))
    normed = center * inverse
    scaled = summed * gains[2:3, :]
    result = inverse * (
        scaled
        - jnp.mean(scaled, axis=-1, keepdims=True)
        - normed * jnp.mean(scaled * normed, axis=-1, keepdims=True)
    )
    block = result.astype(jnp.bfloat16)
    for copy in range(grads.shape[0]):
        grads[copy] = block


def enc_backward_kernel(
    grads, out_shard, queries, values, probs, context, normed, term
):
    grad_rows = grads[...]
    att_grad = dot_nt(grad_rows, out_shard[...]).astype(jnp.bfloat16)
    query_rows, value_rows = queries[...], values[...]
    key_parts, value_parts = [], []
    for head in range(query_rows.shape[1] // HS):
        at = slice(head * HS, (head + 1) * HS)
        weights = probs[head]
        grad_scores = scores_grad(weights, att_grad[:, at], value_rows[:, at])
        key_parts.append(dot_tn(grad_scores, query_rows[:, at]) * SCALING)
        value_parts.append(dot_tn(weights.astype(jnp.bfloat16), att_grad[:, at]))
    products = [
        dot_tn(side_by_side(key_parts), normed[...]),
        dot_tn(side_by_side(value_parts), normed[...]),
        dot_tn(context[...], grad_rows),
    ]
    store_terms(products, term)


def chunks_kernel(core, enc_term, enc_sent, dec_term, dec_sent, tiles):
    first = core[0] == 0
    rows, cols = enc_term.shape
    high = rows // 8
    for block in range(cols // 128):
        at = slice(block * 128, (block + 1) * 128)
        kept = jnp.where(first, enc_term[:, at], dec_term[:, at])
        received = jnp.where(first, enc_sent[:, at], dec_sent[:, at])
        total = kept.astype(jnp.float32) + received.astype(jnp.float32)
        part = total.reshape(high, 8, 128)
        tiles[block * high : (block + 1) * high] = part.astype(jnp.bfloat16)


def sum_copies_kernel(pieces, copies):
    summed = pieces[0].astype(jnp.float32)
    for index in range(1, pieces.shape[0]):
        summed = summed + pieces[index].astype(jnp.float32)
    block = summed.astype(jnp.bfloat16)
    for copy in range(copies.shape[0]):
        copies[copy] = block


def pick_copies_kernel(core, blocks, copies):
    block = jnp.where(core[0] == 0, blocks[0], blocks[1])
    for copy in range(copies.shape[0]):
        copies[copy] = block


def from_chunks_kernel(tiles, gradient):
    rows, cols = gradient.shape
    high = rows // 8
    for block in range(cols // 128):
        part = tiles[block * high : (block + 1) * high].astype(jnp.float32)
        gradient[:, block * 128 : (block + 1) * 128] = part.reshape(rows, 128)


def call(
    kernel, outs, scalars, arrays, blocks=None, scratch=(), kept=(), read=(), cost=None
):
    blocks = blocks or {}

    def spec(index, array):
        shape, at = blocks.get(index, (array.shape, (0,) * array.ndim))
        return pl.BlockSpec(shape, lambda i: at)

    def out(index, shape, dtype):
        return pltpu.HBM(shape, dtype) if index in kept else jax.ShapeDtypeStruct(shape, dtype)

    arrays = [
        pltpu.with_memory_space_constraint(array, pltpu.HBM) if index in read else array
        for index, array in enumerate(arrays)
    ]
    result = pl.pallas_call(
        kernel,
        grid=(1,),
        out_shape=[out(index, *what) for index, what in enumerate(outs)],
        in_specs=[pl.BlockSpec(memory_space=pltpu.SMEM) for _ in scalars]
        + [spec(index, array) for index, array in enumerate(arrays)],
        out_specs=[
            pl.BlockSpec(shape, functools.partial(lambda n, i: (0,) * n, len(shape)))
            for shape, _ in outs
        ],
        scratch_shapes=list(scratch),
        cost_estimate=cost,
        compiler_params=pltpu.CompilerParams(vmem_limit_bytes=48 << 20),
    )(*scalars, *arrays)
    return result[0] if len(outs) == 1 else result


def swap(block):
    return lax.ppermute(block, "segment", [(0, 1), (1, 0)])


def shards(
    frames, dec_states, out_grad, frame_lengths, token_lengths, weights, norm_gains, norm_biases
):
    bf16, f32 = jnp.bfloat16, jnp.float32
    core = lax.axis_index("segment")
    first = core == 0
    own = weights[0]
    shard_rows, features = frames.shape[1:]
    mp = lax.axis_size("mp")
    dp = lax.axis_size("dp")
    head_cols = own.shape[1]
    heads = head_cols // HS
    rows = shard_rows * mp
    count = dec_states.shape[1]
    near_groups = [[x * 8 + y * 2 + b for x in range(4) for b in range(2)] for y in range(4)]
    far_groups = [[x * 8 + y * 2 + b for y in range(4)] for x in range(4) for b in range(2)]
    near, far = len(near_groups[0]), len(far_groups[0])

    def exchange(blocks, axis="mp", groups=None):
        return lax.all_to_all(blocks, axis, 0, 0, axis_index_groups=groups)

    core_id = core.astype(jnp.int32).reshape(1)
    place = lax.axis_index("mp").astype(jnp.int32).reshape(1)

    copies = call(
        pick_copies_kernel,
        [((mp, shard_rows, features), bf16)],
        (core_id,),
        (frames,),
        kept=(0,),
        read=(0,),
    )
    copies, own = lax.optimization_barrier((copies, own))
    other = swap(own)
    shard = jnp.where(first, own[3], other[3])
    def passing(block, hop):
        up = [(i, (i + hop) % mp) for i in range(mp)]
        down = [(mp + i, mp + (i - hop) % mp) for i in range(mp)]
        return lax.ppermute(block, ("segment", "mp"), up + down)

    passed = [shard]
    for _ in range(mp // 2 - 1):
        passed.append(passing(passed[-1], 1))
    passed.append(passing(passed[-2], 2))
    swapped = [swap(block) for block in passed[1:-1]]
    enc_full = exchange(copies).reshape(rows, features)

    token_queries, token_grads, dec_weights = call(
        token_kernel,
        [((count, head_cols), bf16)] * 2 + [((2, head_cols, features), bf16)],
        (core_id,),
        (dec_states, out_grad, own, other, norm_gains, norm_biases),
        kept=(0, 1, 2),
        read=(0, 1),
    )
    enc_full, token_queries, token_grads, dec_weights = lax.optimization_barrier(
        (enc_full, token_queries, token_grads, dec_weights)
    )
    weight_block = ((3, head_cols, features), (0, 0, 0))
    enc_scalars = (core_id, frame_lengths)
    enc_arrays = (enc_full, own, other, norm_gains, norm_biases)
    enc_blocks = {1: weight_block, 2: weight_block}
    context_copies = call(
        enc_forward_kernel,
        [((mp, rows, head_cols), bf16)],
        enc_scalars,
        enc_arrays,
        enc_blocks,
        kept=(0,),
        cost=pl.CostEstimate(flops=3_000_000_000, transcendentals=0, bytes_accessed=0),
    )
    normed, queries, values, context, probs = call(
        enc_keep_kernel,
        [
            ((rows, features), bf16),
            ((rows, head_cols), bf16),
            ((rows, head_cols), bf16),
            ((rows, head_cols), bf16),
            ((heads, rows, rows), f32),
        ],
        enc_scalars,
        (*enc_arrays, context_copies),
        {**enc_blocks, 5: ((1, rows, head_cols), (0, 0, 0))},
        kept=(0, 1, 2, 3, 4),
    )
    context_full = exchange(context_copies)
    half_states = call(
        half_states_kernel,
        [((rows, features), f32)],
        (core_id, place),
        (enc_full, context_full, *passed[1:-2], *swapped[:-1]),
    )
    partial, states, state_normed, dec_key_grad, dec_value_grad, dec_context = call(
        dec_kernel,
        [
            ((rows, features), bf16),
            ((shard_rows, features), bf16),
            ((rows, features), bf16),
            ((rows, head_cols), bf16),
            ((rows, head_cols), bf16),
            ((count, head_cols), bf16),
        ],
        (core_id, place, frame_lengths, token_lengths),
        (
            half_states, context_full, dec_weights, token_queries, token_grads,
            norm_gains, norm_biases, passed[-2], swapped[-1], shard, passed[-1],
        ),
        scratch=[pltpu.VMEM((rows, features), f32)],
        kept=(2, 3, 4, 5),
        read=(8,),
    )
    pieces = exchange(partial.reshape(mp, shard_rows, features))
    whole = [((3 * head_cols, features), bf16)]
    dec_term = call(
        dec_terms_kernel,
        whole,
        (core_id,),
        (dec_key_grad, dec_value_grad, dec_context, state_normed, out_grad),
        kept=(0,),
        read=(0, 1, 2, 3, 4),
    )
    grads = call(
        norm_backward_kernel,
        [((mp, shard_rows, features), bf16)],
        (),
        (pieces, states, norm_gains),
        kept=(0,),
    )
    grads_full = exchange(grads).reshape(rows, features)
    enc_term = call(
        enc_backward_kernel,
        whole,
        (),
        (grads_full, shard, queries, values, probs, context, normed),
    )
    dec_sent = lax.ppermute(dec_term, "segment", [(0, 1)])
    enc_sent = lax.ppermute(enc_term, "segment", [(1, 0)])
    size = 3 * head_cols * features // 1024
    each = size // near
    tiles = call(
        chunks_kernel,
        [((size, 8, 128), bf16)],
        (core_id,),
        (enc_term, enc_sent, dec_term, dec_sent),
    )
    parts = exchange(tiles.reshape(near, each, 8, 128), "dp", near_groups)
    parts = call(sum_copies_kernel, [((far, each, 8, 128), bf16)], (), (parts,))
    parts = exchange(parts, "dp", far_groups)
    parts = call(sum_copies_kernel, [((near, each, 8, 128), bf16)], (), (parts,))
    parts = exchange(parts, "dp", near_groups).reshape(size, 8, 128)
    gradient = call(from_chunks_kernel, [((3 * head_cols, features), f32)], (), (parts,))
    return gradient.reshape(1, 3, head_cols, features)


def solution(mesh):
    placed = (
        P(None, ("dp", "mp"), None),
        P(None, "dp", None),
        P(None, "dp", None),
        P(None, "dp", None),
        P(None, "dp", None),
        P("segment", None, "mp", None),
        P(),
        P(),
    )
    return jax.shard_map(
        shards,
        mesh=mesh,
        in_specs=placed,
        out_specs=P("segment", None, "mp", None),
        check_vma=False,
    )
```

```python
import functools
import math

import jax
import jax.numpy as jnp
from jax import lax
from jax.experimental import pallas as pl
from jax.experimental.pallas import tpu as pltpu
from jax.sharding import PartitionSpec as P

HS = 64
SCALING = 1.0 / math.sqrt(HS)
EPSILON = 1e-05
ROWS_DIMS = (((0,), (0,)), ((), ()))
FEAT_DIMS = (((1,), (1,)), ((), ()))


def dot_nn(a, b):
    return lax.dot_general(a, b, (((1,), (0,)), ((), ())), preferred_element_type=jnp.float32)


def dot_nt(a, b):
    return lax.dot_general(a, b, FEAT_DIMS, preferred_element_type=jnp.float32)


def dot_tn(a, b):
    return lax.dot_general(a, b, ROWS_DIMS, preferred_element_type=jnp.float32)


def row_stats(values):
    center = values - jnp.mean(values, axis=-1, keepdims=True)
    variance = jnp.mean(center * center, axis=-1, keepdims=True)
    return center, lax.rsqrt(variance + EPSILON)


def layer_norm(values, norm_gain, offset):
    center, inverse = row_stats(values.astype(jnp.float32))
    return (center * inverse * norm_gain + offset).astype(jnp.bfloat16)


def ids_along(lengths_ref, row, shape, axis):
    places = lax.broadcasted_iota(jnp.int32, shape, axis)
    bound = 0
    ids = jnp.zeros(shape, jnp.int32)
    for piece in range(lengths_ref.shape[2]):
        bound = bound + lengths_ref[row, 0, piece]
        ids = ids + (places >= bound).astype(jnp.int32)
    return ids


def softmax(queries, keys, allowed):
    scores = jnp.where(allowed, dot_nt(queries, keys) * SCALING, -1e30)
    raised = jnp.exp(scores - jnp.max(scores, axis=-1, keepdims=True))
    return raised / jnp.sum(raised, axis=-1, keepdims=True)


def scores_grad(probs, grad_context, values):
    grad_probs = dot_nt(grad_context, values)
    inner = jnp.sum(grad_probs * probs, axis=-1, keepdims=True)
    return (probs * (grad_probs - inner)).astype(jnp.bfloat16)


def side_by_side(parts):
    return jnp.concatenate(parts, axis=1).astype(jnp.bfloat16)


def enc_forward_kernel(
    core, lengths, x, own, other, gains, biases, normed, queries, values, context, copies, probs
):
    first = core[0] == 0
    rows = x.shape[0]
    normed_rows = layer_norm(x[...], gains[0:1, :], biases[0:1, :])
    normed[...] = normed_rows
    projected = []
    for kind in range(3):
        matrix = jnp.where(first, own[kind], other[kind])
        projected.append(dot_nt(normed_rows, matrix).astype(jnp.bfloat16))
    queries[...] = projected[0]
    values[...] = projected[2]
    allowed = ids_along(lengths, core[0], (rows, 1), 0) == ids_along(lengths, core[0], (1, rows), 1)
    parts = []
    for head in range(queries.shape[1] // HS):
        at = slice(head * HS, (head + 1) * HS)
        weights = softmax(projected[0][:, at], projected[1][:, at], allowed)
        probs[head] = weights
        parts.append(dot_nn(weights.astype(jnp.bfloat16), projected[2][:, at]))
    block = side_by_side(parts)
    context[...] = block
    for copy in range(copies.shape[0]):
        copies[copy] = block


def token_kernel(
    core, tokens, upstream, own, other, gains, biases, queries, grad_context, picked
):
    first = core[0] == 0
    own_tokens = jnp.where(first, tokens[0], tokens[1])
    normed_tokens = layer_norm(own_tokens, gains[1:2, :], biases[1:2, :])
    matrix = jnp.where(first, other[0], own[0])
    queries[...] = dot_nt(normed_tokens, matrix).astype(jnp.bfloat16)
    matrix = jnp.where(first, other[3], own[3])
    own_upstream = jnp.where(first, upstream[0], upstream[1])
    grad_context[...] = dot_nt(own_upstream, matrix).astype(jnp.bfloat16)
    for kind in (1, 2):
        picked[kind - 1] = jnp.where(first, other[kind], own[kind])


def shard_products(core, place, context, pairs):
    first = core[0] == 0
    devices = context.shape[0]

    def context_at(back):
        return context[(place[0] + jnp.where(first, devices - back, back)) % devices]

    summed = 0.0
    for back, shard, far_back, far_shard in pairs:
        left = jnp.concatenate([context_at(back), context_at(far_back)], axis=1)
        right = jnp.concatenate([shard[...], far_shard[...]], axis=0)
        summed = summed + dot_nn(left, right)
    return summed


def half_states_kernel(core, place, x, context, *refs):
    states, shards_in = refs[-1], refs[:-1]
    devices = context.shape[0]
    count = len(shards_in) // 2
    pairs = [
        (back + 1, shards_in[back], devices - 1 - back, shards_in[count + back])
        for back in range(count)
    ]
    states[...] = x[...].astype(jnp.float32) + shard_products(core, place, context, pairs)


def dec_kernel(
    core, place, frame_lens, token_lens, half_states, context, weights, token_queries, token_grads,
    gains, biases, *refs,
):
    near, near_swapped, own_shard, far, partial, states, normed = refs[:7]
    key_grad, value_grad, dec_context, scratch = refs[7:]
    rows = half_states.shape[0]
    steps = context.shape[0] // 2
    pairs = [(0, own_shard, steps, far), (steps - 1, near, steps + 1, near_swapped)]
    summed = half_states[...] + shard_products(core, place, context, pairs)
    scratch[...] = summed
    all_states = scratch[...].astype(jnp.bfloat16)
    shard = states.shape[0]
    start = pl.multiple_of(place[0] * shard, shard)
    states[...] = scratch[pl.ds(start, shard), :].astype(jnp.bfloat16)
    normed_rows = layer_norm(all_states, gains[2:3, :], biases[2:3, :])
    normed[...] = normed_rows
    matrix = [weights[0], weights[1]]
    queries = token_queries[...]
    grad_context = token_grads[...]
    keys = dot_nt(normed_rows, matrix[0]).astype(jnp.bfloat16)
    values = dot_nt(normed_rows, matrix[1]).astype(jnp.bfloat16)
    count = queries.shape[0]
    token_ids = ids_along(token_lens, core[0], (count, 1), 0)
    allowed = token_ids == ids_along(frame_lens, core[0], (1, rows), 1)
    key_parts, value_parts, context_parts = [], [], []
    for head in range(queries.shape[1] // HS):
        at = slice(head * HS, (head + 1) * HS)
        probs = softmax(queries[:, at], keys[:, at], allowed)
        rounded = probs.astype(jnp.bfloat16)
        context_parts.append(dot_nn(rounded, values[:, at]))
        grad_scores = scores_grad(probs, grad_context[:, at], values[:, at])
        key_parts.append(dot_tn(grad_scores, queries[:, at]) * SCALING)
        value_parts.append(dot_tn(rounded, grad_context[:, at]))
    key_block, value_block = side_by_side(key_parts), side_by_side(value_parts)
    key_grad[...] = key_block
    value_grad[...] = value_block
    dec_context[...] = side_by_side(context_parts)
    partial[...] = (dot_nn(key_block, matrix[0]) + dot_nn(value_block, matrix[1])).astype(
        jnp.bfloat16
    )


def store_terms(products, term):
    high = products[0].shape[0]
    for index, product in enumerate(products):
        term[index * high : (index + 1) * high, :] = product.astype(jnp.bfloat16)


def dec_terms_kernel(core, key_grad, value_grad, context, normed, upstream, term):
    products = [
        dot_tn(key_grad[...], normed[...]),
        dot_tn(value_grad[...], normed[...]),
        dot_tn(context[...], jnp.where(core[0] == 0, upstream[0], upstream[1])),
    ]
    store_terms(products, term)


def norm_backward_kernel(pieces, states, gains, grads):
    summed = pieces[0].astype(jnp.float32)
    for index in range(1, pieces.shape[0]):
        summed = summed + pieces[index].astype(jnp.float32)
    center, inverse = row_stats(states[...].astype(jnp.float32))
    normed = center * inverse
    scaled = summed * gains[2:3, :]
    result = inverse * (
        scaled
        - jnp.mean(scaled, axis=-1, keepdims=True)
        - normed * jnp.mean(scaled * normed, axis=-1, keepdims=True)
    )
    block = result.astype(jnp.bfloat16)
    for copy in range(grads.shape[0]):
        grads[copy] = block


def enc_backward_kernel(
    grads, out_shard, queries, values, probs, context, normed, term
):
    grad_rows = grads[...]
    att_grad = dot_nt(grad_rows, out_shard[...]).astype(jnp.bfloat16)
    query_rows, value_rows = queries[...], values[...]
    key_parts, value_parts = [], []
    for head in range(query_rows.shape[1] // HS):
        at = slice(head * HS, (head + 1) * HS)
        weights = probs[head]
        grad_scores = scores_grad(weights, att_grad[:, at], value_rows[:, at])
        key_parts.append(dot_tn(grad_scores, query_rows[:, at]) * SCALING)
        value_parts.append(dot_tn(weights.astype(jnp.bfloat16), att_grad[:, at]))
    products = [
        dot_tn(side_by_side(key_parts), normed[...]),
        dot_tn(side_by_side(value_parts), normed[...]),
        dot_tn(context[...], grad_rows),
    ]
    store_terms(products, term)


def chunks_kernel(core, enc_term, enc_sent, dec_term, dec_sent, tiles):
    first = core[0] == 0
    rows, cols = enc_term.shape
    high = rows // 8
    for block in range(cols // 128):
        at = slice(block * 128, (block + 1) * 128)
        kept = jnp.where(first, enc_term[:, at], dec_term[:, at])
        received = jnp.where(first, enc_sent[:, at], dec_sent[:, at])
        total = kept.astype(jnp.float32) + received.astype(jnp.float32)
        part = total.reshape(high, 8, 128)
        tiles[block * high : (block + 1) * high] = part.astype(jnp.bfloat16)


def sum_copies_kernel(pieces, copies):
    summed = pieces[0].astype(jnp.float32)
    for index in range(1, pieces.shape[0]):
        summed = summed + pieces[index].astype(jnp.float32)
    block = summed.astype(jnp.bfloat16)
    for copy in range(copies.shape[0]):
        copies[copy] = block


def pick_copies_kernel(core, blocks, copies):
    block = jnp.where(core[0] == 0, blocks[0], blocks[1])
    for copy in range(copies.shape[0]):
        copies[copy] = block


def from_chunks_kernel(tiles, gradient):
    rows, cols = gradient.shape
    high = rows // 8
    for block in range(cols // 128):
        part = tiles[block * high : (block + 1) * high].astype(jnp.float32)
        gradient[:, block * 128 : (block + 1) * 128] = part.reshape(rows, 128)


def call(
    kernel, outs, scalars, arrays, blocks=None, scratch=(), kept=(), read=(), cost=None
):
    blocks = blocks or {}

    def spec(index, array):
        shape, at = blocks.get(index, (array.shape, (0,) * array.ndim))
        return pl.BlockSpec(shape, lambda i: at)

    def out(index, shape, dtype):
        return pltpu.HBM(shape, dtype) if index in kept else jax.ShapeDtypeStruct(shape, dtype)

    arrays = [
        pltpu.with_memory_space_constraint(array, pltpu.HBM) if index in read else array
        for index, array in enumerate(arrays)
    ]
    result = pl.pallas_call(
        kernel,
        grid=(1,),
        out_shape=[out(index, *what) for index, what in enumerate(outs)],
        in_specs=[pl.BlockSpec(memory_space=pltpu.SMEM) for _ in scalars]
        + [spec(index, array) for index, array in enumerate(arrays)],
        out_specs=[
            pl.BlockSpec(shape, functools.partial(lambda n, i: (0,) * n, len(shape)))
            for shape, _ in outs
        ],
        scratch_shapes=list(scratch),
        cost_estimate=cost,
        compiler_params=pltpu.CompilerParams(vmem_limit_bytes=48 << 20),
    )(*scalars, *arrays)
    return result[0] if len(outs) == 1 else result


def swap(block):
    return lax.ppermute(block, "segment", [(0, 1), (1, 0)])


def shards(
    frames, dec_states, out_grad, frame_lengths, token_lengths, weights, norm_gains, norm_biases
):
    bf16, f32 = jnp.bfloat16, jnp.float32
    core = lax.axis_index("segment")
    first = core == 0
    own = weights[0]
    shard_rows, features = frames.shape[1:]
    mp = lax.axis_size("mp")
    dp = lax.axis_size("dp")
    head_cols = own.shape[1]
    heads = head_cols // HS
    rows = shard_rows * mp
    count = dec_states.shape[1]
    near_groups = [[x * 8 + y * 2 + b for x in range(4) for b in range(2)] for y in range(4)]
    far_groups = [[x * 8 + y * 2 + b for y in range(4)] for x in range(4) for b in range(2)]
    near, far = len(near_groups[0]), len(far_groups[0])

    def exchange(blocks, axis="mp", groups=None):
        return lax.all_to_all(blocks, axis, 0, 0, axis_index_groups=groups)

    core_id = core.astype(jnp.int32).reshape(1)
    place = lax.axis_index("mp").astype(jnp.int32).reshape(1)

    copies = call(
        pick_copies_kernel,
        [((mp, shard_rows, features), bf16)],
        (core_id,),
        (frames,),
        kept=(0,),
        read=(0,),
    )
    copies, own = lax.optimization_barrier((copies, own))
    other = swap(own)
    shard = jnp.where(first, own[3], other[3])
    def passing(block, hop):
        up = [(i, (i + hop) % mp) for i in range(mp)]
        down = [(mp + i, mp + (i - hop) % mp) for i in range(mp)]
        return lax.ppermute(block, ("segment", "mp"), up + down)

    passed = [shard]
    for _ in range(mp // 2 - 1):
        passed.append(passing(passed[-1], 1))
    passed.append(passing(passed[-2], 2))
    swapped = [swap(block) for block in passed[1:-1]]
    enc_full = exchange(copies).reshape(rows, features)

    token_queries, token_grads, dec_weights = call(
        token_kernel,
        [((count, head_cols), bf16)] * 2 + [((2, head_cols, features), bf16)],
        (core_id,),
        (dec_states, out_grad, own, other, norm_gains, norm_biases),
        kept=(0, 1, 2),
        read=(0, 1),
    )
    enc_full, token_queries, token_grads, dec_weights = lax.optimization_barrier(
        (enc_full, token_queries, token_grads, dec_weights)
    )
    weight_block = ((3, head_cols, features), (0, 0, 0))
    normed, queries, values, context, context_copies, probs = call(
        enc_forward_kernel,
        [
            ((rows, features), bf16),
            ((rows, head_cols), bf16),
            ((rows, head_cols), bf16),
            ((rows, head_cols), bf16),
            ((mp, rows, head_cols), bf16),
            ((heads, rows, rows), f32),
        ],
        (core_id, frame_lengths),
        (enc_full, own, other, norm_gains, norm_biases),
        {1: weight_block, 2: weight_block},
        kept=(0, 1, 2, 3, 4, 5),
        cost=pl.CostEstimate(flops=3_000_000_000, transcendentals=0, bytes_accessed=0),
    )
    context_full = exchange(context_copies)
    half_states = call(
        half_states_kernel,
        [((rows, features), f32)],
        (core_id, place),
        (enc_full, context_full, *passed[1:-2], *swapped[:-1]),
    )
    partial, states, state_normed, dec_key_grad, dec_value_grad, dec_context = call(
        dec_kernel,
        [
            ((rows, features), bf16),
            ((shard_rows, features), bf16),
            ((rows, features), bf16),
            ((rows, head_cols), bf16),
            ((rows, head_cols), bf16),
            ((count, head_cols), bf16),
        ],
        (core_id, place, frame_lengths, token_lengths),
        (
            half_states, context_full, dec_weights, token_queries, token_grads,
            norm_gains, norm_biases, passed[-2], swapped[-1], shard, passed[-1],
        ),
        scratch=[pltpu.VMEM((rows, features), f32)],
        kept=(2, 3, 4, 5),
        read=(8,),
    )
    pieces = exchange(partial.reshape(mp, shard_rows, features))
    whole = [((3 * head_cols, features), bf16)]
    dec_term = call(
        dec_terms_kernel,
        whole,
        (core_id,),
        (dec_key_grad, dec_value_grad, dec_context, state_normed, out_grad),
        kept=(0,),
        read=(0, 1, 2, 3, 4),
    )
    grads = call(
        norm_backward_kernel,
        [((mp, shard_rows, features), bf16)],
        (),
        (pieces, states, norm_gains),
    )
    grads_full = exchange(grads).reshape(rows, features)
    enc_term = call(
        enc_backward_kernel,
        whole,
        (),
        (grads_full, shard, queries, values, probs, context, normed),
    )
    dec_sent = lax.ppermute(dec_term, "segment", [(0, 1)])
    enc_sent = lax.ppermute(enc_term, "segment", [(1, 0)])
    size = 3 * head_cols * features // 1024
    each = size // near
    tiles = call(
        chunks_kernel,
        [((size, 8, 128), bf16)],
        (core_id,),
        (enc_term, enc_sent, dec_term, dec_sent),
    )
    parts = exchange(tiles.reshape(near, each, 8, 128), "dp", near_groups)
    parts = call(sum_copies_kernel, [((far, each, 8, 128), bf16)], (), (parts,))
    parts = exchange(parts, "dp", far_groups)
    parts = call(sum_copies_kernel, [((near, each, 8, 128), bf16)], (), (parts,))
    parts = exchange(parts, "dp", near_groups).reshape(size, 8, 128)
    gradient = call(from_chunks_kernel, [((3 * head_cols, features), f32)], (), (parts,))
    return gradient.reshape(1, 3, head_cols, features)


def solution(mesh):
    placed = (
        P(None, ("dp", "mp"), None),
        P(None, "dp", None),
        P(None, "dp", None),
        P(None, "dp", None),
        P(None, "dp", None),
        P("segment", None, "mp", None),
        P(),
        P(),
    )
    return jax.shard_map(
        shards,
        mesh=mesh,
        in_specs=placed,
        out_specs=P("segment", None, "mp", None),
        check_vma=False,
    )
```

```python
import functools
import math

import jax
import jax.numpy as jnp
from jax import lax
from jax.experimental import pallas as pl
from jax.experimental.pallas import tpu as pltpu
from jax.sharding import PartitionSpec as P

HS = 64
SCALING = 1.0 / math.sqrt(HS)
EPSILON = 1e-05
ROWS_DIMS = (((0,), (0,)), ((), ()))
FEAT_DIMS = (((1,), (1,)), ((), ()))


def dot_nn(a, b):
    return lax.dot_general(a, b, (((1,), (0,)), ((), ())), preferred_element_type=jnp.float32)


def dot_nt(a, b):
    return lax.dot_general(a, b, FEAT_DIMS, preferred_element_type=jnp.float32)


def dot_tn(a, b):
    return lax.dot_general(a, b, ROWS_DIMS, preferred_element_type=jnp.float32)


def row_stats(values):
    center = values - jnp.mean(values, axis=-1, keepdims=True)
    variance = jnp.mean(center * center, axis=-1, keepdims=True)
    return center, lax.rsqrt(variance + EPSILON)


def layer_norm(values, norm_gain, offset):
    center, inverse = row_stats(values.astype(jnp.float32))
    return (center * inverse * norm_gain + offset).astype(jnp.bfloat16)


def ids_along(lengths_ref, row, shape, axis):
    places = lax.broadcasted_iota(jnp.int32, shape, axis)
    bound = 0
    ids = jnp.zeros(shape, jnp.int32)
    for piece in range(lengths_ref.shape[2]):
        bound = bound + lengths_ref[row, 0, piece]
        ids = ids + (places >= bound).astype(jnp.int32)
    return ids


def softmax(queries, keys, allowed):
    scores = jnp.where(allowed, dot_nt(queries, keys) * SCALING, -1e30)
    raised = jnp.exp(scores - jnp.max(scores, axis=-1, keepdims=True))
    return raised / jnp.sum(raised, axis=-1, keepdims=True)


def scores_grad(probs, grad_context, values):
    grad_probs = dot_nt(grad_context, values)
    inner = jnp.sum(grad_probs * probs, axis=-1, keepdims=True)
    return (probs * (grad_probs - inner)).astype(jnp.bfloat16)


def side_by_side(parts):
    return jnp.concatenate(parts, axis=1).astype(jnp.bfloat16)


def enc_forward_kernel(
    core, lengths, x, own, other, gains, biases, normed, queries, values, context, copies, probs
):
    first = core[0] == 0
    rows = x.shape[0]
    normed_rows = layer_norm(x[...], gains[0:1, :], biases[0:1, :])
    normed[...] = normed_rows
    projected = []
    for kind in range(3):
        matrix = jnp.where(first, own[kind], other[kind])
        projected.append(dot_nt(normed_rows, matrix).astype(jnp.bfloat16))
    queries[...] = projected[0]
    values[...] = projected[2]
    allowed = ids_along(lengths, core[0], (rows, 1), 0) == ids_along(lengths, core[0], (1, rows), 1)
    parts = []
    for head in range(queries.shape[1] // HS):
        at = slice(head * HS, (head + 1) * HS)
        weights = softmax(projected[0][:, at], projected[1][:, at], allowed)
        probs[head] = weights
        parts.append(dot_nn(weights.astype(jnp.bfloat16), projected[2][:, at]))
    block = side_by_side(parts)
    context[...] = block
    for copy in range(copies.shape[0]):
        copies[copy] = block


def token_kernel(
    core, tokens, upstream, own, other, gains, biases, queries, grad_context, picked
):
    first = core[0] == 0
    own_tokens = jnp.where(first, tokens[0], tokens[1])
    normed_tokens = layer_norm(own_tokens, gains[1:2, :], biases[1:2, :])
    matrix = jnp.where(first, other[0], own[0])
    queries[...] = dot_nt(normed_tokens, matrix).astype(jnp.bfloat16)
    matrix = jnp.where(first, other[3], own[3])
    own_upstream = jnp.where(first, upstream[0], upstream[1])
    grad_context[...] = dot_nt(own_upstream, matrix).astype(jnp.bfloat16)
    for kind in (1, 2):
        picked[kind - 1] = jnp.where(first, other[kind], own[kind])


def shard_products(core, place, context, pairs):
    first = core[0] == 0
    devices = context.shape[0]

    def context_at(back):
        return context[(place[0] + jnp.where(first, devices - back, back)) % devices]

    summed = 0.0
    for back, shard, far_back, far_shard in pairs:
        left = jnp.concatenate([context_at(back), context_at(far_back)], axis=1)
        right = jnp.concatenate([shard[...], far_shard[...]], axis=0)
        summed = summed + dot_nn(left, right)
    return summed


def half_states_kernel(core, place, x, context, *refs):
    states, shards_in = refs[-1], refs[:-1]
    devices = context.shape[0]
    count = len(shards_in) // 2
    pairs = [
        (back + 1, shards_in[back], devices - 1 - back, shards_in[count + back])
        for back in range(count)
    ]
    states[...] = x[...].astype(jnp.float32) + shard_products(core, place, context, pairs)


def dec_kernel(
    core, place, frame_lens, token_lens, half_states, context, weights, token_queries, token_grads,
    gains, biases, *refs,
):
    near, near_swapped, own_shard, far, partial, states, normed = refs[:7]
    key_grad, value_grad, dec_context, scratch = refs[7:]
    rows = half_states.shape[0]
    steps = context.shape[0] // 2
    pairs = [(0, own_shard, steps, far), (steps - 1, near, steps + 1, near_swapped)]
    summed = half_states[...] + shard_products(core, place, context, pairs)
    scratch[...] = summed
    all_states = scratch[...].astype(jnp.bfloat16)
    shard = states.shape[0]
    start = pl.multiple_of(place[0] * shard, shard)
    states[...] = scratch[pl.ds(start, shard), :].astype(jnp.bfloat16)
    normed_rows = layer_norm(all_states, gains[2:3, :], biases[2:3, :])
    normed[...] = normed_rows
    matrix = [weights[0], weights[1]]
    queries = token_queries[...]
    grad_context = token_grads[...]
    keys = dot_nt(normed_rows, matrix[0]).astype(jnp.bfloat16)
    values = dot_nt(normed_rows, matrix[1]).astype(jnp.bfloat16)
    count = queries.shape[0]
    token_ids = ids_along(token_lens, core[0], (count, 1), 0)
    allowed = token_ids == ids_along(frame_lens, core[0], (1, rows), 1)
    key_parts, value_parts, context_parts = [], [], []
    for head in range(queries.shape[1] // HS):
        at = slice(head * HS, (head + 1) * HS)
        probs = softmax(queries[:, at], keys[:, at], allowed)
        rounded = probs.astype(jnp.bfloat16)
        context_parts.append(dot_nn(rounded, values[:, at]))
        grad_scores = scores_grad(probs, grad_context[:, at], values[:, at])
        key_parts.append(dot_tn(grad_scores, queries[:, at]) * SCALING)
        value_parts.append(dot_tn(rounded, grad_context[:, at]))
    key_block, value_block = side_by_side(key_parts), side_by_side(value_parts)
    key_grad[...] = key_block
    value_grad[...] = value_block
    dec_context[...] = side_by_side(context_parts)
    partial[...] = (dot_nn(key_block, matrix[0]) + dot_nn(value_block, matrix[1])).astype(
        jnp.bfloat16
    )


def store_terms(products, term):
    high = products[0].shape[0]
    for index, product in enumerate(products):
        term[index * high : (index + 1) * high, :] = product.astype(jnp.bfloat16)


def dec_terms_kernel(core, key_grad, value_grad, context, normed, upstream, term):
    products = [
        dot_tn(key_grad[...], normed[...]),
        dot_tn(value_grad[...], normed[...]),
        dot_tn(context[...], jnp.where(core[0] == 0, upstream[0], upstream[1])),
    ]
    store_terms(products, term)


def norm_backward_kernel(pieces, states, gains, grads):
    summed = pieces[0].astype(jnp.float32)
    for index in range(1, pieces.shape[0]):
        summed = summed + pieces[index].astype(jnp.float32)
    center, inverse = row_stats(states[...].astype(jnp.float32))
    normed = center * inverse
    scaled = summed * gains[2:3, :]
    result = inverse * (
        scaled
        - jnp.mean(scaled, axis=-1, keepdims=True)
        - normed * jnp.mean(scaled * normed, axis=-1, keepdims=True)
    )
    block = result.astype(jnp.bfloat16)
    for copy in range(grads.shape[0]):
        grads[copy] = block


def enc_backward_kernel(
    grads, out_shard, queries, values, probs, context, normed, term
):
    grad_rows = grads[...]
    att_grad = dot_nt(grad_rows, out_shard[...]).astype(jnp.bfloat16)
    query_rows, value_rows = queries[...], values[...]
    key_parts, value_parts = [], []
    for head in range(query_rows.shape[1] // HS):
        at = slice(head * HS, (head + 1) * HS)
        weights = probs[head]
        grad_scores = scores_grad(weights, att_grad[:, at], value_rows[:, at])
        key_parts.append(dot_tn(grad_scores, query_rows[:, at]) * SCALING)
        value_parts.append(dot_tn(weights.astype(jnp.bfloat16), att_grad[:, at]))
    products = [
        dot_tn(side_by_side(key_parts), normed[...]),
        dot_tn(side_by_side(value_parts), normed[...]),
        dot_tn(context[...], grad_rows),
    ]
    store_terms(products, term)


def chunks_kernel(core, enc_term, enc_sent, dec_term, dec_sent, tiles):
    first = core[0] == 0
    rows, cols = enc_term.shape
    high = rows // 8
    for block in range(cols // 128):
        at = slice(block * 128, (block + 1) * 128)
        kept = jnp.where(first, enc_term[:, at], dec_term[:, at])
        received = jnp.where(first, enc_sent[:, at], dec_sent[:, at])
        total = kept.astype(jnp.float32) + received.astype(jnp.float32)
        part = total.reshape(high, 8, 128)
        tiles[block * high : (block + 1) * high] = part.astype(jnp.bfloat16)


def sum_copies_kernel(pieces, copies):
    summed = pieces[0].astype(jnp.float32)
    for index in range(1, pieces.shape[0]):
        summed = summed + pieces[index].astype(jnp.float32)
    block = summed.astype(jnp.bfloat16)
    for copy in range(copies.shape[0]):
        copies[copy] = block


def pick_copies_kernel(core, blocks, copies):
    block = jnp.where(core[0] == 0, blocks[0], blocks[1])
    for copy in range(copies.shape[0]):
        copies[copy] = block


def from_chunks_kernel(tiles, gradient):
    rows, cols = gradient.shape
    high = rows // 8
    for block in range(cols // 128):
        part = tiles[block * high : (block + 1) * high].astype(jnp.float32)
        gradient[:, block * 128 : (block + 1) * 128] = part.reshape(rows, 128)


def call(
    kernel, outs, scalars, arrays, blocks=None, scratch=(), kept=(), read=(), cost=None
):
    blocks = blocks or {}

    def spec(index, array):
        shape, at = blocks.get(index, (array.shape, (0,) * array.ndim))
        return pl.BlockSpec(shape, lambda i: at)

    def out(index, shape, dtype):
        return pltpu.HBM(shape, dtype) if index in kept else jax.ShapeDtypeStruct(shape, dtype)

    arrays = [
        pltpu.with_memory_space_constraint(array, pltpu.HBM) if index in read else array
        for index, array in enumerate(arrays)
    ]
    result = pl.pallas_call(
        kernel,
        grid=(1,),
        out_shape=[out(index, *what) for index, what in enumerate(outs)],
        in_specs=[pl.BlockSpec(memory_space=pltpu.SMEM) for _ in scalars]
        + [spec(index, array) for index, array in enumerate(arrays)],
        out_specs=[
            pl.BlockSpec(shape, functools.partial(lambda n, i: (0,) * n, len(shape)))
            for shape, _ in outs
        ],
        scratch_shapes=list(scratch),
        cost_estimate=cost,
        compiler_params=pltpu.CompilerParams(vmem_limit_bytes=48 << 20),
    )(*scalars, *arrays)
    return result[0] if len(outs) == 1 else result


def swap(block):
    return lax.ppermute(block, "segment", [(0, 1), (1, 0)])


def shards(
    frames, dec_states, out_grad, frame_lengths, token_lengths, weights, norm_gains, norm_biases
):
    bf16, f32 = jnp.bfloat16, jnp.float32
    core = lax.axis_index("segment")
    first = core == 0
    own = weights[0]
    shard_rows, features = frames.shape[1:]
    mp = lax.axis_size("mp")
    dp = lax.axis_size("dp")
    head_cols = own.shape[1]
    heads = head_cols // HS
    rows = shard_rows * mp
    count = dec_states.shape[1]
    near_groups = [[x * 8 + y * 2 + b for x in range(4) for b in range(2)] for y in range(4)]
    far_groups = [[x * 8 + y * 2 + b for y in range(4)] for x in range(4) for b in range(2)]
    near, far = len(near_groups[0]), len(far_groups[0])

    def exchange(blocks, axis="mp", groups=None):
        return lax.all_to_all(blocks, axis, 0, 0, axis_index_groups=groups)

    core_id = core.astype(jnp.int32).reshape(1)
    place = lax.axis_index("mp").astype(jnp.int32).reshape(1)

    copies = call(
        pick_copies_kernel,
        [((mp, shard_rows, features), bf16)],
        (core_id,),
        (frames,),
        kept=(0,),
        read=(0,),
    )
    copies, own = lax.optimization_barrier((copies, own))
    other = swap(own)
    shard = jnp.where(first, own[3], other[3])
    def passing(block, hop):
        up = [(i, (i + hop) % mp) for i in range(mp)]
        down = [(mp + i, mp + (i - hop) % mp) for i in range(mp)]
        return lax.ppermute(block, ("segment", "mp"), up + down)

    passed = [shard]
    for _ in range(mp // 2 - 1):
        passed.append(passing(passed[-1], 1))
    passed.append(passing(passed[-2], 2))
    swapped = [swap(block) for block in passed[1:-1]]
    enc_full = exchange(copies).reshape(rows, features)

    token_queries, token_grads, dec_weights = call(
        token_kernel,
        [((count, head_cols), bf16)] * 2 + [((2, head_cols, features), bf16)],
        (core_id,),
        (dec_states, out_grad, own, other, norm_gains, norm_biases),
        kept=(0, 1, 2),
        read=(0, 1),
    )
    enc_full, token_queries, token_grads, dec_weights = lax.optimization_barrier(
        (enc_full, token_queries, token_grads, dec_weights)
    )
    weight_block = ((3, head_cols, features), (0, 0, 0))
    normed, queries, values, context, context_copies, probs = call(
        enc_forward_kernel,
        [
            ((rows, features), bf16),
            ((rows, head_cols), bf16),
            ((rows, head_cols), bf16),
            ((rows, head_cols), bf16),
            ((mp, rows, head_cols), bf16),
            ((heads, rows, rows), f32),
        ],
        (core_id, frame_lengths),
        (enc_full, own, other, norm_gains, norm_biases),
        {1: weight_block, 2: weight_block},
        kept=(0, 1, 2, 3, 4, 5),
        cost=pl.CostEstimate(flops=3_000_000_000, transcendentals=0, bytes_accessed=0),
    )
    context_full = exchange(context_copies)
    half_states = call(
        half_states_kernel,
        [((rows, features), f32)],
        (core_id, place),
        (enc_full, context_full, *passed[1:-2], *swapped[:-1]),
    )
    partial, states, state_normed, dec_key_grad, dec_value_grad, dec_context = call(
        dec_kernel,
        [
            ((rows, features), bf16),
            ((shard_rows, features), bf16),
            ((rows, features), bf16),
            ((rows, head_cols), bf16),
            ((rows, head_cols), bf16),
            ((count, head_cols), bf16),
        ],
        (core_id, place, frame_lengths, token_lengths),
        (
            half_states, context_full, dec_weights, token_queries, token_grads,
            norm_gains, norm_biases, passed[-2], swapped[-1], shard, passed[-1],
        ),
        scratch=[pltpu.VMEM((rows, features), f32)],
        kept=(2, 3, 4, 5),

    )
    pieces = exchange(partial.reshape(mp, shard_rows, features))
    whole = [((3 * head_cols, features), bf16)]
    dec_term = call(
        dec_terms_kernel,
        whole,
        (core_id,),
        (dec_key_grad, dec_value_grad, dec_context, state_normed, out_grad),
        kept=(0,),
        read=(0, 1, 2, 3, 4),
    )
    grads = call(
        norm_backward_kernel,
        [((mp, shard_rows, features), bf16)],
        (),
        (pieces, states, norm_gains),
    )
    grads_full = exchange(grads).reshape(rows, features)
    enc_term = call(
        enc_backward_kernel,
        whole,
        (),
        (grads_full, shard, queries, values, probs, context, normed),
    )
    dec_sent = lax.ppermute(dec_term, "segment", [(0, 1)])
    enc_sent = lax.ppermute(enc_term, "segment", [(1, 0)])
    size = 3 * head_cols * features // 1024
    each = size // near
    tiles = call(
        chunks_kernel,
        [((size, 8, 128), bf16)],
        (core_id,),
        (enc_term, enc_sent, dec_term, dec_sent),
    )
    parts = exchange(tiles.reshape(near, each, 8, 128), "dp", near_groups)
    parts = call(sum_copies_kernel, [((far, each, 8, 128), bf16)], (), (parts,))
    parts = exchange(parts, "dp", far_groups)
    parts = call(sum_copies_kernel, [((near, each, 8, 128), bf16)], (), (parts,))
    parts = exchange(parts, "dp", near_groups).reshape(size, 8, 128)
    gradient = call(from_chunks_kernel, [((3 * head_cols, features), f32)], (), (parts,))
    return gradient.reshape(1, 3, head_cols, features)


def solution(mesh):
    placed = (
        P(None, ("dp", "mp"), None),
        P(None, "dp", None),
        P(None, "dp", None),
        P(None, "dp", None),
        P(None, "dp", None),
        P("segment", None, "mp", None),
        P(),
        P(),
    )
    return jax.shard_map(
        shards,
        mesh=mesh,
        in_specs=placed,
        out_specs=P("segment", None, "mp", None),
        check_vma=False,
    )
```

```python
import functools
import math

import jax
import jax.numpy as jnp
from jax import lax
from jax.experimental import pallas as pl
from jax.experimental.pallas import tpu as pltpu
from jax.sharding import PartitionSpec as P

HS = 64
SCALING = 1.0 / math.sqrt(HS)
EPSILON = 1e-05
ROWS_DIMS = (((0,), (0,)), ((), ()))
FEAT_DIMS = (((1,), (1,)), ((), ()))


def dot_nn(a, b):
    return lax.dot_general(a, b, (((1,), (0,)), ((), ())), preferred_element_type=jnp.float32)


def dot_nt(a, b):
    return lax.dot_general(a, b, FEAT_DIMS, preferred_element_type=jnp.float32)


def dot_tn(a, b):
    return lax.dot_general(a, b, ROWS_DIMS, preferred_element_type=jnp.float32)


def row_stats(values):
    center = values - jnp.mean(values, axis=-1, keepdims=True)
    variance = jnp.mean(center * center, axis=-1, keepdims=True)
    return center, lax.rsqrt(variance + EPSILON)


def layer_norm(values, norm_gain, offset):
    center, inverse = row_stats(values.astype(jnp.float32))
    return (center * inverse * norm_gain + offset).astype(jnp.bfloat16)


def ids_along(lengths_ref, row, shape, axis):
    places = lax.broadcasted_iota(jnp.int32, shape, axis)
    bound = 0
    ids = jnp.zeros(shape, jnp.int32)
    for piece in range(lengths_ref.shape[2]):
        bound = bound + lengths_ref[row, 0, piece]
        ids = ids + (places >= bound).astype(jnp.int32)
    return ids


def softmax(queries, keys, allowed):
    scores = jnp.where(allowed, dot_nt(queries, keys) * SCALING, -1e30)
    raised = jnp.exp(scores - jnp.max(scores, axis=-1, keepdims=True))
    return raised / jnp.sum(raised, axis=-1, keepdims=True)


def scores_grad(probs, grad_context, values):
    grad_probs = dot_nt(grad_context, values)
    inner = jnp.sum(grad_probs * probs, axis=-1, keepdims=True)
    return (probs * (grad_probs - inner)).astype(jnp.bfloat16)


def side_by_side(parts):
    return jnp.concatenate(parts, axis=1).astype(jnp.bfloat16)


def enc_forward_kernel(
    core, lengths, x, own, other, gains, biases, normed, queries, values, context, copies, probs
):
    first = core[0] == 0
    rows = x.shape[0]
    normed_rows = layer_norm(x[...], gains[0:1, :], biases[0:1, :])
    normed[...] = normed_rows
    projected = []
    for kind in range(3):
        matrix = jnp.where(first, own[kind], other[kind])
        projected.append(dot_nt(normed_rows, matrix).astype(jnp.bfloat16))
    queries[...] = projected[0]
    values[...] = projected[2]
    allowed = ids_along(lengths, core[0], (rows, 1), 0) == ids_along(lengths, core[0], (1, rows), 1)
    parts = []
    for head in range(queries.shape[1] // HS):
        at = slice(head * HS, (head + 1) * HS)
        weights = softmax(projected[0][:, at], projected[1][:, at], allowed)
        probs[head] = weights
        parts.append(dot_nn(weights.astype(jnp.bfloat16), projected[2][:, at]))
    block = side_by_side(parts)
    context[...] = block
    for copy in range(copies.shape[0]):
        copies[copy] = block


def token_kernel(
    core, tokens, upstream, own, other, gains, biases, queries, grad_context, picked
):
    first = core[0] == 0
    own_tokens = jnp.where(first, tokens[0], tokens[1])
    normed_tokens = layer_norm(own_tokens, gains[1:2, :], biases[1:2, :])
    matrix = jnp.where(first, other[0], own[0])
    queries[...] = dot_nt(normed_tokens, matrix).astype(jnp.bfloat16)
    matrix = jnp.where(first, other[3], own[3])
    own_upstream = jnp.where(first, upstream[0], upstream[1])
    grad_context[...] = dot_nt(own_upstream, matrix).astype(jnp.bfloat16)
    for kind in (1, 2):
        picked[kind - 1] = jnp.where(first, other[kind], own[kind])


def shard_products(core, place, context, pairs):
    first = core[0] == 0
    devices = context.shape[0]

    def context_at(back):
        return context[(place[0] + jnp.where(first, devices - back, back)) % devices]

    summed = 0.0
    for back, shard, far_back, far_shard in pairs:
        left = jnp.concatenate([context_at(back), context_at(far_back)], axis=1)
        right = jnp.concatenate([shard[...], far_shard[...]], axis=0)
        summed = summed + dot_nn(left, right)
    return summed


def half_states_kernel(core, place, x, context, *refs):
    states, shards_in = refs[-1], refs[:-1]
    devices = context.shape[0]
    count = len(shards_in) // 2
    pairs = [
        (back + 1, shards_in[back], devices - 1 - back, shards_in[count + back])
        for back in range(count)
    ]
    states[...] = x[...].astype(jnp.float32) + shard_products(core, place, context, pairs)


def dec_kernel(
    core, place, frame_lens, token_lens, half_states, context, weights, token_queries, token_grads,
    gains, biases, *refs,
):
    near, near_swapped, own_shard, far, partial, states, normed = refs[:7]
    key_grad, value_grad, dec_context, scratch = refs[7:]
    rows = half_states.shape[0]
    steps = context.shape[0] // 2
    pairs = [(0, own_shard, steps, far), (steps - 1, near, steps + 1, near_swapped)]
    summed = half_states[...] + shard_products(core, place, context, pairs)
    scratch[...] = summed
    all_states = scratch[...].astype(jnp.bfloat16)
    shard = states.shape[0]
    start = pl.multiple_of(place[0] * shard, shard)
    states[...] = scratch[pl.ds(start, shard), :].astype(jnp.bfloat16)
    normed_rows = layer_norm(all_states, gains[2:3, :], biases[2:3, :])
    normed[...] = normed_rows
    matrix = [weights[0], weights[1]]
    queries = token_queries[...]
    grad_context = token_grads[...]
    keys = dot_nt(normed_rows, matrix[0]).astype(jnp.bfloat16)
    values = dot_nt(normed_rows, matrix[1]).astype(jnp.bfloat16)
    count = queries.shape[0]
    token_ids = ids_along(token_lens, core[0], (count, 1), 0)
    allowed = token_ids == ids_along(frame_lens, core[0], (1, rows), 1)
    key_parts, value_parts, context_parts = [], [], []
    for head in range(queries.shape[1] // HS):
        at = slice(head * HS, (head + 1) * HS)
        probs = softmax(queries[:, at], keys[:, at], allowed)
        rounded = probs.astype(jnp.bfloat16)
        context_parts.append(dot_nn(rounded, values[:, at]))
        grad_scores = scores_grad(probs, grad_context[:, at], values[:, at])
        key_parts.append(dot_tn(grad_scores, queries[:, at]) * SCALING)
        value_parts.append(dot_tn(rounded, grad_context[:, at]))
    key_block, value_block = side_by_side(key_parts), side_by_side(value_parts)
    key_grad[...] = key_block
    value_grad[...] = value_block
    dec_context[...] = side_by_side(context_parts)
    partial[...] = (dot_nn(key_block, matrix[0]) + dot_nn(value_block, matrix[1])).astype(
        jnp.bfloat16
    )


def store_terms(products, term):
    high = products[0].shape[0]
    for index, product in enumerate(products):
        term[index * high : (index + 1) * high, :] = product.astype(jnp.bfloat16)


def dec_terms_kernel(core, key_grad, value_grad, context, normed, upstream, term):
    products = [
        dot_tn(key_grad[...], normed[...]),
        dot_tn(value_grad[...], normed[...]),
        dot_tn(context[...], jnp.where(core[0] == 0, upstream[0], upstream[1])),
    ]
    store_terms(products, term)


def norm_backward_kernel(pieces, states, gains, grads):
    summed = pieces[0].astype(jnp.float32)
    for index in range(1, pieces.shape[0]):
        summed = summed + pieces[index].astype(jnp.float32)
    center, inverse = row_stats(states[...].astype(jnp.float32))
    normed = center * inverse
    scaled = summed * gains[2:3, :]
    result = inverse * (
        scaled
        - jnp.mean(scaled, axis=-1, keepdims=True)
        - normed * jnp.mean(scaled * normed, axis=-1, keepdims=True)
    )
    block = result.astype(jnp.bfloat16)
    for copy in range(grads.shape[0]):
        grads[copy] = block


def enc_backward_kernel(
    grads, out_shard, queries, values, probs, context, normed, term
):
    grad_rows = grads[...]
    att_grad = dot_nt(grad_rows, out_shard[...]).astype(jnp.bfloat16)
    query_rows, value_rows = queries[...], values[...]
    key_parts, value_parts = [], []
    for head in range(query_rows.shape[1] // HS):
        at = slice(head * HS, (head + 1) * HS)
        weights = probs[head]
        grad_scores = scores_grad(weights, att_grad[:, at], value_rows[:, at])
        key_parts.append(dot_tn(grad_scores, query_rows[:, at]) * SCALING)
        value_parts.append(dot_tn(weights.astype(jnp.bfloat16), att_grad[:, at]))
    products = [
        dot_tn(side_by_side(key_parts), normed[...]),
        dot_tn(side_by_side(value_parts), normed[...]),
        dot_tn(context[...], grad_rows),
    ]
    store_terms(products, term)


def chunks_kernel(core, enc_term, enc_sent, dec_term, dec_sent, tiles):
    first = core[0] == 0
    rows, cols = enc_term.shape
    high = rows // 8
    for block in range(cols // 128):
        at = slice(block * 128, (block + 1) * 128)
        kept = jnp.where(first, enc_term[:, at], dec_term[:, at])
        received = jnp.where(first, enc_sent[:, at], dec_sent[:, at])
        total = kept.astype(jnp.float32) + received.astype(jnp.float32)
        part = total.reshape(high, 8, 128)
        tiles[block * high : (block + 1) * high] = part.astype(jnp.bfloat16)


def sum_copies_kernel(pieces, copies):
    summed = pieces[0].astype(jnp.float32)
    for index in range(1, pieces.shape[0]):
        summed = summed + pieces[index].astype(jnp.float32)
    block = summed.astype(jnp.bfloat16)
    for copy in range(copies.shape[0]):
        copies[copy] = block


def pick_copies_kernel(core, blocks, copies):
    block = jnp.where(core[0] == 0, blocks[0], blocks[1])
    for copy in range(copies.shape[0]):
        copies[copy] = block


def from_chunks_kernel(tiles, gradient):
    rows, cols = gradient.shape
    high = rows // 8
    for block in range(cols // 128):
        part = tiles[block * high : (block + 1) * high].astype(jnp.float32)
        gradient[:, block * 128 : (block + 1) * 128] = part.reshape(rows, 128)


def call(
    kernel, outs, scalars, arrays, blocks=None, scratch=(), kept=(), read=(), cost=None
):
    blocks = blocks or {}

    def spec(index, array):
        shape, at = blocks.get(index, (array.shape, (0,) * array.ndim))
        return pl.BlockSpec(shape, lambda i: at)

    def out(index, shape, dtype):
        return pltpu.HBM(shape, dtype) if index in kept else jax.ShapeDtypeStruct(shape, dtype)

    arrays = [
        pltpu.with_memory_space_constraint(array, pltpu.HBM) if index in read else array
        for index, array in enumerate(arrays)
    ]
    result = pl.pallas_call(
        kernel,
        grid=(1,),
        out_shape=[out(index, *what) for index, what in enumerate(outs)],
        in_specs=[pl.BlockSpec(memory_space=pltpu.SMEM) for _ in scalars]
        + [spec(index, array) for index, array in enumerate(arrays)],
        out_specs=[
            pl.BlockSpec(shape, functools.partial(lambda n, i: (0,) * n, len(shape)))
            for shape, _ in outs
        ],
        scratch_shapes=list(scratch),
        cost_estimate=cost,
        compiler_params=pltpu.CompilerParams(vmem_limit_bytes=48 << 20),
    )(*scalars, *arrays)
    return result[0] if len(outs) == 1 else result


def swap(block):
    return lax.ppermute(block, "segment", [(0, 1), (1, 0)])


def shards(
    frames, dec_states, out_grad, frame_lengths, token_lengths, weights, norm_gains, norm_biases
):
    bf16, f32 = jnp.bfloat16, jnp.float32
    core = lax.axis_index("segment")
    first = core == 0
    own = weights[0]
    shard_rows, features = frames.shape[1:]
    mp = lax.axis_size("mp")
    dp = lax.axis_size("dp")
    head_cols = own.shape[1]
    heads = head_cols // HS
    rows = shard_rows * mp
    count = dec_states.shape[1]
    near_groups = [[x * 8 + y * 2 + b for x in range(4) for b in range(2)] for y in range(4)]
    far_groups = [[x * 8 + y * 2 + b for y in range(4)] for x in range(4) for b in range(2)]
    near, far = len(near_groups[0]), len(far_groups[0])

    def exchange(blocks, axis="mp", groups=None):
        return lax.all_to_all(blocks, axis, 0, 0, axis_index_groups=groups)

    core_id = core.astype(jnp.int32).reshape(1)
    place = lax.axis_index("mp").astype(jnp.int32).reshape(1)

    copies = call(
        pick_copies_kernel,
        [((mp, shard_rows, features), bf16)],
        (core_id,),
        (frames,),
        kept=(0,),
    )
    copies, own = lax.optimization_barrier((copies, own))
    other = swap(own)
    shard = jnp.where(first, own[3], other[3])
    def passing(block, hop):
        up = [(i, (i + hop) % mp) for i in range(mp)]
        down = [(mp + i, mp + (i - hop) % mp) for i in range(mp)]
        return lax.ppermute(block, ("segment", "mp"), up + down)

    passed = [shard]
    for _ in range(mp // 2 - 1):
        passed.append(passing(passed[-1], 1))
    passed.append(passing(passed[-2], 2))
    swapped = [swap(block) for block in passed[1:-1]]
    enc_full = exchange(copies).reshape(rows, features)

    token_queries, token_grads, dec_weights = call(
        token_kernel,
        [((count, head_cols), bf16)] * 2 + [((2, head_cols, features), bf16)],
        (core_id,),
        (dec_states, out_grad, own, other, norm_gains, norm_biases),
        kept=(0, 1, 2),
        read=(0, 1),
    )
    enc_full, token_queries, token_grads, dec_weights = lax.optimization_barrier(
        (enc_full, token_queries, token_grads, dec_weights)
    )
    weight_block = ((3, head_cols, features), (0, 0, 0))
    normed, queries, values, context, context_copies, probs = call(
        enc_forward_kernel,
        [
            ((rows, features), bf16),
            ((rows, head_cols), bf16),
            ((rows, head_cols), bf16),
            ((rows, head_cols), bf16),
            ((mp, rows, head_cols), bf16),
            ((heads, rows, rows), f32),
        ],
        (core_id, frame_lengths),
        (enc_full, own, other, norm_gains, norm_biases),
        {1: weight_block, 2: weight_block},
        kept=(0, 1, 2, 3, 4, 5),
        cost=pl.CostEstimate(flops=3_000_000_000, transcendentals=0, bytes_accessed=0),
    )
    context_full = exchange(context_copies)
    half_states = call(
        half_states_kernel,
        [((rows, features), f32)],
        (core_id, place),
        (enc_full, context_full, *passed[1:-2], *swapped[:-1]),
    )
    partial, states, state_normed, dec_key_grad, dec_value_grad, dec_context = call(
        dec_kernel,
        [
            ((rows, features), bf16),
            ((shard_rows, features), bf16),
            ((rows, features), bf16),
            ((rows, head_cols), bf16),
            ((rows, head_cols), bf16),
            ((count, head_cols), bf16),
        ],
        (core_id, place, frame_lengths, token_lengths),
        (
            half_states, context_full, dec_weights, token_queries, token_grads,
            norm_gains, norm_biases, passed[-2], swapped[-1], shard, passed[-1],
        ),
        scratch=[pltpu.VMEM((rows, features), f32)],
        kept=(2, 3, 4, 5),

    )
    pieces = exchange(partial.reshape(mp, shard_rows, features))
    whole = [((3 * head_cols, features), bf16)]
    dec_term = call(
        dec_terms_kernel,
        whole,
        (core_id,),
        (dec_key_grad, dec_value_grad, dec_context, state_normed, out_grad),
        kept=(0,),
        read=(0, 1, 2, 3, 4),
    )
    grads = call(
        norm_backward_kernel,
        [((mp, shard_rows, features), bf16)],
        (),
        (pieces, states, norm_gains),
    )
    grads_full = exchange(grads).reshape(rows, features)
    enc_term = call(
        enc_backward_kernel,
        whole,
        (),
        (grads_full, shard, queries, values, probs, context, normed),
    )
    dec_sent = lax.ppermute(dec_term, "segment", [(0, 1)])
    enc_sent = lax.ppermute(enc_term, "segment", [(1, 0)])
    size = 3 * head_cols * features // 1024
    each = size // near
    tiles = call(
        chunks_kernel,
        [((size, 8, 128), bf16)],
        (core_id,),
        (enc_term, enc_sent, dec_term, dec_sent),
    )
    parts = exchange(tiles.reshape(near, each, 8, 128), "dp", near_groups)
    parts = call(sum_copies_kernel, [((far, each, 8, 128), bf16)], (), (parts,))
    parts = exchange(parts, "dp", far_groups)
    parts = call(sum_copies_kernel, [((near, each, 8, 128), bf16)], (), (parts,))
    parts = exchange(parts, "dp", near_groups).reshape(size, 8, 128)
    gradient = call(from_chunks_kernel, [((3 * head_cols, features), f32)], (), (parts,))
    return gradient.reshape(1, 3, head_cols, features)


def solution(mesh):
    placed = (
        P(None, ("dp", "mp"), None),
        P(None, "dp", None),
        P(None, "dp", None),
        P(None, "dp", None),
        P(None, "dp", None),
        P("segment", None, "mp", None),
        P(),
        P(),
    )
    return jax.shard_map(
        shards,
        mesh=mesh,
        in_specs=placed,
        out_specs=P("segment", None, "mp", None),
        check_vma=False,
    )
```
